32 devices in a mesh: dp: 16 (over z, y, x), tensor: 2 (over core).
Axes of the slice: x: 2, y: 2, z: 4, core: 2. Of those that a mesh axis runs over, the one named last changes fastest.
Arguments:
- tokens_in: bfloat16 [32768, 768], P('dp'), may hold values from -6 to 6
- segment_ids: int32 [64, 512], P('dp'), may hold values from 0 to 3, never falling along the last dimension, each value on 1 to 256 neighbouring positions
- w_qkv: bfloat16 [3, 768, 768], P(None, None, 'tensor'), may hold values from -0.3125 to 0.3125
- bias_qv: bfloat16 [2, 768], P(None, 'tensor'), may hold values from -1.796875 to 1.796875
- w_out: bfloat16 [768, 768], P('tensor'), may hold values from -0.875 to 0.875
- bias_out: bfloat16 [768], replicated, may hold values from -1.796875 to 1.796875
- norm1_gain: bfloat16 [768], replicated, may hold values from 0.25 to 1.75
- norm1_shift: bfloat16 [768], replicated, may hold values from -1.796875 to 1.796875
- w_in: bfloat16 [768, 3072], P(None, 'tensor'), may hold values from -0.21875 to 0.21875
- bias_in: bfloat16 [3072], P('tensor'), may hold values from -1.796875 to 1.796875
- w_down: bfloat16 [3072, 768], P('tensor'), may hold values from -0.15625 to 0.15625
- bias_down: bfloat16 [768], replicated, may hold values from -1.796875 to 1.796875
- norm2_gain: bfloat16 [768], replicated, may hold values from 0.25 to 1.75
- norm2_shift: bfloat16 [768], replicated, may hold values from -1.796875 to 1.796875
- grad_output: bfloat16 [32768, 768], P('dp'), may hold values from -6 to 6
Outputs:
- output: bfloat16 [32768, 768], P('dp')
- grad_input: bfloat16 [32768, 768], P('dp')
- grad_w_qkv: float32 [3, 768, 768], P(None, 'dp', 'tensor')
- grad_bias_qv: float32 [2, 768], P(None, 'tensor')
- grad_w_out: float32 [768, 768], P('tensor', 'dp')
- grad_bias_out: float32 [768], replicated
- grad_norm1_gain: float32 [768], replicated
- grad_norm1_shift: float32 [768], replicated
- grad_w_in: float32 [768, 3072], P('dp', 'tensor')
- grad_bias_in: float32 [3072], P('tensor')
- grad_w_down: float32 [3072, 768], P('tensor', 'dp')
- grad_bias_down: float32 [768], replicated
- grad_norm2_gain: float32 [768], replicated
- grad_norm2_shift: float32 [768], replicated
The draws below stay inside these ranges and needn't reach their ends.
Inputs may be any that keep to these rules, and one draw needn't show every extreme that they name: `segment_ids`: within each sequence the page numbers never fall; every page 0 to 3 is present, with 1 to 256 tokens.
All inputs are finite; a program needn't handle non-finite values.
Results may differ from the reference program's by a relative error of at most 0.02.
The reference program's roundings to bfloat16 on the way count: a program that leaves them out, or rounds other values in their place, can miss the bound.
Values may be sent and summed in bfloat16 or wider, within the bound.
No kernel may reach another device: no remote copies, remote signals or barrier semaphores. Data moves between devices by JAX's collectives and lax.ppermute only.
A program may use at most 192 MiB of HBM per device.

```python
import math
import jax
import jax.numpy as jnp
import numpy as np
from jax import lax

D = 768
HEADS = 12
HEAD_DIM = 64
FF = 3072
SEQ_LEN = 512
PAGES = 4
SEQ_DEV = 4
SEQS = 64
TOKENS = 32768
N_DP = 16
N_TENSOR = 2


def strengthened(values, key, source, target, shards_of, factor):
    def block_of(dim):
        return (jnp.arange(values.shape[dim]) // (values.shape[dim] // shards_of)).reshape((-1,) + (1,) * (values.ndim - 1 - dim))

    near = jax.random.permutation(key, shards_of)[block_of(target)]
    other_side = (block_of(target) + shards_of // 2) % shards_of
    return jnp.where((block_of(source) == near) | (block_of(source) == other_side), factor * values, values)


def steps_of(own_key, extent, pieces, low, top_value):
    factor_of, own = 1.0, jax.random.fold_in(own_key, 6)
    for axis_at, parts in pieces:
        heights = jnp.exp(jax.random.uniform(jax.random.fold_in(own, axis_at), (parts,), jnp.float32, low / len(pieces), top_value / len(pieces)))
        factor_of = factor_of * jnp.repeat(heights, extent[axis_at] // parts).reshape([-1 if axis == axis_at else 1 for axis in range(len(extent))])
    return factor_of


def profile(amount, total, bound, skew):
    portions = [(1 << 20) // math.isqrt(rank ** skew) + 1 for rank in range(2, amount + 1)]
    surplus, counts = total - bound - (amount - 1), [1] * (amount - 1)
    while surplus > 0:
        free = [i for i in range(amount - 1) if counts[i] < bound]
        whole, budget = sum([portions[i] for i in free]), surplus
        for i in free:
            extra = min(bound - counts[i], max(1, budget * portions[i] // whole), surplus)
            counts[i] = counts[i] + extra
            surplus = surplus - extra
    return np.array([bound] + counts)


def uneven(stream_key, amount, total, limit, skew):
    if amount == 2:
        one = jax.random.randint(stream_key, (), max(1, total - limit), min(limit, total - 1) + 1)
        return jnp.stack([one, total - one])
    tallies = jnp.asarray(profile(amount, total, limit, skew), jnp.int32)
    couples = (amount - 1) // 2
    donor, taker = tallies[1:1 + 2 * couples:2], tallies[2:2 + 2 * couples:2]
    margin = jnp.minimum(donor - 1, limit - taker)
    moved = jax.random.randint(jax.random.fold_in(stream_key, 1), (couples,), 0, 1 << 20) % (margin + 1)
    tallies = tallies.at[1:1 + 2 * couples:2].set(donor - moved).at[2:2 + 2 * couples:2].set(taker + moved)
    return tallies[jax.random.permutation(jax.random.fold_in(stream_key, 2), amount)]


def gaussian(stream_key, shape, deviation, most, pieces=(), held_as=jnp.bfloat16):
    values = deviation * jax.random.normal(stream_key, shape, jnp.float32)
    if pieces:
        values = values * steps_of(stream_key, shape, pieces, -0.22, 0.18)
    return jnp.clip(values, -most, most).astype(held_as)


def noise_with(key, extent, scale, reach, cuts, heavy, kind=jnp.bfloat16):
    values = scale * jax.random.normal(key, extent, jnp.float32)
    if cuts:
        values = values * steps_of(key, extent, cuts, -0.22, 0.18)
    return jnp.clip(strengthened(values, jax.random.fold_in(key, 3), *heavy), -reach, reach).astype(kind)


def setup_inputs(seed: int = 0) -> dict:
    key_list = jax.random.split(jax.random.key(seed), 16)
    return {
        "tokens_in": noise_with(key_list[0], (TOKENS, D), 1.0, 6.0, ((0, 16),), (0, 1, 16, 2.0)),
        "segment_ids": jax.vmap(lambda own: jnp.searchsorted(jnp.cumsum(uneven(own, PAGES, SEQ_LEN, SEQ_LEN // 2, 0)), jnp.arange(SEQ_LEN), side="right"))(jax.random.split(key_list[1], SEQS)).reshape((SEQS, SEQ_LEN)).astype(jnp.int32),
        "w_qkv": gaussian(key_list[2], (3, D, D), (D // 2) ** -0.5, 0.3125, ((2, 2),)),
        "bias_qv": gaussian(key_list[3], (2, D), 0.3, 1.796875, ((1, 2),)),
        "w_out": gaussian(key_list[4], (D, D), (D // 16) ** -0.5, 0.875, ((0, 2),)),
        "bias_out": gaussian(key_list[5], (D,), 0.3, 1.796875),
        "norm1_gain": jnp.clip(1.0 + 0.15 * jax.random.normal(key_list[6], (D,), jnp.float32), 0.25, 1.75).astype(jnp.bfloat16),
        "norm1_shift": gaussian(key_list[7], (D,), 0.3, 1.796875),
        "w_in": gaussian(key_list[8], (D, FF), D ** -0.5, 0.21875, ((1, 2),)),
        "bias_in": gaussian(key_list[9], (FF,), 0.3, 1.796875, ((0, 2),)),
        "w_down": gaussian(key_list[10], (FF, D), (FF // 2) ** -0.5, 0.15625, ((0, 2),)),
        "bias_down": gaussian(key_list[11], (D,), 0.3, 1.796875),
        "norm2_gain": jnp.clip(1.0 + 0.15 * jax.random.normal(key_list[12], (D,), jnp.float32), 0.25, 1.75).astype(jnp.bfloat16),
        "norm2_shift": gaussian(key_list[13], (D,), 0.3, 1.796875),
        "grad_output": noise_with(key_list[14], (TOKENS, D), 1.0, 6.0, ((0, 16),), (0, 1, 16, 2.0)),
    }


EPSILON = 1e-05
NEGATIVE = -1e+30
ROOT_HALF = 0.7071067811865476

@jax.custom_vjp
def low(v):
    return lax.optimization_barrier(v.astype(jnp.bfloat16)).astype(jnp.float32)

@jax.custom_vjp
def low_back(v):
    return v

def low_keep(v):
    return (low(v), None)

def low_pass(kept, grad):
    return (grad,)

def back_keep(v):
    return (v, None)

def back_low(kept, grad):
    return (low(grad),)
low.defvjp(low_keep, low_pass)
low_back.defvjp(back_keep, back_low)

def product_highest(left, right):
    return jnp.dot(left, right, precision=lax.Precision.HIGHEST, preferred_element_type=jnp.float32)

def layer_norm(summed, gain_vec, shift_vec):
    centered = summed - lax.optimization_barrier(jnp.mean(summed, axis=-1, keepdims=True))
    variance = lax.optimization_barrier(jnp.mean(centered * centered, axis=-1, keepdims=True))
    return centered * lax.rsqrt(variance + EPSILON) * gain_vec + shift_vec

def layer(tokens, segments, params):
    w_qkv, bias_qv, w_out, bias_out, gain_one, shift_one, w_in, bias_in, w_down, bias_down, gain_two, shift_two = params
    group_heads = HEADS // N_TENSOR
    group_cols = group_heads * HEAD_DIM
    group_hidden = FF // N_TENSOR
    seq_count = segments.shape[0]
    same_page = (segments[:, :, None] == segments[:, None, :])[:, None]
    scaling = 1.0 / math.sqrt(HEAD_DIM)
    attention = jnp.zeros_like(tokens)
    for group_idx in range(N_TENSOR):
        column_range = slice(group_idx * group_cols, (group_idx + 1) * group_cols)
        tokens_group = low_back(tokens)
        query = low_back(low(product_highest(tokens_group, w_qkv[0][:, column_range]) + bias_qv[0][column_range]))
        keys = low_back(low(product_highest(tokens_group, w_qkv[1][:, column_range])))
        values = low_back(low(product_highest(tokens_group, w_qkv[2][:, column_range]) + bias_qv[1][column_range]))
        shape_four = (seq_count, -1, group_heads, HEAD_DIM)
        query = query.reshape(shape_four)
        keys = keys.reshape(shape_four)
        values = values.reshape(shape_four)
        scores = low_back(scaling * jnp.einsum('bqhd,bkhd->bhqk', query, keys, precision=lax.Precision.HIGHEST))
        scores = jnp.where(same_page, scores, NEGATIVE)
        row_max = lax.optimization_barrier(jnp.max(scores, axis=-1, keepdims=True))
        exp_scores = jnp.exp(scores - row_max)
        probs = exp_scores / lax.optimization_barrier(jnp.sum(exp_scores, axis=-1, keepdims=True))
        weights_low = low(probs)
        context = jnp.einsum('bhqk,bkhd->bqhd', weights_low, values, precision=lax.Precision.HIGHEST)
        context = low_back(low(context)).reshape(-1, group_cols)
        attention = attention + low(low_back(product_highest(context, w_out[column_range, :])))
    normed_one = layer_norm(tokens + attention + bias_out, gain_one, shift_one)
    feedforward = jnp.zeros_like(tokens)
    for group_idx in range(N_TENSOR):
        hidden_range = slice(group_idx * group_hidden, (group_idx + 1) * group_hidden)
        normed_group = low_back(low(normed_one))
        preact = low_back(product_highest(normed_group, w_in[:, hidden_range]) + bias_in[hidden_range])
        hidden = low(preact * 0.5 * (1.0 + lax.erf(preact * ROOT_HALF)))
        feedforward = feedforward + low(low_back(product_highest(hidden, w_down[hidden_range, :])))
    return layer_norm(normed_one + feedforward + bias_down, gain_two, shift_two)

def reference(tokens_in, segment_ids, w_qkv, bias_qv, w_out, bias_out, norm1_gain, norm1_shift, w_in, bias_in, w_down, bias_down, norm2_gain, norm2_shift, grad_output):
    params = tuple((member.astype(jnp.float32) for member in (w_qkv, bias_qv, w_out, bias_out, norm1_gain, norm1_shift, w_in, bias_in, w_down, bias_down, norm2_gain, norm2_shift)))
    tokens = tokens_in.astype(jnp.float32).reshape(N_DP, -1, D)
    segments = segment_ids.reshape(N_DP, SEQ_DEV, SEQ_LEN)
    block_layer = jax.checkpoint(layer)

    def forward(tokens_all, params_all):
        return lax.map(lambda operands: block_layer(operands[0], operands[1], params_all), (tokens_all, segments))
    result, pullback = jax.vjp(forward, tokens, params)
    grad_tokens, grad_params = pullback(grad_output.astype(jnp.float32).reshape(N_DP, -1, D))
    return (result.reshape(-1, D).astype(jnp.bfloat16), grad_tokens.reshape(-1, D).astype(jnp.bfloat16), grad_params[0], grad_params[1], grad_params[2], grad_params[3], grad_params[4], grad_params[5], grad_params[6], grad_params[7], grad_params[8], grad_params[9], grad_params[10], grad_params[11])
```

```python
import math

import jax
import jax.numpy as jnp
from jax import lax
from jax.sharding import PartitionSpec as P

HEAD_DIM = 64


EPSILON = 1e-05
NEGATIVE = -1e30
ROOT_HALF = 0.7071067811865476
ROOT_TWO_PI_INV = 0.3989422804014327
F32 = jnp.float32
BF16 = jnp.bfloat16


def norm_forward(summed, gain_vec, shift_vec):
    centered = summed - jnp.mean(summed, axis=-1, keepdims=True)
    variance = jnp.mean(centered * centered, axis=-1, keepdims=True)
    inv_std = lax.rsqrt(variance + EPSILON)
    normed = centered * inv_std
    return (normed * gain_vec + shift_vec, normed, inv_std)


def norm_backward(upstream, normed, inv_std, gain_vec):
    scaled_grad = upstream * gain_vec
    first_mean = jnp.mean(scaled_grad, axis=-1, keepdims=True)
    second_mean = jnp.mean(scaled_grad * normed, axis=-1, keepdims=True)
    grad_summed = inv_std * (scaled_grad - first_mean - normed * second_mean)
    return (grad_summed, jnp.sum(upstream * normed, axis=0), jnp.sum(upstream, axis=0))


def gelu_pair(preact):
    cumulative = 0.5 * (1.0 + lax.erf(preact * ROOT_HALF))
    derivative = cumulative + preact * jnp.exp(-0.5 * preact * preact) * ROOT_TWO_PI_INV
    return (preact * cumulative, derivative)


def swap_pair(value):
    return lax.ppermute(value, "tensor", [(0, 1), (1, 0)])


def swap_bits(value, count, mask):
    return lax.ppermute(value, "dp", [(i, i ^ mask) for i in range(count)])


def scatter_stages(count, flip):
    bits = count.bit_length() - 1
    singles = max(0, bits - 2)
    order = list(range(singles))
    if flip and singles >= 2:
        order[0], order[1] = order[1], order[0]
    return (order, list(range(singles, bits)))


def scatter_rows(partial, count, flip):
    rows, cols = partial.shape
    bits = count.bit_length() - 1
    index = lax.axis_index("dp")
    current = partial.reshape((2,) * bits + (rows // count, cols))
    order, last = scatter_stages(count, flip)
    alive = list(range(bits - 1, -1, -1))
    for bit in order:
        axis = alive.index(bit)
        mine = (index >> bit) & 1
        keep = lax.dynamic_index_in_dim(current, mine, axis, keepdims=False)
        send = lax.dynamic_index_in_dim(current, 1 - mine, axis, keepdims=False)
        received = swap_bits(send.astype(BF16), count, 1 << bit)
        current = keep.astype(F32) + received.astype(F32)
        alive.remove(bit)
    current = current.reshape((1 << len(last), rows // count, cols))
    shift = last[0] if last else 0
    mine = index >> shift
    total = lax.dynamic_index_in_dim(current, mine, 0, keepdims=False).astype(F32)
    for step in range(1, 1 << len(last)):
        send = lax.dynamic_index_in_dim(current, mine ^ step, 0, keepdims=False)
        total = total + swap_bits(send.astype(BF16), count, step << shift).astype(F32)
    return total


def sum_all(value, count):
    bits = count.bit_length() - 1
    for bit in range(bits):
        value = value + swap_bits(value, count, 1 << bit)
    return value


def attend(query, keys, values, same_page, scaling):
    scores = jnp.einsum("bqhd,bkhd->bhqk", query, keys, preferred_element_type=F32) * scaling
    scores = jnp.where(same_page[:, None], scores, NEGATIVE)
    row_max = jnp.max(scores, axis=-1, keepdims=True)
    exp_scores = jnp.exp(scores - row_max)
    row_sum = jnp.sum(exp_scores, axis=-1, keepdims=True)
    weights_low = (exp_scores / row_sum).astype(BF16)
    context = jnp.einsum("bhqk,bkhd->bqhd", weights_low, values, preferred_element_type=F32)
    return (context.astype(BF16), weights_low)


def attend_backward(query, keys, values, probs, grad_context, scaling):
    grad_values = jnp.einsum("bhqk,bqhd->bkhd", probs, grad_context, preferred_element_type=F32)
    grad_probs = jnp.einsum("bqhd,bkhd->bhqk", grad_context, values, preferred_element_type=F32)
    probs_wide = probs.astype(F32)
    row_dot = jnp.sum(probs_wide * grad_probs, axis=-1, keepdims=True)
    grad_scores = (probs_wide * (grad_probs - row_dot)).astype(BF16)
    grad_query = jnp.einsum("bhqk,bkhd->bqhd", grad_scores, keys, preferred_element_type=F32)
    grad_keys = jnp.einsum("bhqk,bqhd->bkhd", grad_scores, query, preferred_element_type=F32)
    return (
        (grad_query * scaling).astype(BF16),
        (grad_keys * scaling).astype(BF16),
        grad_values.astype(BF16),
    )


def shards(
    dp_count,
    tokens_in,
    segment_ids,
    w_qkv,
    bias_qv,
    w_out,
    bias_out,
    norm1_gain,
    norm1_shift,
    w_in,
    bias_in,
    w_down,
    bias_down,
    norm2_gain,
    norm2_shift,
    grad_output,
):
    seq_count, seq_length = segment_ids.shape
    half_seqs = seq_count // 2
    rows = half_seqs * seq_length
    width = tokens_in.shape[1]
    local_cols = w_qkv.shape[2]
    head_count = local_cols // HEAD_DIM
    scaling = 1.0 / math.sqrt(HEAD_DIM)
    side = lax.axis_index("tensor")
    shape_four = (half_seqs, seq_length, head_count, HEAD_DIM)

    def my_half(array, size):
        return lax.dynamic_slice_in_dim(array, side * size, size, 0)

    tokens = my_half(tokens_in, rows)
    segments = my_half(segment_ids, half_seqs)
    upstream = my_half(grad_output, rows).astype(F32)
    same_page = segments[:, :, None] == segments[:, None, :]
    w_qkv_two = (w_qkv, swap_pair(w_qkv))
    bias_qv_two = (bias_qv, swap_pair(bias_qv))
    w_out_two = (w_out, swap_pair(w_out))
    w_in_two = (w_in, swap_pair(w_in))
    bias_in_two = (bias_in, swap_pair(bias_in))
    w_down_two = (w_down, swap_pair(w_down))

    saved = []
    attention = 0.0
    for wq, bq, wo in zip(w_qkv_two, bias_qv_two, w_out_two):
        projected = jnp.einsum("nd,jdc->jnc", tokens, wq, preferred_element_type=F32)
        query = (projected[0] + bq[0]).astype(BF16).reshape(shape_four)
        keys = projected[1].astype(BF16).reshape(shape_four)
        values = (projected[2] + bq[1]).astype(BF16).reshape(shape_four)
        context, probs = attend(query, keys, values, same_page, scaling)
        context = context.reshape(rows, local_cols)
        saved.append((query, keys, values, probs, context))
        part = jnp.dot(context, wo, preferred_element_type=F32).astype(BF16)
        attention = attention + part.astype(F32)
    normed_one, normed1, inv_std_one = norm_forward(
        tokens.astype(F32) + attention + bias_out, norm1_gain, norm1_shift
    )
    normed_low = normed_one.astype(BF16)
    feedforward = 0.0
    gelus = []
    for wi, bi, wd in zip(w_in_two, bias_in_two, w_down_two):
        preact = jnp.dot(normed_low, wi, preferred_element_type=F32) + bi
        hidden, derivative = gelu_pair(preact)
        hidden_low = hidden.astype(BF16)
        gelus.append((hidden_low, derivative))
        part = jnp.dot(hidden_low, wd, preferred_element_type=F32).astype(BF16)
        feedforward = feedforward + part.astype(F32)
    result, normed2, inv_std_two = norm_forward(
        normed_one + feedforward + bias_down, norm2_gain, norm2_shift
    )
    output = result.astype(BF16)
    grad_summed_two, grad_gain_two, grad_shift_two = norm_backward(
        upstream, normed2, inv_std_two, norm2_gain
    )
    grad_bias_down = jnp.sum(grad_summed_two, axis=0)
    grad_two_low = grad_summed_two.astype(BF16)
    grad_normed_one = grad_summed_two
    grads_down, grads_in, grads_bias_in = [], [], []
    for (hidden_low, derivative), wi, wd in zip(gelus, w_in_two, w_down_two):
        grads_down.append(
            jnp.einsum("nd,nf->df", grad_two_low, hidden_low, preferred_element_type=F32)
        )
        grad_hidden = jnp.einsum("nd,fd->nf", grad_two_low, wd, preferred_element_type=F32)
        grad_preact = (grad_hidden * derivative).astype(BF16)
        grads_bias_in.append(jnp.sum(grad_preact, axis=0, dtype=F32))
        grads_in.append(
            jnp.einsum("nd,nf->df", normed_low, grad_preact, preferred_element_type=F32)
        )
        part = jnp.einsum("nf,df->nd", grad_preact, wi, preferred_element_type=F32)
        grad_normed_one = grad_normed_one + part.astype(BF16).astype(F32)

    def pair_sum(two):
        return two[0] + swap_pair(two[1].astype(BF16)).astype(F32)

    summed_w_down = scatter_rows(pair_sum(grads_down), dp_count, True).T
    summed_w_in = scatter_rows(pair_sum(grads_in), dp_count, False)

    grad_summed_one, grad_gain_one, grad_shift_one = norm_backward(
        grad_normed_one, normed1, inv_std_one, norm1_gain
    )
    grad_bias_out = jnp.sum(grad_summed_one, axis=0)
    grad_one_low = grad_summed_one.astype(BF16)
    grads_out, grads_qkv, grads_bias_qv = [], [], []
    grad_input = grad_summed_one
    for (query, keys, values, probs, context), wq, wo in zip(saved, w_qkv_two, w_out_two):
        grads_out.append(
            jnp.einsum("nd,nc->dc", grad_one_low, context, preferred_element_type=F32)
        )
        grad_context = jnp.einsum(
            "nd,cd->nc", grad_one_low, wo, preferred_element_type=F32
        ).astype(BF16)
        triple = attend_backward(
            query, keys, values, probs, grad_context.reshape(shape_four), scaling
        )
        flat = [member.reshape(rows, local_cols) for member in triple]
        grads_bias_qv.append(
            jnp.concatenate([jnp.sum(flat[0], axis=0, dtype=F32), jnp.sum(flat[2], axis=0, dtype=F32)])
        )
        grads_qkv.append(
            jnp.concatenate(
                [jnp.einsum("nd,nc->dc", tokens, m, preferred_element_type=F32) for m in flat], axis=1
            )
        )
        part = sum(
            jnp.einsum("nc,dc->nd", m, w, preferred_element_type=F32) for m, w in zip(flat, wq)
        )
        grad_input = grad_input + part.astype(BF16).astype(F32)
    grad_input = grad_input.astype(BF16)

    summed_w_out = scatter_rows(pair_sum(grads_out), dp_count, False).T
    qkv_rows = pair_sum(grads_qkv)
    middle = qkv_rows.shape[1] // 3
    middle = middle + middle // 2
    summed_qkv = jnp.concatenate(
        [
            scatter_rows(qkv_rows[:, :middle], dp_count, False),
            scatter_rows(qkv_rows[:, middle:], dp_count, True),
        ],
        axis=1,
    )
    summed_w_qkv = jnp.swapaxes(summed_qkv.reshape(-1, 3, local_cols), 0, 1)

    common = [
        grad_bias_out,
        grad_gain_one,
        grad_shift_one,
        grad_bias_down,
        grad_gain_two,
        grad_shift_two,
    ]
    own_vec = jnp.concatenate([grads_bias_qv[0], grads_bias_in[0]] + common)
    other_vec = jnp.concatenate([grads_bias_qv[1], grads_bias_in[1]] + common)
    vec = sum_all(own_vec + swap_pair(other_vec), dp_count)
    cut = 2 * local_cols
    summed_bias_qv = vec[:cut].reshape(2, local_cols)
    summed_bias_in = vec[cut : cut + bias_in.shape[0]]
    tail = vec[cut + bias_in.shape[0] :].reshape(6, width)

    def whole(mine):
        other = swap_pair(mine)
        both = jnp.zeros((2,) + mine.shape, mine.dtype)
        both = lax.dynamic_update_index_in_dim(both, mine, side, 0)
        both = lax.dynamic_update_index_in_dim(both, other, 1 - side, 0)
        return both.reshape((2 * mine.shape[0],) + mine.shape[1:])

    return (
        whole(output),
        whole(grad_input),
        summed_w_qkv,
        summed_bias_qv,
        summed_w_out,
        tail[0],
        tail[1],
        tail[2],
        summed_w_in,
        summed_bias_in,
        summed_w_down,
        tail[3],
        tail[4],
        tail[5],
    )


def solution(mesh):
    dp_count = mesh.shape["dp"]

    def body(*args):
        return shards(dp_count, *args)

    return jax.shard_map(
        body,
        mesh=mesh,
        in_specs=(
            P("dp", None),
            P("dp", None),
            P(None, None, "tensor"),
            P(None, "tensor"),
            P("tensor", None),
            P(),
            P(),
            P(),
            P(None, "tensor"),
            P("tensor"),
            P("tensor", None),
            P(),
            P(),
            P(),
            P("dp", None),
        ),
        out_specs=(
            P("dp", None),
            P("dp", None),
            P(None, "dp", "tensor"),
            P(None, "tensor"),
            P("tensor", "dp"),
            P(),
            P(),
            P(),
            P("dp", "tensor"),
            P("tensor"),
            P("tensor", "dp"),
            P(),
            P(),
            P(),
        ),
        check_vma=False,
    )
```

```python
import functools
import math

import jax
import jax.numpy as jnp
from jax import lax
from jax.experimental import pallas as pl
from jax.experimental.pallas import tpu as pltpu
from jax.sharding import PartitionSpec as P

HEAD_DIM = 64


EPSILON = 1e-05
NEGATIVE = -1e30
ROOT_HALF = 0.7071067811865476
ROOT_TWO_PI_INV = 0.3989422804014327
F32 = jnp.float32
BF16 = jnp.bfloat16


def norm_forward(summed, gain_vec, shift_vec):
    centered = summed - jnp.mean(summed, axis=-1, keepdims=True)
    variance = jnp.mean(centered * centered, axis=-1, keepdims=True)
    inv_std = lax.rsqrt(variance + EPSILON)
    normed = centered * inv_std
    return (normed * gain_vec + shift_vec, normed, inv_std)


def norm_backward(upstream, normed, inv_std, gain_vec):
    scaled_grad = upstream * gain_vec
    first_mean = jnp.mean(scaled_grad, axis=-1, keepdims=True)
    second_mean = jnp.mean(scaled_grad * normed, axis=-1, keepdims=True)
    grad_summed = inv_std * (scaled_grad - first_mean - normed * second_mean)
    return (grad_summed, jnp.sum(upstream * normed, axis=0), jnp.sum(upstream, axis=0))


def gelu_pair(preact):
    cumulative = 0.5 * (1.0 + lax.erf(preact * ROOT_HALF))
    derivative = cumulative + preact * jnp.exp(-0.5 * preact * preact) * ROOT_TWO_PI_INV
    return (preact * cumulative, derivative)


def swap_pair(value):
    return lax.ppermute(value, "tensor", [(0, 1), (1, 0)])


def swap_bits(value, count, mask):
    return lax.ppermute(value, "dp", [(i, i ^ mask) for i in range(count)])


def fence(values, *others):
    return lax.optimization_barrier((values,) + others)


class RowScatter:
    def __init__(self, partial, count, order):
        rows, cols = partial.shape
        bits = count.bit_length() - 1
        order = [bit for bit in order if bit < bits]
        self.order = order + [bit for bit in range(bits) if bit not in order]
        self.count = count
        self.index = lax.axis_index("dp")
        self.alive = list(range(bits - 1, -1, -1))
        self.current = partial.reshape((2,) * bits + (rows // count, cols))

    def send(self):
        bit = self.order.pop(0)
        axis = self.alive.index(bit)
        self.alive.remove(bit)
        mine = (self.index >> bit) & 1
        self.keep = lax.dynamic_index_in_dim(self.current, mine, axis, keepdims=False)
        away = lax.dynamic_index_in_dim(self.current, 1 - mine, axis, keepdims=False)
        self.received = swap_bits(away.astype(BF16), self.count, 1 << bit)

    def add(self, dtype=BF16):
        total = self.keep.astype(F32) + self.received.astype(F32)
        self.current = total.astype(dtype) if self.order else total

    def finish(self):
        while self.order:
            self.send()
            self.add()
        return self.current


def sum_all(value, count):
    bits = count.bit_length() - 1
    for bit in range(bits):
        value = value + swap_bits(value, count, 1 << bit)
    return value


NT = (((1,), (1,)), ((), ()))
NN = (((1,), (0,)), ((), ()))
PAIR = 2 * HEAD_DIM
VMEM_LIMIT = 56 * 1024 * 1024


def dot(left, right, dims=NN):
    return lax.dot_general(left, right, dims, preferred_element_type=F32)


def attend_kernel(
    tok_ref, pen_ref, hot_ref, wq_ref, bq_ref, wo_ref, q_ref, k_ref, v_ref, p_ref, c_ref, part_ref
):
    tok = tok_ref[...]
    scale = 1.0 / math.sqrt(HEAD_DIM)
    bias = bq_ref[...].astype(F32)
    q_ref[...] = ((dot(tok, wq_ref[0]) + bias[0:1]).astype(BF16) * scale).astype(BF16)
    k_ref[...] = dot(tok, wq_ref[1]).astype(BF16)
    v_ref[...] = (dot(tok, wq_ref[2]) + bias[1:2]).astype(BF16)
    rows, cols = q_ref.shape
    lane = lax.broadcasted_iota(jnp.int32, (rows, PAIR), 1)
    zero = jnp.zeros((rows, PAIR), BF16)
    for pair in range(cols // PAIR):
        at = pl.ds(pair * PAIR, PAIR)
        q = q_ref[:, at]
        v = v_ref[:, at]
        k_wide = jnp.concatenate([k_ref[:, at], hot_ref[...]], axis=1)
        outs = []
        for half in range(2):
            mine = (lane < HEAD_DIM) if half == 0 else (lane >= HEAD_DIM)
            q_wide = jnp.concatenate([jnp.where(mine, q, zero), pen_ref[...]], axis=1)
            scores = dot(q_wide, k_wide, NT)
            top = jnp.max(scores, axis=1, keepdims=True)
            exp_scores = jnp.exp(scores - top)
            total = jnp.sum(exp_scores, axis=1, keepdims=True)
            probs = (exp_scores * (1.0 / total)).astype(BF16)
            p_ref[0, pair * 2 + half] = probs
            outs.append(dot(probs, v))
        c_ref[:, at] = jnp.where(lane < HEAD_DIM, outs[0], outs[1]).astype(BF16)
    part_ref[...] = dot(c_ref[...], wo_ref[...]).astype(BF16)


def rows_spec(n, c):
    return pl.BlockSpec((n, c), lambda i: (i, 0))


def fixed_spec(shape):
    return pl.BlockSpec(shape, lambda i: (0,) * len(shape), pipeline_mode=pl.Buffered(1))


def attend(tok, pen, hot, wq, bq, wo, seqs):
    rows, width = tok.shape
    n = rows // seqs
    cols = wq.shape[2]
    heads = cols // HEAD_DIM
    sd = jax.ShapeDtypeStruct
    return pl.pallas_call(
        attend_kernel,
        grid=(seqs,),
        in_specs=[
            rows_spec(n, width),
            rows_spec(n, 128),
            rows_spec(n, 128),
            fixed_spec(wq.shape),
            fixed_spec(bq.shape),
            fixed_spec(wo.shape),
        ],
        out_specs=[rows_spec(n, cols)] * 3
        + [pl.BlockSpec((1, heads, n, n), lambda i: (i, 0, 0, 0)), rows_spec(n, cols), rows_spec(n, width)],
        out_shape=[sd((rows, cols), BF16)] * 3
        + [sd((seqs, heads, n, n), BF16), sd((rows, cols), BF16), sd((rows, width), BF16)],
        compiler_params=pltpu.CompilerParams(vmem_limit_bytes=VMEM_LIMIT),
        cost_estimate=pl.CostEstimate(
            flops=8 * rows * width * cols + 12 * rows * n * cols,
            bytes_accessed=2 * (rows * n * heads + 7 * rows * cols + 4 * width * cols),
            transcendentals=rows * n * heads,
        ),
        name="attend",
    )(tok, pen, hot, wq, bq, wo)


def attend_back_kernel(
    groups, g_ref, tok_ref, q_ref, k_ref, v_ref, p_ref, c_ref, wq_ref, wo_ref,
    part_ref, grad_ref, bias_ref, d_ref, acc_ref,
):
    step = pl.program_id(0)
    rows, cols = q_ref.shape
    scale = 1.0 / math.sqrt(HEAD_DIM)
    g = g_ref[...]
    grad_context = dot(g, wo_ref[...], NT).astype(BF16)
    lane = lax.broadcasted_iota(jnp.int32, (rows, PAIR), 1)
    low = lane < HEAD_DIM
    zero = jnp.zeros((rows, PAIR), BF16)
    for pair in range(cols // PAIR):
        lo = pair * PAIR
        at = pl.ds(lo, PAIR)
        q = q_ref[:, at]
        v = v_ref[:, at]
        k = k_ref[:, at]
        do = grad_context[:, lo : lo + PAIR]
        product = do.astype(F32) * c_ref[:, at].astype(F32)
        q_t = q.T
        do_t = do.T
        grads_q, grads_k, grads_v = [], [], []
        for half in range(2):
            mine = low if half == 0 else lane >= HEAD_DIM
            row_dot = jnp.sum(jnp.where(mine, product, 0.0), axis=1, keepdims=True)
            probs = p_ref[0, pair * 2 + half]
            grad_probs = dot(jnp.where(mine, do, zero), v, NT)
            grad_scores = (probs.astype(F32) * (grad_probs - row_dot)).astype(BF16)
            grads_q.append(dot(grad_scores, k))
            own = slice(half * HEAD_DIM, (half + 1) * HEAD_DIM)
            grads_k.append(dot(q_t[own], grad_scores))
            grads_v.append(dot(do_t[own], probs))
        d_ref[0, :, at] = (jnp.where(low, grads_q[0], grads_q[1]) * scale).astype(BF16)
        d_ref[1, :, at] = jnp.concatenate(grads_k, axis=0).T.astype(BF16)
        d_ref[2, :, at] = jnp.concatenate(grads_v, axis=0).T.astype(BF16)
    part = (
        dot(d_ref[0], wq_ref[0], NT) + dot(d_ref[1], wq_ref[1], NT) + dot(d_ref[2], wq_ref[2], NT)
    )
    part_ref[...] = part.astype(BF16)
    tok_t = tok_ref[...].T
    new = [dot(tok_t, d_ref[0]), dot(tok_t, d_ref[1]), dot(tok_t, d_ref[2]), dot(g.T, c_ref[...])]
    bias = [jnp.sum(d_ref[j].astype(F32), axis=0, keepdims=True) for j in (0, 2)]

    @pl.when(step == 0)
    def _():
        for j in range(4):
            acc_ref[j] = new[j]
        for j in range(2):
            bias_ref[j : j + 1] = bias[j]

    @pl.when(step > 0)
    def _():
        for j in range(4):
            acc_ref[j] = acc_ref[j] + new[j]
        for j in range(2):
            bias_ref[j : j + 1] = bias_ref[j : j + 1] + bias[j]

    @pl.when(step == pl.num_programs(0) - 1)
    def _():
        at, start = 0, 0
        for group in groups:
            size = group * PAIR
            for j in range(4):
                grad_ref[:, at : at + size] = acc_ref[j][:, start : start + size].astype(BF16)
                at = at + size
            start = start + size


def attend_back(g, tok, q, k, v, p, c, wq, wo, seqs, pairs):
    rows, width = tok.shape
    n = rows // seqs
    size = len(pairs)
    cols = size * PAIR
    block = pairs[0] // size
    groups = (2, 1) if size == 3 else (size,)
    sd = jax.ShapeDtypeStruct
    column = pl.BlockSpec((n, cols), lambda i: (i, block))
    once = pl.Buffered(1)
    return pl.pallas_call(
        functools.partial(attend_back_kernel, groups),
        grid=(seqs,),
        in_specs=[rows_spec(n, width)] * 2
        + [column] * 3
        + [
            pl.BlockSpec((1, 2 * size, n, n), lambda i: (i, block, 0, 0)),
            column,
            pl.BlockSpec((3, width, cols), lambda i: (0, 0, block), pipeline_mode=once),
            pl.BlockSpec((cols, width), lambda i: (block, 0), pipeline_mode=once),
        ],
        out_specs=[rows_spec(n, width), fixed_spec((width, 4 * cols)), fixed_spec((2, cols))],
        out_shape=[sd((rows, width), BF16), sd((width, 4 * cols), BF16), sd((2, cols), F32)],
        scratch_shapes=[pltpu.VMEM((3, n, cols), BF16), pltpu.VMEM((4, width, cols), F32)],
        compiler_params=pltpu.CompilerParams(vmem_limit_bytes=VMEM_LIMIT),
        cost_estimate=pl.CostEstimate(
            flops=16 * rows * width * cols + 16 * rows * n * cols,
            bytes_accessed=2 * (2 * rows * n * size + 8 * rows * cols + 8 * width * cols),
            transcendentals=0,
        ),
        name="attend_back",
    )(g, tok, q, k, v, p, c, wq, wo)


def shards(
    dp_count,
    tokens_in,
    segment_ids,
    w_qkv,
    bias_qv,
    w_out,
    bias_out,
    norm1_gain,
    norm1_shift,
    w_in,
    bias_in,
    w_down,
    bias_down,
    norm2_gain,
    norm2_shift,
    grad_output,
):
    seq_count, seq_length = segment_ids.shape
    half_seqs = seq_count // 2
    rows = half_seqs * seq_length
    width = tokens_in.shape[1]
    local_cols = w_qkv.shape[2]
    side = lax.axis_index("tensor")

    def my_half(array, size):
        return lax.dynamic_slice_in_dim(array, side * size, size, 0)

    tokens = my_half(tokens_in, rows)
    segments = my_half(segment_ids, half_seqs)
    upstream = my_half(grad_output, rows).astype(F32)
    page = segments.reshape(rows, 1)
    lanes = lax.broadcasted_iota(jnp.int32, (1, 128), 1)
    hot = (page == lanes).astype(BF16)
    pen = jnp.where((page != lanes) & (lanes < 4), NEGATIVE, 0.0).astype(BF16)
    w_qkv_two = (w_qkv, swap_pair(w_qkv))
    bias_qv_two = (bias_qv, swap_pair(bias_qv))
    w_out_two = (w_out, swap_pair(w_out))
    w_in_two = (w_in, swap_pair(w_in))
    bias_in_two = (bias_in, swap_pair(bias_in))
    w_down_two = (w_down, swap_pair(w_down))

    saved = []
    attention = 0.0
    for wq, bq, wo in zip(w_qkv_two, bias_qv_two, w_out_two):
        *kept, part = attend(tokens, pen, hot, wq, bq, wo, half_seqs)
        saved.append(kept)
        attention = attention + part.astype(F32)
    normed_one, normed1, inv_std_one = norm_forward(
        tokens.astype(F32) + attention + bias_out, norm1_gain, norm1_shift
    )
    normed_low = normed_one.astype(BF16)
    feedforward = 0.0
    gelus = []
    for wi, bi, wd in zip(w_in_two, bias_in_two, w_down_two):
        preact = jnp.dot(normed_low, wi, preferred_element_type=F32) + bi
        hidden, derivative = gelu_pair(preact)
        hidden_low = hidden.astype(BF16)
        gelus.append((hidden_low, derivative))
        part = jnp.dot(hidden_low, wd, preferred_element_type=F32).astype(BF16)
        feedforward = feedforward + part.astype(F32)
    result, normed2, inv_std_two = norm_forward(
        normed_one + feedforward + bias_down, norm2_gain, norm2_shift
    )
    output = result.astype(BF16)
    grad_summed_two, grad_gain_two, grad_shift_two = norm_backward(
        upstream, normed2, inv_std_two, norm2_gain
    )
    grad_bias_down = jnp.sum(grad_summed_two, axis=0)
    grad_two_low = grad_summed_two.astype(BF16)
    grad_normed_one = grad_summed_two
    two = (0, 1)
    count = dp_count

    def outer(left, right):
        return jnp.einsum("nd,nf->df", left, right, preferred_element_type=F32)

    down_recv = swap_pair(outer(grad_two_low, gelus[1][0]).astype(BF16))
    grads_preact = []
    for at in two:
        grad_hidden = jnp.einsum("nd,fd->nf", grad_two_low, w_down_two[at], preferred_element_type=F32)
        grads_preact.append((grad_hidden * gelus[at][1]).astype(BF16))
    grads_bias_in = [jnp.sum(m, axis=0, dtype=F32) for m in grads_preact]
    in_recv = swap_pair(outer(normed_low, grads_preact[1]).astype(BF16))
    down = RowScatter(
        (outer(grad_two_low, gelus[0][0]) + down_recv.astype(F32)).astype(BF16), count, (0, 2, 3, 1)
    )
    down.send()
    for at in two:
        part = jnp.einsum("nf,df->nd", grads_preact[at], w_in_two[at], preferred_element_type=F32)
        grad_normed_one = grad_normed_one + part.astype(BF16).astype(F32)
    inner = RowScatter(
        (outer(normed_low, grads_preact[0]) + in_recv.astype(F32)).astype(BF16), count, (1, 2, 3, 0)
    )
    inner.send()
    grad_summed_one, grad_gain_one, grad_shift_one = norm_backward(
        grad_normed_one, normed1, inv_std_one, norm1_gain
    )
    grad_bias_out = jnp.sum(grad_summed_one, axis=0)
    grad_one_low = grad_summed_one.astype(BF16)

    def back(at, g, pairs):
        q, k, v, p, c = saved[at]
        return attend_back(g, tokens, q, k, v, p, c, w_qkv_two[at], w_out_two[at], half_seqs, pairs)

    grad_one_low, down.received = fence(grad_one_low, down.received)
    down.add()
    down.send()
    part_other, grads_other, bias_other = back(1, grad_one_low, (0, 1, 2))
    cut = 2 * PAIR
    split = 4 * cut
    first_recv = swap_pair(grads_other[:, :split])
    second_recv = swap_pair(grads_other[:, split:])
    grad_one_low, part_other, inner.received, down.received, first_recv, second_recv = fence(
        grad_one_low, part_other, inner.received, down.received, first_recv, second_recv
    )
    down.add()
    down.send()
    inner.add()
    inner.send()
    part_first, grads_first, bias_first = back(0, grad_one_low, (0, 1))
    first = RowScatter(
        (grads_first.astype(F32) + first_recv.astype(F32)).astype(BF16), count, (0, 2, 3, 1)
    )
    grad_one_low, part_first, inner.received, down.received = fence(
        grad_one_low, part_first, inner.received, down.received
    )
    first.send()
    down.add()
    down.send()
    inner.add()
    inner.send()
    part_second, grads_second, bias_second = back(0, grad_one_low, (2,))
    second = RowScatter(
        (grads_second.astype(F32) + second_recv.astype(F32)).astype(BF16), count, (1, 0, 2, 3)
    )
    part_own = part_first.astype(F32) + part_second.astype(F32)
    grad_input = (grad_summed_one + part_own + part_other.astype(F32)).astype(BF16)
    down.add()
    inner.add()
    first.add()
    summed_w_down = down.finish().T
    summed_w_in = inner.finish()
    summed_first = first.finish()
    summed_second = second.finish()
    pieces = [
        jnp.concatenate([summed_first[:, j * cut : (j + 1) * cut], summed_second[:, j * PAIR : (j + 1) * PAIR]], axis=1)
        for j in range(4)
    ]
    summed_w_qkv = jnp.stack(pieces[:3])
    summed_w_out = pieces[3].T
    grads_bias_qv = [jnp.concatenate([bias_first, bias_second], axis=1).reshape(-1), bias_other.reshape(-1)]

    common = [
        grad_bias_out,
        grad_gain_one,
        grad_shift_one,
        grad_bias_down,
        grad_gain_two,
        grad_shift_two,
    ]
    own_vec = jnp.concatenate([grads_bias_in[0]] + common)
    other_vec = jnp.concatenate([grads_bias_in[1]] + common)
    vec = sum_all(own_vec + swap_pair(other_vec), dp_count)
    summed_bias_in = vec[: bias_in.shape[0]]
    tail = vec[bias_in.shape[0] :].reshape(6, width)
    bias_vec = sum_all(grads_bias_qv[0] + swap_pair(grads_bias_qv[1]), dp_count)
    summed_bias_qv = bias_vec.reshape(2, local_cols)

    def whole(mine):
        other = swap_pair(mine)
        both = jnp.zeros((2,) + mine.shape, mine.dtype)
        both = lax.dynamic_update_index_in_dim(both, mine, side, 0)
        both = lax.dynamic_update_index_in_dim(both, other, 1 - side, 0)
        return both.reshape((2 * mine.shape[0],) + mine.shape[1:])

    return (
        whole(output),
        whole(grad_input),
        summed_w_qkv,
        summed_bias_qv,
        summed_w_out,
        tail[0],
        tail[1],
        tail[2],
        summed_w_in,
        summed_bias_in,
        summed_w_down,
        tail[3],
        tail[4],
        tail[5],
    )


def solution(mesh):
    dp_count = mesh.shape["dp"]

    def body(*args):
        return shards(dp_count, *args)

    return jax.shard_map(
        body,
        mesh=mesh,
        in_specs=(
            P("dp", None),
            P("dp", None),
            P(None, None, "tensor"),
            P(None, "tensor"),
            P("tensor", None),
            P(),
            P(),
            P(),
            P(None, "tensor"),
            P("tensor"),
            P("tensor", None),
            P(),
            P(),
            P(),
            P("dp", None),
        ),
        out_specs=(
            P("dp", None),
            P("dp", None),
            P(None, "dp", "tensor"),
            P(None, "tensor"),
            P("tensor", "dp"),
            P(),
            P(),
            P(),
            P("dp", "tensor"),
            P("tensor"),
            P("tensor", "dp"),
            P(),
            P(),
            P(),
        ),
        check_vma=False,
    )
```

```python
import functools
import math

import jax
import jax.numpy as jnp
from jax import lax
from jax.experimental import pallas as pl
from jax.experimental.pallas import tpu as pltpu
from jax.sharding import PartitionSpec as P

HEAD_DIM = 64
PAIR = 2 * HEAD_DIM
LANES = 128


EPSILON = 1e-05
NEGATIVE = -1e30
ROOT_HALF = 0.7071067811865476
ROOT_TWO_PI_INV = 0.3989422804014327
F32 = jnp.float32
BF16 = jnp.bfloat16
NT = (((1,), (1,)), ((), ()))
NN = (((1,), (0,)), ((), ()))
VMEM_LIMIT = 56 * 1024 * 1024
CHUNK = 512
sd = jax.ShapeDtypeStruct


def dot(left, right, dims=NN):
    return lax.dot_general(left, right, dims, preferred_element_type=F32)


def mean_of(value):
    return jnp.sum(value, axis=1, keepdims=True) * (1.0 / value.shape[1])


def norm_forward(summed):
    centered = summed - mean_of(summed)
    inv_std = lax.rsqrt(mean_of(centered * centered) + EPSILON)
    return (centered * inv_std, inv_std)


def norm_backward(upstream, normed, inv_std, gain_vec):
    scaled_grad = upstream * gain_vec
    second_mean = mean_of(scaled_grad * normed)
    return inv_std * (scaled_grad - mean_of(scaled_grad) - normed * second_mean)


def gelu_pair(preact):
    cumulative = 0.5 + 0.5 * lax.erf(preact * ROOT_HALF)
    derivative = cumulative + preact * (jnp.exp(-0.5 * preact * preact) * ROOT_TWO_PI_INV)
    return (preact * cumulative, derivative)


def column_sum(value):
    return jnp.sum(value, axis=0, keepdims=True)


def rows_spec(n, c):
    return pl.BlockSpec((n, c), lambda i, s: (i, 0))


def side_spec(n, c, steps):
    return pl.BlockSpec((n, c), lambda i, s: (s[0] * steps + i, 0))


def fixed_spec(shape):
    return pl.BlockSpec(shape, lambda i, s: (0,) * len(shape), pipeline_mode=pl.Buffered(1))


def call(kernel, name, grid, in_specs, out_specs, out_shape, scratch, cost):
    flops, moved, transcendentals = cost
    return pl.pallas_call(
        kernel,
        grid_spec=pltpu.PrefetchScalarGridSpec(
            num_scalar_prefetch=1,
            grid=grid,
            in_specs=in_specs,
            out_specs=out_specs,
            scratch_shapes=scratch,
        ),
        out_shape=out_shape,
        compiler_params=pltpu.CompilerParams(vmem_limit_bytes=VMEM_LIMIT),
        cost_estimate=pl.CostEstimate(
            flops=flops, bytes_accessed=moved, transcendentals=transcendentals
        ),
        name=name,
    )


def put_transposed(out_ref, value, scratch, me, masks):
    scratch[...] = value.T.reshape(scratch.shape)
    if len(masks) == 1:
        out_ref[...] = scratch[...]
    else:
        for j, mask in enumerate(masks):
            out_ref[j] = scratch[me ^ mask]


def page_columns(page):
    line = lax.broadcasted_iota(jnp.int32, (LANES, page.shape[1]), 0)
    same = jnp.where(line == page, 1.0, 0.0).T
    lane = lax.broadcasted_iota(jnp.int32, same.shape, 1)
    pen = jnp.where((lane < 4) & (same == 0.0), NEGATIVE, 0.0)
    return (pen.astype(BF16), same.astype(BF16))


def attend_kernel(
    masks, scalars, tok_ref, seg_ref, wq_ref, bq_ref, wo_ref, q_ref, k_ref, v_ref, p_ref, c_ref, part_ref, *rest
):
    if masks:
        put_transposed(rest[0], tok_ref[...], rest[1], scalars[1], masks)
    row = scalars[0] * pl.num_programs(0) + pl.program_id(0)
    pen, hot = page_columns(seg_ref[pl.ds(row, 1), :])
    tok = tok_ref[...]
    scale = 1.0 / math.sqrt(HEAD_DIM)
    bias = bq_ref[...].astype(F32)
    q_ref[...] = ((dot(tok, wq_ref[0]) + bias[0:1]).astype(BF16) * scale).astype(BF16)
    k_ref[...] = dot(tok, wq_ref[1]).astype(BF16)
    v_ref[...] = (dot(tok, wq_ref[2]) + bias[1:2]).astype(BF16)
    rows, cols = q_ref.shape
    lane = lax.broadcasted_iota(jnp.int32, (rows, PAIR), 1)
    zero = jnp.zeros((rows, PAIR), BF16)
    for pair in range(cols // PAIR):
        at = pl.ds(pair * PAIR, PAIR)
        q = q_ref[:, at]
        v = v_ref[:, at]
        k_wide = jnp.concatenate([k_ref[:, at], hot], axis=1)
        outs = []
        for half in range(2):
            mine = (lane < HEAD_DIM) if half == 0 else (lane >= HEAD_DIM)
            q_wide = jnp.concatenate([jnp.where(mine, q, zero), pen], axis=1)
            scores = dot(q_wide, k_wide, NT)
            top = jnp.max(scores, axis=1, keepdims=True)
            exp_scores = jnp.exp(scores - top)
            total = jnp.sum(exp_scores, axis=1, keepdims=True)
            probs = (exp_scores * (1.0 / total)).astype(BF16)
            p_ref[0, pair * 2 + half] = probs
            outs.append(dot(probs, v))
        c_ref[:, at] = jnp.where(lane < HEAD_DIM, outs[0], outs[1]).astype(BF16)
    part_ref[...] = dot(c_ref[...], wo_ref[...]).astype(BF16)


def attend(scalars, tok, seg, wq, bq, wo, order):
    width = tok.shape[1]
    seqs = seg.shape[0] // 2
    n = seg.shape[1]
    rows = seqs * n
    cols = wq.shape[2]
    heads = cols // HEAD_DIM
    masks, shape = order_blocks(width, order) if order else ((), ())
    return call(
        functools.partial(attend_kernel, masks),
        "attend",
        (seqs,),
        [
            side_spec(n, width, seqs),
            fixed_spec(seg.shape),
            fixed_spec(wq.shape),
            fixed_spec(bq.shape),
            fixed_spec(wo.shape),
        ],
        [rows_spec(n, cols)] * 3
        + [
            pl.BlockSpec((1, heads, n, n), lambda i, s: (i, 0, 0, 0)),
            rows_spec(n, cols),
            rows_spec(n, width),
        ]
        + [transposed_spec(shape, n)] * bool(masks),
        [sd((rows, cols), BF16)] * 3
        + [sd((seqs, heads, n, n), BF16), sd((rows, cols), BF16), sd((rows, width), BF16)]
        + [sd(shape + (rows,), BF16)] * bool(masks),
        [pltpu.VMEM(shape + (n,), BF16)] * bool(masks),
        (
            8 * rows * width * cols + 12 * rows * n * cols,
            2 * (rows * n * heads + 7 * rows * cols + 4 * width * cols),
            rows * n * heads,
        ),
    )(scalars, tok, seg, wq, bq, wo)


def mlp_kernel(
    masks, scalars, tok_ref, pa_ref, pb_ref, up_ref, vec_ref, ba_ref, bb_ref,
    wia_hbm, wib_hbm, wda_hbm, wdb_hbm,
    out_ref, mine_ref, g2t_ref, lowt_ref, g1t_ref, ha_ref, hb_ref, gpa_ref, gpb_ref, g1_ref, g1low_ref,
    sumsa_ref, sumsb_ref,
    wia, wib, wda, wdb, dv_ref, low_ref, g2low_ref, turn, sem,
):
    step = pl.program_id(0)
    pairs = ((wia_hbm, wia), (wib_hbm, wib), (wda_hbm, wda), (wdb_hbm, wdb))
    copies = [pltpu.make_async_copy(s, d, sem.at[i]) for i, (s, d) in enumerate(pairs)]

    @pl.when(step == 0)
    def _():
        for copy in copies:
            copy.start()

    def arrive(i):
        @pl.when(step == 0)
        def _():
            copies[i].wait()

    vec = vec_ref[...].astype(F32)
    bias_out, gain1, shift1, bias_down, gain2, shift2 = [vec[i : i + 1] for i in range(6)]
    attention = pa_ref[...].astype(F32) + pb_ref[...].astype(F32)
    normed1, inv1 = norm_forward(tok_ref[...].astype(F32) + attention + bias_out)
    normed_one = normed1 * gain1 + shift1
    low_ref[...] = normed_one.astype(BF16)
    f = wia.shape[1]
    for k, (wi, bi) in enumerate(((wia, ba_ref), (wib, bb_ref))):
        arrive(k)
        for c in range(0, f, CHUNK):
            preact = dot(low_ref[...], wi[:, c : c + CHUNK]) + bi[:, c : c + CHUNK].astype(F32)
            hidden, derivative = gelu_pair(preact)
            at = k * f + c
            h_ref = (ha_ref, hb_ref)[k]
            h_ref[:, c : c + CHUNK] = hidden.astype(BF16)
            dv_ref[:, at : at + CHUNK] = derivative.astype(BF16)
    put_transposed(lowt_ref, low_ref[...], turn, scalars[1], masks[1])
    parts = []
    for k, (wd, h_ref) in enumerate(((wda, ha_ref), (wdb, hb_ref))):
        arrive(2 + k)
        parts.append(dot(h_ref[...], wd[...]).astype(BF16).astype(F32))
    normed2, inv2 = norm_forward(normed_one + (parts[0] + parts[1]) + bias_down)
    mine_ref[...] = (normed2 * gain2 + shift2).astype(BF16)
    out_ref[...] = mine_ref[...]
    up = up_ref[...].astype(F32)
    g2 = norm_backward(up, normed2, inv2, gain2)
    g2low_ref[...] = g2.astype(BF16)
    stats = [column_sum(g2), column_sum(up * normed2), column_sum(up)]
    put_transposed(g2t_ref, g2low_ref[...], turn, scalars[1], masks[0])
    sums = []
    for k, (wd, gp_ref) in enumerate(((wda, gpa_ref), (wdb, gpb_ref))):
        for c in range(0, f, CHUNK):
            at = k * f + c
            grad_hidden = dot(g2low_ref[...], wd[c : c + CHUNK, :], NT)
            grad_preact = (grad_hidden * dv_ref[:, at : at + CHUNK].astype(F32)).astype(BF16)
            gp_ref[:, c : c + CHUNK] = grad_preact
            sums.append(column_sum(grad_preact.astype(F32)))
    parts = []
    for wi, gp_ref in ((wia, gpa_ref), (wib, gpb_ref)):
        parts.append(dot(gp_ref[...], wi[...], NT).astype(BF16).astype(F32))
    grad = g2 + (parts[0] + parts[1])
    g1 = norm_backward(grad, normed1, inv1, gain1)
    g1_ref[...] = g1
    g1low_ref[...] = g1.astype(BF16)
    put_transposed(g1t_ref, g1low_ref[...], turn, scalars[1], masks[2])
    stats = [column_sum(g1), column_sum(grad * normed1), column_sum(grad)] + stats
    width = g1.shape[1]
    lines = [
        jnp.concatenate(s, axis=1)
        for s in (sums[: f // CHUNK], sums[f // CHUNK :])
    ]
    for line, sums_ref in zip(lines, (sumsa_ref, sumsb_ref)):
        block = [line[:, c : c + width] for c in range(0, f, width)] + stats
        block = jnp.concatenate(block, axis=0)

        @pl.when(step == 0)
        def _():
            sums_ref[...] = block

        @pl.when(step > 0)
        def _():
            sums_ref[...] = sums_ref[...] + block


def mlp(scalars, tok, pa, pb, up, vec, ba, bb, wia, wib, wda, wdb, tile, orders):
    rows, width = pa.shape
    f = wia.shape[1]
    steps = rows // tile
    hbm = pl.BlockSpec(memory_space=pl.ANY)
    tok_spec = rows_spec(tile, width)
    mine_spec = side_spec(tile, width, steps)
    masks = [order_blocks(width, order)[0] for order in orders]
    shape = order_blocks(width, orders[0])[1]
    lines = f // width + 6
    return call(
        functools.partial(mlp_kernel, masks),
        "mlp",
        (steps,),
        [mine_spec, tok_spec, tok_spec, mine_spec]
        + [fixed_spec(vec.shape), fixed_spec(ba.shape), fixed_spec(bb.shape)]
        + [hbm] * 4,
        [mine_spec, tok_spec]
        + [transposed_spec(shape, tile)] * 3
        + [rows_spec(tile, f)] * 4
        + [tok_spec] * 2
        + [fixed_spec((lines, width))] * 2,
        [sd((2 * rows, width), BF16), sd((rows, width), BF16)]
        + [sd(shape + (rows,), BF16)] * 3
        + [sd((rows, f), BF16)] * 4
        + [sd((rows, width), F32), sd((rows, width), BF16)]
        + [sd((lines, width), F32)] * 2,
        [pltpu.VMEM((width, f), BF16)] * 2
        + [pltpu.VMEM((f, width), BF16)] * 2
        + [pltpu.VMEM((tile, 2 * f), BF16)]
        + [pltpu.VMEM((tile, width), BF16)] * 2
        + [pltpu.VMEM(shape + (tile,), BF16), pltpu.SemaphoreType.DMA((4,))],
        (16 * rows * width * f, 8 * width * f + 30 * rows * width + 8 * rows * f, 4 * rows * f),
    )(scalars, tok, pa, pb, up, vec, ba, bb, wia, wib, wda, wdb)


class Order:
    def __init__(self, count, bits, groups):
        total = count.bit_length() - 1
        bits = [bit for bit in bits if bit < total]
        bits = bits + [bit for bit in range(total) if bit not in bits]
        self.count = count
        self.groups = []
        rest = list(bits)
        for group in groups:
            self.groups.append(rest[: min(group, len(rest))])
            rest = rest[group:]
        while len(rest) > 2:
            self.groups.append(rest[:1])
            rest = rest[1:]
        if rest:
            self.groups.append(rest)
        self.groups = [group for group in self.groups if group]
        self.bits = bits

    def masks(self):
        return [self.mask_of(self.bits, j) for j in range(self.count)]

    @staticmethod
    def mask_of(bits, j):
        size = len(bits)
        return sum(((j >> (size - 1 - k)) & 1) << bit for k, bit in enumerate(bits))


def order_blocks(width, order):
    if (width // order.count) % 16 == 0:
        return (order.masks(), (order.count, width // order.count))
    return ([0], (1, width))


def transposed_spec(shape, n):
    return pl.BlockSpec(shape + (n,), lambda i, s: (0, 0, i))


def in_order(grad, order):
    rows, cols = grad.shape
    if len(order_blocks(rows, order)[0]) > 1:
        return grad.reshape(order.count, rows // order.count, cols)
    total = len(order.bits)
    index = lax.axis_index("dp")
    view = grad.reshape((2,) * total + (rows // order.count, cols))
    for bit in range(total):
        axis = total - 1 - bit
        view = jnp.where(((index >> bit) & 1) == 1, jnp.flip(view, axis), view)
    axes = [total - 1 - bit for bit in order.bits]
    view = jnp.transpose(view, axes + [total, total + 1])
    return view.reshape(order.count, rows // order.count, cols)


def swap_pair(value):
    return lax.ppermute(value, "tensor", [(0, 1), (1, 0)])


def swap_bits(value, count, mask):
    return lax.ppermute(value, "dp", [(i, i ^ mask) for i in range(count)])


def total_of(terms):
    total = terms[0].astype(F32)
    for term in terms[1:]:
        total = total + term.astype(F32)
    return total


class RowScatter:
    def __init__(self, terms, order):
        self.terms = list(terms)
        self.count = order.count
        self.groups = list(order.groups)
        self.pending = []

    def send(self):
        bits = self.groups.pop(0)
        parts = 1 << len(bits)
        size = self.terms[0].shape[0] // parts
        self.pending = []
        for j in range(1, parts):
            away = total_of([t[j * size : (j + 1) * size] for t in self.terms]).astype(BF16)
            self.pending.append(swap_bits(away, self.count, Order.mask_of(bits, j)))
        self.terms = [t[:size] for t in self.terms]

    def add(self):
        self.terms = self.terms + self.pending
        self.pending = []

    def finish(self):
        self.add()
        while self.groups:
            self.send()
            self.add()
        return total_of([t[0] for t in self.terms])


def sum_all(vec, count):
    total = count.bit_length() - 1
    bit = 0
    while bit < total:
        if total - bit >= 2:
            one, two, both = [swap_bits(vec, count, m << bit) for m in (1, 2, 3)]
            vec = (vec + one) + (two + both)
            bit = bit + 2
        else:
            vec = vec + swap_bits(vec, count, 1 << bit)
            bit = bit + 1
    return vec


def fence(*values):
    return lax.optimization_barrier(values)


def attend_back_kernel(
    groups, last, scalars, g_ref, gt_ref, tokt_ref, q_ref, k_ref, v_ref, p_ref, c_ref, wq_ref, wo_ref,
    sums_ref, *rest,
):
    if last:
        g1_ref, pa_ref, pb_ref, bias_ref, whole_ref, part_ref, lines_ref, *rest = rest
    else:
        part_ref, lines_ref, *rest = rest
    *grad_refs, d_ref, acc_ref = rest
    step = pl.program_id(0)
    rows, cols = q_ref.shape
    scale = 1.0 / math.sqrt(HEAD_DIM)
    g = g_ref[...]
    grad_context = dot(g, wo_ref[...], NT).astype(BF16)
    lane = lax.broadcasted_iota(jnp.int32, (rows, PAIR), 1)
    low = lane < HEAD_DIM
    zero = jnp.zeros((rows, PAIR), BF16)
    for pair in range(cols // PAIR):
        lo = pair * PAIR
        at = pl.ds(lo, PAIR)
        q = q_ref[:, at]
        v = v_ref[:, at]
        k = k_ref[:, at]
        do = grad_context[:, lo : lo + PAIR]
        product = do.astype(F32) * c_ref[:, at].astype(F32)
        q_t = q.T
        do_t = do.T
        grads_q, grads_k, grads_v = [], [], []
        for half in range(2):
            mine = low if half == 0 else lane >= HEAD_DIM
            row_dot = jnp.sum(jnp.where(mine, product, 0.0), axis=1, keepdims=True)
            probs = p_ref[0, pair * 2 + half]
            grad_probs = dot(jnp.where(mine, do, zero), v, NT)
            grad_scores = (probs.astype(F32) * (grad_probs - row_dot)).astype(BF16)
            grads_q.append(dot(grad_scores, k))
            own = slice(half * HEAD_DIM, (half + 1) * HEAD_DIM)
            grads_k.append(dot(q_t[own], grad_scores))
            grads_v.append(dot(do_t[own], probs))
        d_ref[0, :, at] = (jnp.where(low, grads_q[0], grads_q[1]) * scale).astype(BF16)
        d_ref[1, :, at] = jnp.concatenate(grads_k, axis=0).T.astype(BF16)
        d_ref[2, :, at] = jnp.concatenate(grads_v, axis=0).T.astype(BF16)
    part = (
        dot(d_ref[0], wq_ref[0], NT) + dot(d_ref[1], wq_ref[1], NT) + dot(d_ref[2], wq_ref[2], NT)
    )
    if last:
        others = pa_ref[...].astype(F32) + pb_ref[...].astype(F32)
        part_ref[...] = (g1_ref[...] + (others + part)).astype(BF16)
        whole_ref[...] = part_ref[...]
    else:
        part_ref[...] = part.astype(BF16)
    tok_t = tokt_ref[...].reshape(-1, rows)
    g_t = gt_ref[...].reshape(-1, rows)
    new = [dot(tok_t, d_ref[j]) for j in range(3)] + [dot(g_t, c_ref[...])]
    bias = [column_sum(d_ref[j].astype(F32)) for j in (0, 2)]
    lines = sums_ref.shape[0] if lines_ref.shape[0] > 1 else 0
    spots = []
    for j in range(2):
        start = j * (lines_ref.shape[1] // 2)
        if last:
            start = start + bias_ref.shape[1] // 2
        spots.append((slice(lines, lines + 1), slice(start, start + cols)))

    @pl.when(step == 0)
    def _():
        if lines:
            lines_ref[...] = jnp.zeros(lines_ref.shape, F32)
            lines_ref[:lines] = sums_ref[...]
        if last:
            size = bias_ref.shape[1] // 2
            for j in range(2):
                start = j * (lines_ref.shape[1] // 2)
                lines_ref[lines : lines + 1, start : start + size] = bias_ref[:, j * size : (j + 1) * size]
        for j in range(4):
            acc_ref[j] = new[j]
        for spot, line in zip(spots, bias):
            lines_ref[spot] = line

    @pl.when(step > 0)
    def _():
        for j in range(4):
            acc_ref[j] = acc_ref[j] + new[j]
        for spot, line in zip(spots, bias):
            lines_ref[spot] = lines_ref[spot] + line

    @pl.when(step == pl.num_programs(0) - 1)
    def _():
        start = 0
        for group, grad_ref in zip(groups, grad_refs):
            size = group * PAIR
            for j in range(4):
                piece = acc_ref[j][:, start : start + size]
                grad_ref[:, j * size : (j + 1) * size] = piece.astype(BF16)
            start = start + size


def attend_back(scalars, g, g_t, tok_t, q, k, v, p, c, wq, wo, sums, pairs, tail=()):
    rows, width = g.shape
    seqs, _, n, _ = p.shape
    size = len(pairs)
    cols = size * PAIR
    block = pairs[0] // size
    groups = (2, 1) if size == 3 else (size,)
    column = pl.BlockSpec((n, cols), lambda i, s: (i, block))
    once = pl.Buffered(1)
    tok_spec = rows_spec(n, width)
    shape = (16, width) if tail or size == 3 else (1, 2 * cols)
    tail_specs = [tok_spec] * 3 + [fixed_spec(tail[3].shape)] if tail else []
    return call(
        functools.partial(attend_back_kernel, groups, bool(tail)),
        "attend_back",
        (seqs,),
        [tok_spec, transposed_spec(g_t.shape[:2], n), transposed_spec(g_t.shape[:2], n)]
        + [column] * 3
        + [
            pl.BlockSpec((1, 2 * size, n, n), lambda i, s: (i, block, 0, 0)),
            column,
            pl.BlockSpec((3, width, cols), lambda i, s: (0, 0, block), pipeline_mode=once),
            pl.BlockSpec((cols, width), lambda i, s: (block, 0), pipeline_mode=once),
            fixed_spec(sums.shape),
        ]
        + tail_specs,
        [side_spec(n, width, seqs)] * bool(tail)
        + [tok_spec, fixed_spec(shape)]
        + [fixed_spec((width, 4 * group * PAIR)) for group in groups],
        [sd((2 * rows, width), BF16)] * bool(tail)
        + [sd((rows, width), BF16), sd(shape, F32)]
        + [sd((width, 4 * group * PAIR), BF16) for group in groups],
        [pltpu.VMEM((3, n, cols), BF16), pltpu.VMEM((4, width, cols), F32)],
        (
            16 * rows * width * cols + 16 * rows * n * cols,
            2 * (2 * rows * n * size + 8 * rows * cols + 8 * width * cols),
            0,
        ),
    )(scalars, g, g_t, tok_t, q, k, v, p, c, wq, wo, sums, *tail)


def shards(
    dp_count,
    tokens_in,
    segment_ids,
    w_qkv,
    bias_qv,
    w_out,
    bias_out,
    norm1_gain,
    norm1_shift,
    w_in,
    bias_in,
    w_down,
    bias_down,
    norm2_gain,
    norm2_shift,
    grad_output,
):
    seq_count, seq_length = segment_ids.shape
    half_seqs = seq_count // 2
    rows = half_seqs * seq_length
    width = tokens_in.shape[1]
    local_cols = w_qkv.shape[2]
    f = w_in.shape[1]
    side = lax.axis_index("tensor")
    scalars = jnp.stack([side, lax.axis_index("dp")]).astype(jnp.int32)
    x_first = Order(dp_count, (0, 1, 2, 3), (1, 1))
    y_first = Order(dp_count, (1, 0, 2, 3), (1, 1))
    direct = Order(dp_count, (0, 1, 2, 3), (2,))

    others = [swap_pair(w) for w in (w_qkv, bias_qv, w_out, w_in, bias_in, w_down)]
    vec = jnp.stack([bias_out, norm1_gain, norm1_shift, bias_down, norm2_gain, norm2_shift])

    *kept, part, tok_t = attend(scalars, tokens_in, segment_ids, w_qkv, bias_qv, w_out, direct)
    saved, parts = [kept], [part]
    w_qkv_two, bias_qv_two, w_out_two, w_in_two, bias_in_two, w_down_two = [
        (own, other)
        for own, other in zip(
            (w_qkv, bias_qv, w_out, w_in, bias_in, w_down), others
        )
    ]
    *kept, part = attend(
        scalars, tokens_in, segment_ids, w_qkv_two[1], bias_qv_two[1], w_out_two[1], None
    )
    saved.append(kept)
    parts.append(part)
    output, output_mine, g2_t, low_t, g1_t, h_own, h_other, gp_own, gp_other, g1, g1low, sums_own, sums_other = mlp(
        scalars, tokens_in, *parts, grad_output, vec,
        *[b.reshape(1, f) for b in bias_in_two], *w_in_two, *w_down_two, 256, (x_first, y_first, direct),
    )

    def outer(left, right):
        return dot(left.reshape(width, rows), right).astype(BF16)

    down_recv = swap_pair(outer(g2_t, h_other))
    in_recv = swap_pair(outer(low_t, gp_other))
    down_own = outer(g2_t, h_own)
    in_own = outer(low_t, gp_own)
    output_recv = swap_pair(output_mine)
    g1low, down_recv, in_recv, down_own, in_own = fence(g1low, down_recv, in_recv, down_own, in_own)
    down = RowScatter([in_order(m, x_first) for m in (down_own, down_recv)], x_first)
    inner = RowScatter([in_order(m, y_first) for m in (in_own, in_recv)], y_first)

    def back(at, g, sums, pairs, tail=()):
        return attend_back(
            scalars, g, g1_t, tok_t, *saved[at], w_qkv_two[at], w_out_two[at], sums, pairs, tail
        )

    down.send()
    inner.send()
    part_other, lines_other, first_other, second_other = back(1, g1low, sums_other, (0, 1, 2))
    part_other, lines_other, first_other, second_other, down.pending, inner.pending = fence(
        part_other, lines_other, first_other, second_other, down.pending, inner.pending
    )
    first_recv = swap_pair(first_other)
    second_recv = swap_pair(second_other)
    down.add()
    inner.add()
    down.send()
    inner.send()
    g1low, part_other = fence(g1low, part_other)
    part_first, lines_first, grads_first = back(0, g1low, sums_own, (0, 1))
    part_first, lines_first, grads_first, first_recv, second_recv, down.pending, inner.pending = fence(
        part_first, lines_first, grads_first, first_recv, second_recv, down.pending, inner.pending
    )
    first = RowScatter([in_order(m, direct) for m in (grads_first, first_recv)], direct)
    first.send()
    down.add()
    inner.add()
    down.send()
    inner.send()
    g1low, part_first = fence(g1low, part_first)
    grad_input, grad_mine, lines_own, grads_second = back(
        0, g1low, sums_own, (2,), (g1, part_other, part_first, lines_first)
    )
    grad_input, grad_mine, lines_own, grads_second, first.pending = fence(
        grad_input, grad_mine, lines_own, grads_second, first.pending
    )
    second = RowScatter([in_order(m, direct) for m in (grads_second, second_recv)], direct)
    second.send()
    grad_recv = swap_pair(grad_mine)
    both = sum_all(jnp.stack([lines_own, lines_other]), dp_count)
    total = both[0] + swap_pair(both[1])
    at_stats = sums_own.shape[0] - 6
    summed_bias_in = total[:at_stats].reshape(f)
    summed = [total[at_stats + i] for i in range(6)]
    summed_bias_qv = total[at_stats + 6].reshape(2, local_cols)

    summed_first = first.finish()
    summed_second = second.finish()
    summed_w_down = down.finish().T
    summed_w_in = inner.finish()
    cut = 2 * PAIR
    pieces = [
        jnp.concatenate(
            [summed_first[:, j * cut : (j + 1) * cut], summed_second[:, j * PAIR : (j + 1) * PAIR]], axis=1
        )
        for j in range(4)
    ]
    summed_w_qkv = jnp.stack(pieces[:3])
    summed_w_out = pieces[3].T

    def whole(full, other):
        return lax.dynamic_update_slice_in_dim(full, other, (1 - side) * rows, 0)

    return (
        whole(output, output_recv),
        whole(grad_input, grad_recv),
        summed_w_qkv,
        summed_bias_qv,
        summed_w_out,
        summed[0],
        summed[1],
        summed[2],
        summed_w_in,
        summed_bias_in,
        summed_w_down,
        summed[3],
        summed[4],
        summed[5],
    )


def solution(mesh):
    dp_count = mesh.shape["dp"]

    def body(*args):
        return shards(dp_count, *args)

    return jax.shard_map(
        body,
        mesh=mesh,
        in_specs=(
            P("dp", None),
            P("dp", None),
            P(None, None, "tensor"),
            P(None, "tensor"),
            P("tensor", None),
            P(),
            P(),
            P(),
            P(None, "tensor"),
            P("tensor"),
            P("tensor", None),
            P(),
            P(),
            P(),
            P("dp", None),
        ),
        out_specs=(
            P("dp", None),
            P("dp", None),
            P(None, "dp", "tensor"),
            P(None, "tensor"),
            P("tensor", "dp"),
            P(),
            P(),
            P(),
            P("dp", "tensor"),
            P("tensor"),
            P("tensor", "dp"),
            P(),
            P(),
            P(),
        ),
        check_vma=False,
    )
```

```python
import functools
import math

import jax
import jax.numpy as jnp
from jax import lax
from jax.experimental import pallas as pl
from jax.experimental.pallas import tpu as pltpu
from jax.sharding import PartitionSpec as P

HEAD_DIM = 64
PAIR = 2 * HEAD_DIM
LANES = 128


EPSILON = 1e-05
NEGATIVE = -1e30
ROOT_HALF = 0.7071067811865476
ROOT_TWO_PI_INV = 0.3989422804014327
F32 = jnp.float32
BF16 = jnp.bfloat16
NT = (((1,), (1,)), ((), ()))
NN = (((1,), (0,)), ((), ()))
VMEM_LIMIT = 56 * 1024 * 1024
CHUNK = 512
sd = jax.ShapeDtypeStruct


def dot(left, right, dims=NN):
    return lax.dot_general(left, right, dims, preferred_element_type=F32)


def mean_of(value):
    return jnp.sum(value, axis=1, keepdims=True) * (1.0 / value.shape[1])


def norm_forward(summed):
    centered = summed - mean_of(summed)
    inv_std = lax.rsqrt(mean_of(centered * centered) + EPSILON)
    return (centered * inv_std, inv_std)


def norm_backward(upstream, normed, inv_std, gain_vec):
    scaled_grad = upstream * gain_vec
    second_mean = mean_of(scaled_grad * normed)
    return inv_std * (scaled_grad - mean_of(scaled_grad) - normed * second_mean)


def gelu_pair(preact):
    cumulative = 0.5 + 0.5 * lax.erf(preact * ROOT_HALF)
    derivative = cumulative + preact * (jnp.exp(-0.5 * preact * preact) * ROOT_TWO_PI_INV)
    return (preact * cumulative, derivative)


def column_sum(value):
    return jnp.sum(value, axis=0, keepdims=True)


def rows_spec(n, c):
    return pl.BlockSpec((n, c), lambda i, s: (i, 0))


def side_spec(n, c, steps):
    return pl.BlockSpec((n, c), lambda i, s: (s[0] * steps + i, 0))


def fixed_spec(shape):
    return pl.BlockSpec(shape, lambda i, s: (0,) * len(shape), pipeline_mode=pl.Buffered(1))


def call(kernel, name, grid, in_specs, out_specs, out_shape, scratch, cost):
    flops, moved, transcendentals = cost
    return pl.pallas_call(
        kernel,
        grid_spec=pltpu.PrefetchScalarGridSpec(
            num_scalar_prefetch=1,
            grid=grid,
            in_specs=in_specs,
            out_specs=out_specs,
            scratch_shapes=scratch,
        ),
        out_shape=out_shape,
        compiler_params=pltpu.CompilerParams(vmem_limit_bytes=VMEM_LIMIT),
        cost_estimate=pl.CostEstimate(
            flops=flops, bytes_accessed=moved, transcendentals=transcendentals
        ),
        name=name,
    )


def put_transposed(out_ref, value, scratch, me, masks):
    scratch[...] = value.T.reshape(scratch.shape)
    if len(masks) == 1:
        out_ref[...] = scratch[...]
    else:
        for j, mask in enumerate(masks):
            out_ref[j] = scratch[me ^ mask]


def page_columns(page):
    line = lax.broadcasted_iota(jnp.int32, (LANES, page.shape[1]), 0)
    same = jnp.where(line == page, 1.0, 0.0).T
    lane = lax.broadcasted_iota(jnp.int32, same.shape, 1)
    pen = jnp.where((lane < 4) & (same == 0.0), NEGATIVE, 0.0)
    return (pen.astype(BF16), same.astype(BF16))


def attend_kernel(
    masks, scalars, tok_ref, seg_ref, wq_ref, bq_ref, wo_ref, q_ref, k_ref, v_ref, p_ref, c_ref, part_ref, *rest
):
    if masks:
        put_transposed(rest[0], tok_ref[...], rest[1], scalars[1], masks)
    row = scalars[0] * pl.num_programs(0) + pl.program_id(0)
    pen, hot = page_columns(seg_ref[pl.ds(row, 1), :])
    tok = tok_ref[...]
    scale = 1.0 / math.sqrt(HEAD_DIM)
    bias = bq_ref[...].astype(F32)
    q_ref[...] = ((dot(tok, wq_ref[0]) + bias[0:1]).astype(BF16) * scale).astype(BF16)
    k_ref[...] = dot(tok, wq_ref[1]).astype(BF16)
    v_ref[...] = (dot(tok, wq_ref[2]) + bias[1:2]).astype(BF16)
    rows, cols = q_ref.shape
    lane = lax.broadcasted_iota(jnp.int32, (rows, PAIR), 1)
    zero = jnp.zeros((rows, PAIR), BF16)
    for pair in range(cols // PAIR):
        at = pl.ds(pair * PAIR, PAIR)
        q = q_ref[:, at]
        v = v_ref[:, at]
        k_wide = jnp.concatenate([k_ref[:, at], hot], axis=1)
        outs = []
        for half in range(2):
            mine = (lane < HEAD_DIM) if half == 0 else (lane >= HEAD_DIM)
            q_wide = jnp.concatenate([jnp.where(mine, q, zero), pen], axis=1)
            scores = dot(q_wide, k_wide, NT)
            top = jnp.max(scores, axis=1, keepdims=True)
            exp_scores = jnp.exp(scores - top)
            total = jnp.sum(exp_scores, axis=1, keepdims=True)
            probs = (exp_scores * (1.0 / total)).astype(BF16)
            p_ref[0, pair * 2 + half] = probs
            outs.append(dot(probs, v))
        c_ref[:, at] = jnp.where(lane < HEAD_DIM, outs[0], outs[1]).astype(BF16)
    part_ref[...] = dot(c_ref[...], wo_ref[...]).astype(BF16)


def attend(scalars, tok, seg, wq, bq, wo, order):
    width = tok.shape[1]
    seqs = seg.shape[0] // 2
    n = seg.shape[1]
    rows = seqs * n
    cols = wq.shape[2]
    heads = cols // HEAD_DIM
    masks, shape = order_blocks(width, order) if order else ((), ())
    return call(
        functools.partial(attend_kernel, masks),
        "attend",
        (seqs,),
        [
            side_spec(n, width, seqs),
            fixed_spec(seg.shape),
            fixed_spec(wq.shape),
            fixed_spec(bq.shape),
            fixed_spec(wo.shape),
        ],
        [rows_spec(n, cols)] * 3
        + [
            pl.BlockSpec((1, heads, n, n), lambda i, s: (i, 0, 0, 0)),
            rows_spec(n, cols),
            rows_spec(n, width),
        ]
        + [transposed_spec(shape, n)] * bool(masks),
        [sd((rows, cols), BF16)] * 3
        + [sd((seqs, heads, n, n), BF16), sd((rows, cols), BF16), sd((rows, width), BF16)]
        + [sd(shape + (rows,), BF16)] * bool(masks),
        [pltpu.VMEM(shape + (n,), BF16)] * bool(masks),
        (
            8 * rows * width * cols + 12 * rows * n * cols,
            2 * (rows * n * heads + 7 * rows * cols + 4 * width * cols),
            rows * n * heads,
        ),
    )(scalars, tok, seg, wq, bq, wo)


def mlp_kernel(
    masks, scalars, tok_ref, pa_ref, pb_ref, up_ref, vec_ref, ba_ref, bb_ref,
    wia_hbm, wib_hbm, wda_hbm, wdb_hbm,
    out_ref, mine_ref, g2t_ref, lowt_ref, g1t_ref, ha_ref, hb_ref, gpa_ref, gpb_ref, g1_ref, g1low_ref,
    sumsa_ref, sumsb_ref,
    wia, wib, wda, wdb, dv_ref, low_ref, g2low_ref, turn, sem,
):
    step = pl.program_id(0)
    pairs = ((wia_hbm, wia), (wib_hbm, wib), (wda_hbm, wda), (wdb_hbm, wdb))
    copies = [pltpu.make_async_copy(s, d, sem.at[i]) for i, (s, d) in enumerate(pairs)]

    @pl.when(step == 0)
    def _():
        for copy in copies:
            copy.start()

    def arrive(i):
        @pl.when(step == 0)
        def _():
            copies[i].wait()

    vec = vec_ref[...].astype(F32)
    bias_out, gain1, shift1, bias_down, gain2, shift2 = [vec[i : i + 1] for i in range(6)]
    attention = pa_ref[...].astype(F32) + pb_ref[...].astype(F32)
    normed1, inv1 = norm_forward(tok_ref[...].astype(F32) + attention + bias_out)
    normed_one = normed1 * gain1 + shift1
    low_ref[...] = normed_one.astype(BF16)
    f = wia.shape[1]
    for k, (wi, bi) in enumerate(((wia, ba_ref), (wib, bb_ref))):
        arrive(k)
        for c in range(0, f, CHUNK):
            preact = dot(low_ref[...], wi[:, c : c + CHUNK]) + bi[:, c : c + CHUNK].astype(F32)
            hidden, derivative = gelu_pair(preact)
            at = k * f + c
            h_ref = (ha_ref, hb_ref)[k]
            h_ref[:, c : c + CHUNK] = hidden.astype(BF16)
            dv_ref[:, at : at + CHUNK] = derivative.astype(BF16)
    put_transposed(lowt_ref, low_ref[...], turn, scalars[1], masks[1])
    parts = []
    for k, (wd, h_ref) in enumerate(((wda, ha_ref), (wdb, hb_ref))):
        arrive(2 + k)
        parts.append(dot(h_ref[...], wd[...]).astype(BF16).astype(F32))
    normed2, inv2 = norm_forward(normed_one + (parts[0] + parts[1]) + bias_down)
    mine_ref[...] = (normed2 * gain2 + shift2).astype(BF16)
    out_ref[...] = mine_ref[...]
    up = up_ref[...].astype(F32)
    g2 = norm_backward(up, normed2, inv2, gain2)
    g2low_ref[...] = g2.astype(BF16)
    stats = [column_sum(g2), column_sum(up * normed2), column_sum(up)]
    put_transposed(g2t_ref, g2low_ref[...], turn, scalars[1], masks[0])
    sums = []
    for k, (wd, gp_ref) in enumerate(((wda, gpa_ref), (wdb, gpb_ref))):
        for c in range(0, f, CHUNK):
            at = k * f + c
            grad_hidden = dot(g2low_ref[...], wd[c : c + CHUNK, :], NT)
            grad_preact = (grad_hidden * dv_ref[:, at : at + CHUNK].astype(F32)).astype(BF16)
            gp_ref[:, c : c + CHUNK] = grad_preact
            sums.append(column_sum(grad_preact.astype(F32)))
    parts = []
    for wi, gp_ref in ((wia, gpa_ref), (wib, gpb_ref)):
        parts.append(dot(gp_ref[...], wi[...], NT).astype(BF16).astype(F32))
    grad = g2 + (parts[0] + parts[1])
    g1 = norm_backward(grad, normed1, inv1, gain1)
    g1_ref[...] = g1
    g1low_ref[...] = g1.astype(BF16)
    put_transposed(g1t_ref, g1low_ref[...], turn, scalars[1], masks[2])
    stats = [column_sum(g1), column_sum(grad * normed1), column_sum(grad)] + stats
    width = g1.shape[1]
    lines = [
        jnp.concatenate(s, axis=1)
        for s in (sums[: f // CHUNK], sums[f // CHUNK :])
    ]
    for line, sums_ref in zip(lines, (sumsa_ref, sumsb_ref)):
        block = [line[:, c : c + width] for c in range(0, f, width)] + stats
        block = jnp.concatenate(block, axis=0)

        @pl.when(step == 0)
        def _():
            sums_ref[...] = block

        @pl.when(step > 0)
        def _():
            sums_ref[...] = sums_ref[...] + block


def mlp(scalars, tok, pa, pb, up, vec, ba, bb, wia, wib, wda, wdb, tile, orders):
    rows, width = pa.shape
    f = wia.shape[1]
    steps = rows // tile
    hbm = pl.BlockSpec(memory_space=pl.ANY)
    tok_spec = rows_spec(tile, width)
    mine_spec = side_spec(tile, width, steps)
    masks = [order_blocks(width, order)[0] for order in orders]
    shape = order_blocks(width, orders[0])[1]
    lines = f // width + 6
    return call(
        functools.partial(mlp_kernel, masks),
        "mlp",
        (steps,),
        [mine_spec, tok_spec, tok_spec, mine_spec]
        + [fixed_spec(vec.shape), fixed_spec(ba.shape), fixed_spec(bb.shape)]
        + [hbm] * 4,
        [mine_spec, tok_spec]
        + [transposed_spec(shape, tile)] * 3
        + [rows_spec(tile, f)] * 4
        + [tok_spec] * 2
        + [fixed_spec((lines, width))] * 2,
        [sd((2 * rows, width), BF16), sd((rows, width), BF16)]
        + [sd(shape + (rows,), BF16)] * 3
        + [sd((rows, f), BF16)] * 4
        + [sd((rows, width), F32), sd((rows, width), BF16)]
        + [sd((lines, width), F32)] * 2,
        [pltpu.VMEM((width, f), BF16)] * 2
        + [pltpu.VMEM((f, width), BF16)] * 2
        + [pltpu.VMEM((tile, 2 * f), BF16)]
        + [pltpu.VMEM((tile, width), BF16)] * 2
        + [pltpu.VMEM(shape + (tile,), BF16), pltpu.SemaphoreType.DMA((4,))],
        (16 * rows * width * f, 8 * width * f + 30 * rows * width + 8 * rows * f, 4 * rows * f),
    )(scalars, tok, pa, pb, up, vec, ba, bb, wia, wib, wda, wdb)


class Order:
    def __init__(self, count):
        self.count = count
        self.bits = list(range(count.bit_length() - 1))

    def masks(self):
        return [mask_of(self.bits, j) for j in range(self.count)]


def mask_of(bits, j):
    size = len(bits)
    return sum(((j >> (size - 1 - k)) & 1) << bit for k, bit in enumerate(bits))


def order_blocks(width, order):
    if (width // order.count) % 16 == 0:
        return (order.masks(), (order.count, width // order.count))
    return ([0], (1, width))


def transposed_spec(shape, n):
    return pl.BlockSpec(shape + (n,), lambda i, s: (0, 0, i))


def in_order(grad, order):
    rows, cols = grad.shape
    if len(order_blocks(rows, order)[0]) > 1:
        return grad.reshape(order.count, rows // order.count, cols)
    total = len(order.bits)
    index = lax.axis_index("dp")
    view = grad.reshape((2,) * total + (rows // order.count, cols))
    for bit in range(total):
        axis = total - 1 - bit
        view = jnp.where(((index >> bit) & 1) == 1, jnp.flip(view, axis), view)
    axes = [total - 1 - bit for bit in order.bits]
    view = jnp.transpose(view, axes + [total, total + 1])
    return view.reshape(order.count, rows // order.count, cols)


def swap_pair(value):
    return lax.ppermute(value, "tensor", [(0, 1), (1, 0)])


def swap_bits(value, count, mask):
    return lax.ppermute(value, "dp", [(i, i ^ mask) for i in range(count)])


def total_of(terms):
    total = terms[0].astype(F32)
    for term in terms[1:]:
        total = total + term.astype(F32)
    return total


class RowScatter:
    def __init__(self, terms, order, stages):
        self.count = order.count
        self.left = list(order.bits)
        self.terms = [(term, tuple(order.bits)) for term in terms]
        stages = [[bit for bit in stage if bit in self.left] for stage in stages]
        used = [bit for stage in stages for bit in stage]
        stages = stages + [[bit] for bit in self.left if bit not in used]
        self.stages = [stage for stage in stages if stage]
        self.pending = []

    def pick(self, chosen):
        total = 0.0
        for term, bits in self.terms:
            view = term.reshape((2,) * len(bits) + term.shape[1:])
            at = tuple(chosen.get(bit, slice(None) if bit in self.left else 0) for bit in bits)
            total = total + view[at].reshape((-1,) + term.shape[1:]).astype(F32)
        return total

    def sums(self):
        bits = self.stages.pop(0)
        away, masks = [], []
        for j in range(1, 1 << len(bits)):
            masks.append(mask_of(bits, j))
            chosen = {bit: (masks[-1] >> bit) & 1 for bit in bits}
            away.append(self.pick(chosen).astype(BF16))
        self.left = [bit for bit in self.left if bit not in bits]
        return (away, masks)

    def send(self):
        self.away, masks = self.sums()
        self.pending = [swap_bits(away, self.count, mask) for away, mask in zip(self.away, masks)]

    def add(self):
        self.terms = self.terms + [(term, tuple(self.left)) for term in self.pending]
        self.pending = []

    def own(self):
        return self.pick({})[0]


class JointScatter:
    def __init__(self, left, right):
        self.chains = (left, right)
        self.pending = []

    def send(self):
        (left, masks), (right, _) = [chain.sums() for chain in self.chains]
        self.away = [jnp.stack(two) for two in zip(left, right)]
        self.pending = [
            swap_bits(away, self.chains[0].count, mask) for away, mask in zip(self.away, masks)
        ]

    def more(self):
        return bool(self.chains[0].stages)

    def add(self):
        for at, chain in enumerate(self.chains):
            chain.terms = chain.terms + [(m[at], tuple(chain.left)) for m in self.pending]
        self.pending = []


class SumAll:
    def __init__(self, value, count):
        self.value = value
        self.count = count
        self.bit = 1

    def send(self):
        self.pending = swap_bits(self.value, self.count, self.bit)
        self.bit = 2 * self.bit

    def add(self):
        self.value = self.value + self.pending

    def finish(self):
        self.add()
        while self.bit < self.count:
            self.send()
            self.add()
        return self.value


def fence(*values):
    return lax.optimization_barrier(values)


def attend_back_kernel(
    scalars, g_ref, gt_ref, tokt_ref, q_ref, k_ref, v_ref, p_ref, c_ref, wo_ref, sums_ref, *rest,
):
    wq_ref = rest[0] if len(rest) == 7 else None
    first_ref, lines_ref, grada_ref, gradb_ref, acc_ref = rest[1:6] if wq_ref is not None else rest
    d_ref = rest[6] if wq_ref is not None else first_ref
    step = pl.program_id(0)
    rows, cols = q_ref.shape
    scale = 1.0 / math.sqrt(HEAD_DIM)
    grad_context = dot(g_ref[...], wo_ref[...], NT).astype(BF16)
    lane = lax.broadcasted_iota(jnp.int32, (rows, PAIR), 1)
    low = lane < HEAD_DIM
    zero = jnp.zeros((rows, PAIR), BF16)
    for pair in range(cols // PAIR):
        lo = pair * PAIR
        at = pl.ds(lo, PAIR)
        q = q_ref[:, at]
        v = v_ref[:, at]
        k = k_ref[:, at]
        do = grad_context[:, lo : lo + PAIR]
        product = do.astype(F32) * c_ref[:, at].astype(F32)
        q_t = q.T
        do_t = do.T
        grads_q, grads_k, grads_v = [], [], []
        for half in range(2):
            mine = low if half == 0 else lane >= HEAD_DIM
            row_dot = jnp.sum(jnp.where(mine, product, 0.0), axis=1, keepdims=True)
            probs = p_ref[0, pair * 2 + half]
            grad_probs = dot(jnp.where(mine, do, zero), v, NT)
            grad_scores = (probs.astype(F32) * (grad_probs - row_dot)).astype(BF16)
            grads_q.append(dot(grad_scores, k))
            own = slice(half * HEAD_DIM, (half + 1) * HEAD_DIM)
            grads_k.append(dot(q_t[own], grad_scores))
            grads_v.append(dot(do_t[own], probs))
        d_ref[0, :, at] = (jnp.where(low, grads_q[0], grads_q[1]) * scale).astype(BF16)
        d_ref[1, :, at] = jnp.concatenate(grads_k, axis=0).T.astype(BF16)
        d_ref[2, :, at] = jnp.concatenate(grads_v, axis=0).T.astype(BF16)
    if wq_ref is not None:
        first_ref[...] = input_part(d_ref, wq_ref).astype(BF16)
    tok_t = tokt_ref[...].reshape(-1, rows)
    g_t = gt_ref[...].reshape(-1, rows)
    new = [dot(tok_t, d_ref[j]) for j in range(3)] + [dot(g_t, c_ref[...])]
    bias = [column_sum(d_ref[j].astype(F32)) for j in (0, 2)]
    lines = sums_ref.shape[0]
    spots = [(slice(lines, lines + 1), slice(j * cols, (j + 1) * cols)) for j in range(2)]

    @pl.when(step == 0)
    def _():
        lines_ref[...] = jnp.zeros(lines_ref.shape, F32)
        lines_ref[:lines] = sums_ref[...]
        for j in range(4):
            acc_ref[j] = new[j]
        for spot, line in zip(spots, bias):
            lines_ref[spot] = line

    @pl.when(step > 0)
    def _():
        for j in range(4):
            acc_ref[j] = acc_ref[j] + new[j]
        for spot, line in zip(spots, bias):
            lines_ref[spot] = lines_ref[spot] + line

    @pl.when(step == pl.num_programs(0) - 1)
    def _():
        for j, grad_ref in enumerate((grada_ref, grada_ref, gradb_ref, gradb_ref)):
            at = (j % 2) * cols
            grad_ref[:, at : at + cols] = acc_ref[j].astype(BF16)


def attend_back(scalars, g, g_t, tok_t, q, k, v, p, c, wo, sums, wq=None):
    rows, width = g.shape
    seqs, heads, n, _ = p.shape
    cols = q.shape[1]
    turned = transposed_spec(g_t.shape[:2], n)
    extra = () if wq is None else (wq,)
    if wq is None:
        first_spec = pl.BlockSpec((3, n, cols), lambda i, s: (0, i, 0))
        first_shape = (3, rows, cols)
    else:
        first_spec = rows_spec(n, width)
        first_shape = (rows, width)
    return call(
        attend_back_kernel,
        "attend_back",
        (seqs,),
        [rows_spec(n, width), turned, turned]
        + [rows_spec(n, cols)] * 3
        + [
            pl.BlockSpec((1, heads, n, n), lambda i, s: (i, 0, 0, 0)),
            rows_spec(n, cols),
            fixed_spec(wo.shape),
            fixed_spec(sums.shape),
        ]
        + [fixed_spec(w.shape) for w in extra],
        [first_spec, fixed_spec((16, 2 * cols))] + [fixed_spec((width, 2 * cols))] * 2,
        [sd(first_shape, BF16), sd((16, 2 * cols), F32)] + [sd((width, 2 * cols), BF16)] * 2,
        [pltpu.VMEM((4, width, cols), F32)] + [pltpu.VMEM((3, n, cols), BF16)] * len(extra),
        (
            (10 + 6 * len(extra)) * rows * width * cols + 16 * rows * n * cols,
            2 * (rows * n * heads + 8 * rows * cols + 8 * width * cols),
            0,
        ),
    )(scalars, g, g_t, tok_t, q, k, v, p, c, wo, sums, *extra)


def input_part(d_ref, w_ref):
    return dot(d_ref[0], w_ref[0], NT) + dot(d_ref[1], w_ref[1], NT) + dot(d_ref[2], w_ref[2], NT)


def input_grad_kernel(scalars, g1_ref, part_ref, d_ref, w_ref, whole_ref, mine_ref):
    own = input_part(d_ref, w_ref).astype(BF16).astype(F32)
    mine_ref[...] = (g1_ref[...] + (own + part_ref[...].astype(F32))).astype(BF16)
    whole_ref[...] = mine_ref[...]


def input_grad(scalars, g1, part, d, w, tile):
    rows, width = g1.shape
    cols = d.shape[2]
    steps = rows // tile
    tok_spec = rows_spec(tile, width)
    return call(
        input_grad_kernel,
        "input_grad",
        (steps,),
        [tok_spec, tok_spec, pl.BlockSpec((3, tile, cols), lambda i, s: (0, i, 0)), fixed_spec(w.shape)],
        [side_spec(tile, width, steps), tok_spec],
        [sd((2 * rows, width), BF16), sd((rows, width), BF16)],
        [],
        (6 * rows * width * cols, 10 * rows * width + 6 * rows * cols + 6 * width * cols, 0),
    )(scalars, g1, part, d, w)


def shards(
    dp_count,
    tokens_in,
    segment_ids,
    w_qkv,
    bias_qv,
    w_out,
    bias_out,
    norm1_gain,
    norm1_shift,
    w_in,
    bias_in,
    w_down,
    bias_down,
    norm2_gain,
    norm2_shift,
    grad_output,
):
    seq_count, seq_length = segment_ids.shape
    half_seqs = seq_count // 2
    rows = half_seqs * seq_length
    width = tokens_in.shape[1]
    local_cols = w_qkv.shape[2]
    f = w_in.shape[1]
    side = lax.axis_index("tensor")
    scalars = jnp.stack([side, lax.axis_index("dp")]).astype(jnp.int32)
    order = Order(dp_count)

    vec = jnp.stack([bias_out, norm1_gain, norm1_shift, bias_down, norm2_gain, norm2_shift])
    bias_line = bias_in.reshape(1, f)
    others = [swap_pair(w) for w in (w_qkv, w_out, w_in, w_down)]
    *kept, part, tok_t = attend(scalars, tokens_in, segment_ids, w_qkv, bias_qv, w_out, order)
    part, bias_qv, bias_line = fence(part, bias_qv, bias_line)
    bias_others = [swap_pair(w) for w in (bias_qv, bias_line)]
    saved, parts = [kept], [part]
    others = [others[0], bias_others[0], others[1], others[2], bias_others[1], others[3]]
    w_qkv_two, bias_qv_two, w_out_two, w_in_two, bias_in_two, w_down_two = [
        (own, other)
        for own, other in zip(
            (w_qkv, bias_qv, w_out, w_in, bias_line, w_down), others
        )
    ]
    *kept, part = attend(
        scalars, tokens_in, segment_ids, w_qkv_two[1], bias_qv_two[1], w_out_two[1], None
    )
    saved.append(kept)
    parts.append(part)
    output, output_mine, g2_t, low_t, g1_t, h_own, h_other, gp_own, gp_other, g1, g1low, sums_own, sums_other = mlp(
        scalars, tokens_in, *parts, grad_output, vec,
        *bias_in_two, *w_in_two, *w_down_two, 256, (order, order, order),
    )

    def whole(full, other):
        return lax.dynamic_update_slice_in_dim(full, other, (1 - side) * rows, 0)

    def outer(left, right):
        return dot(left.reshape(width, rows), right).astype(BF16)

    down_recv = swap_pair(outer(g2_t, h_other))
    in_recv = swap_pair(outer(low_t, gp_other))
    down_own = outer(g2_t, h_own)
    in_own = outer(low_t, gp_own)
    output_recv = swap_pair(output_mine)
    g1low, down_recv, in_recv, down_own, in_own = fence(g1low, down_recv, in_recv, down_own, in_own)
    down = RowScatter([in_order(m, order) for m in (down_own, down_recv)], order, ((0,), (1,)))
    inner = RowScatter([in_order(m, order) for m in (in_own, in_recv)], order, ((1,), (0,)))

    def back(at, g, *rest):
        return attend_back(scalars, g, g1_t, tok_t, *saved[at], w_out_two[at], *rest)

    down.send()
    inner.send()
    part_other, lines_other, *grads_other = back(1, g1low, sums_other, w_qkv_two[1])
    part_other, lines_other, grads_other, down.pending, inner.pending = fence(
        part_other, lines_other, grads_other, down.pending, inner.pending
    )
    grads_recv = [swap_pair(grad) for grad in grads_other]
    down.add()
    inner.add()
    down.send()
    inner.send()
    g1low, part_other = fence(g1low, part_other)
    d_own, lines_own, *grads_own = back(0, g1low, sums_own)
    d_own, lines_own, grads_own, grads_recv, down.pending, inner.pending = fence(
        d_own, lines_own, grads_own, grads_recv, down.pending, inner.pending
    )
    last = [order.bits[2:4]] if dp_count <= 16 else []
    head_a, head_b = [
        RowScatter([in_order(m, order) for m in terms], order, [[first], [1 - first]] + last)
        for first, terms in enumerate(zip(grads_own, grads_recv))
    ]
    head_a.send()
    head_b.send()
    down.add()
    inner.add()
    joint = JointScatter(down, inner)
    joint.send()
    lines = SumAll(jnp.stack([lines_own, lines_other]), dp_count)
    lines.send()
    grad_input, grad_mine = input_grad(scalars, g1, part_other, d_own, w_qkv, 256)
    grad_input, grad_mine, head_a.pending, head_b.pending, lines.pending, joint.pending = fence(
        grad_input, grad_mine, head_a.pending, head_b.pending, lines.pending, joint.pending
    )
    head_a.add()
    head_b.add()
    head_a.send()
    head_b.send()
    joint.add()
    while joint.more():
        joint.send()
        joint.add()
    grad_input = whole(grad_input, swap_pair(grad_mine))
    summed_w_down = down.own().T
    summed_w_in = inner.own()
    head_a.add()
    head_b.add()
    heads = JointScatter(head_a, head_b)
    while heads.more():
        heads.send()
        heads.add()
    lines = lines.finish()
    total = lines[0] + swap_pair(lines[1])
    at_stats = sums_own.shape[0] - 6
    summed_bias_in = total[:at_stats].reshape(f)
    summed = [total[at_stats + i] for i in range(6)]
    summed_bias_qv = total[at_stats + 6].reshape(2, local_cols)
    summed_a, summed_b = head_a.own(), head_b.own()
    summed_w_qkv = jnp.stack([summed_a[:, :local_cols], summed_a[:, local_cols:], summed_b[:, :local_cols]])
    summed_w_out = summed_b[:, local_cols:].T

    return (
        whole(output, output_recv),
        grad_input,
        summed_w_qkv,
        summed_bias_qv,
        summed_w_out,
        summed[0],
        summed[1],
        summed[2],
        summed_w_in,
        summed_bias_in,
        summed_w_down,
        summed[3],
        summed[4],
        summed[5],
    )


def solution(mesh):
    dp_count = mesh.shape["dp"]

    def body(*args):
        return shards(dp_count, *args)

    return jax.shard_map(
        body,
        mesh=mesh,
        in_specs=(
            P("dp", None),
            P("dp", None),
            P(None, None, "tensor"),
            P(None, "tensor"),
            P("tensor", None),
            P(),
            P(),
            P(),
            P(None, "tensor"),
            P("tensor"),
            P("tensor", None),
            P(),
            P(),
            P(),
            P("dp", None),
        ),
        out_specs=(
            P("dp", None),
            P("dp", None),
            P(None, "dp", "tensor"),
            P(None, "tensor"),
            P("tensor", "dp"),
            P(),
            P(),
            P(),
            P("dp", "tensor"),
            P("tensor"),
            P("tensor", "dp"),
            P(),
            P(),
            P(),
        ),
        check_vma=False,
    )
```

```python
import functools
import math

import jax
import jax.numpy as jnp
from jax import lax
from jax.experimental import pallas as pl
from jax.experimental.pallas import tpu as pltpu
from jax.sharding import PartitionSpec as P

HEAD_DIM = 64
PAIR = 2 * HEAD_DIM
LANES = 128


EPSILON = 1e-05
NEGATIVE = -1e30
ROOT_HALF = 0.7071067811865476
ROOT_TWO_PI_INV = 0.3989422804014327
F32 = jnp.float32
BF16 = jnp.bfloat16
NT = (((1,), (1,)), ((), ()))
NN = (((1,), (0,)), ((), ()))
CHUNK = 512
sd = jax.ShapeDtypeStruct


def dot(left, right, dims=NN):
    return lax.dot_general(left, right, dims, preferred_element_type=F32)


def mean_of(value):
    return jnp.sum(value, axis=1, keepdims=True) * (1.0 / value.shape[1])


def norm_forward(summed):
    centered = summed - mean_of(summed)
    inv_std = lax.rsqrt(mean_of(centered * centered) + EPSILON)
    return (centered * inv_std, inv_std)


def norm_backward(upstream, normed, inv_std, gain_vec):
    scaled_grad = upstream * gain_vec
    second_mean = mean_of(scaled_grad * normed)
    return inv_std * (scaled_grad - mean_of(scaled_grad) - normed * second_mean)


def gelu_pair(preact):
    cumulative = 0.5 + 0.5 * lax.erf(preact * ROOT_HALF)
    derivative = cumulative + preact * (jnp.exp(-0.5 * preact * preact) * ROOT_TWO_PI_INV)
    return (preact * cumulative, derivative)


def column_sum(value):
    return jnp.sum(value, axis=0, keepdims=True)


def rows_spec(n, c):
    return pl.BlockSpec((n, c), lambda i, s: (i, 0))


def side_spec(n, c, steps):
    return pl.BlockSpec((n, c), lambda i, s: (s[0] * steps + i, 0))


def fixed_spec(shape):
    return pl.BlockSpec(shape, lambda i, s: (0,) * len(shape), pipeline_mode=pl.Buffered(1))


def call(kernel, name, grid, in_specs, out_specs, out_shape, scratch, cost, limit=56):
    flops, moved, transcendentals = cost
    return pl.pallas_call(
        kernel,
        grid_spec=pltpu.PrefetchScalarGridSpec(
            num_scalar_prefetch=1,
            grid=grid,
            in_specs=in_specs,
            out_specs=out_specs,
            scratch_shapes=scratch,
        ),
        out_shape=out_shape,
        compiler_params=pltpu.CompilerParams(vmem_limit_bytes=limit * 1024 * 1024),
        cost_estimate=pl.CostEstimate(
            flops=flops, bytes_accessed=moved, transcendentals=transcendentals
        ),
        name=name,
    )


def put_transposed(out_ref, value, scratch, me, masks):
    scratch[...] = value.T.reshape(scratch.shape)
    if len(masks) == 1:
        out_ref[...] = scratch[...]
    else:
        for j, mask in enumerate(masks):
            out_ref[j] = scratch[me ^ mask]


def page_columns(page):
    line = lax.broadcasted_iota(jnp.int32, (LANES, page.shape[1]), 0)
    same = jnp.where(line == page, 1.0, 0.0).T
    lane = lax.broadcasted_iota(jnp.int32, same.shape, 1)
    pen = jnp.where((lane < 4) & (same == 0.0), NEGATIVE, 0.0)
    return (pen.astype(BF16), same.astype(BF16))


def attend_kernel(
    masks, scalars, tok_ref, seg_ref, wq_ref, bq_ref, wo_ref, q_ref, k_ref, v_ref, p_ref, c_ref, part_ref, *rest
):
    if masks:
        put_transposed(rest[0], tok_ref[...], rest[1], scalars[1], masks)
    row = scalars[0] * pl.num_programs(0) + pl.program_id(0)
    pen, hot = page_columns(seg_ref[pl.ds(row, 1), :])
    tok = tok_ref[...]
    scale = 1.0 / math.sqrt(HEAD_DIM)
    bias = bq_ref[...].astype(F32)
    q_ref[...] = ((dot(tok, wq_ref[0]) + bias[0:1]).astype(BF16) * scale).astype(BF16)
    k_ref[...] = dot(tok, wq_ref[1]).astype(BF16)
    v_ref[...] = (dot(tok, wq_ref[2]) + bias[1:2]).astype(BF16)
    rows, cols = q_ref.shape
    lane = lax.broadcasted_iota(jnp.int32, (rows, PAIR), 1)
    zero = jnp.zeros((rows, PAIR), BF16)
    for pair in range(cols // PAIR):
        at = pl.ds(pair * PAIR, PAIR)
        q = q_ref[:, at]
        v = v_ref[:, at]
        k_wide = jnp.concatenate([k_ref[:, at], hot], axis=1)
        outs = []
        for half in range(2):
            mine = (lane < HEAD_DIM) if half == 0 else (lane >= HEAD_DIM)
            q_wide = jnp.concatenate([jnp.where(mine, q, zero), pen], axis=1)
            scores = dot(q_wide, k_wide, NT)
            top = jnp.max(scores, axis=1, keepdims=True)
            exp_scores = jnp.exp(scores - top)
            total = jnp.sum(exp_scores, axis=1, keepdims=True)
            probs = (exp_scores * (1.0 / total)).astype(BF16)
            p_ref[0, pair * 2 + half] = probs
            outs.append(dot(probs, v))
        c_ref[:, at] = jnp.where(lane < HEAD_DIM, outs[0], outs[1]).astype(BF16)
    part_ref[...] = dot(c_ref[...], wo_ref[...]).astype(BF16)


def attend(scalars, tok, seg, wq, bq, wo, order):
    width = tok.shape[1]
    seqs = seg.shape[0] // 2
    n = seg.shape[1]
    rows = seqs * n
    cols = wq.shape[2]
    heads = cols // HEAD_DIM
    masks, shape = order_blocks(width, order) if order else ((), ())
    return call(
        functools.partial(attend_kernel, masks),
        "attend",
        (seqs,),
        [
            side_spec(n, width, seqs),
            fixed_spec(seg.shape),
            fixed_spec(wq.shape),
            fixed_spec(bq.shape),
            fixed_spec(wo.shape),
        ],
        [rows_spec(n, cols)] * 3
        + [
            pl.BlockSpec((1, heads, n, n), lambda i, s: (i, 0, 0, 0)),
            rows_spec(n, cols),
            rows_spec(n, width),
        ]
        + [transposed_spec(shape, n)] * bool(masks),
        [sd((rows, cols), BF16)] * 3
        + [sd((seqs, heads, n, n), BF16), sd((rows, cols), BF16), sd((rows, width), BF16)]
        + [sd(shape + (rows,), BF16)] * bool(masks),
        [pltpu.VMEM(shape + (n,), BF16)] * bool(masks),
        (
            8 * rows * width * cols + 12 * rows * n * cols,
            2 * (rows * n * heads + 7 * rows * cols + 4 * width * cols),
            rows * n * heads,
        ),
    )(scalars, tok, seg, wq, bq, wo)


def mlp_kernel(
    masks, scalars, tok_ref, pa_ref, pb_ref, up_ref, vec_ref, ba_ref, bb_ref,
    wia_hbm, wib_hbm, wda_hbm, wdb_hbm,
    out_ref, mine_ref, g2t_ref, lowt_ref, g1t_ref, ha_ref, hb_ref, gpa_ref, gpb_ref, g1_ref, g1low_ref,
    sumsa_ref, sumsb_ref,
    wia, wib, wda, wdb, dv_ref, low_ref, g2low_ref, turn, sem,
):
    step = pl.program_id(0)
    pairs = ((wia_hbm, wia), (wib_hbm, wib), (wda_hbm, wda), (wdb_hbm, wdb))
    copies = [pltpu.make_async_copy(s, d, sem.at[i]) for i, (s, d) in enumerate(pairs)]

    def tile(first):
        def arrive(i):
            if first:
                copies[i].wait()

        vec = vec_ref[...].astype(F32)
        bias_out, gain1, shift1, bias_down, gain2, shift2 = [vec[i : i + 1] for i in range(6)]
        attention = pa_ref[...].astype(F32) + pb_ref[...].astype(F32)
        normed1, inv1 = norm_forward(tok_ref[...].astype(F32) + attention + bias_out)
        normed_one = normed1 * gain1 + shift1
        low_ref[...] = normed_one.astype(BF16)
        f = wia.shape[1]
        for k, (wi, bi) in enumerate(((wia, ba_ref), (wib, bb_ref))):
            arrive(k)
            for c in range(0, f, CHUNK):
                preact = dot(low_ref[...], wi[:, c : c + CHUNK]) + bi[:, c : c + CHUNK].astype(F32)
                hidden, derivative = gelu_pair(preact)
                at = k * f + c
                h_ref = (ha_ref, hb_ref)[k]
                h_ref[:, c : c + CHUNK] = hidden.astype(BF16)
                dv_ref[:, at : at + CHUNK] = derivative.astype(BF16)
        put_transposed(lowt_ref, low_ref[...], turn, scalars[1], masks[1])
        parts = []
        for k, (wd, h_ref) in enumerate(((wda, ha_ref), (wdb, hb_ref))):
            arrive(2 + k)
            parts.append(dot(h_ref[...], wd[...]).astype(BF16).astype(F32))
        normed2, inv2 = norm_forward(normed_one + (parts[0] + parts[1]) + bias_down)
        mine_ref[...] = (normed2 * gain2 + shift2).astype(BF16)
        out_ref[...] = mine_ref[...]
        up = up_ref[...].astype(F32)
        g2 = norm_backward(up, normed2, inv2, gain2)
        g2low_ref[...] = g2.astype(BF16)
        stats = [column_sum(g2), column_sum(up * normed2), column_sum(up)]
        put_transposed(g2t_ref, g2low_ref[...], turn, scalars[1], masks[0])
        sums = []
        for k, (wd, gp_ref) in enumerate(((wda, gpa_ref), (wdb, gpb_ref))):
            for c in range(0, f, CHUNK):
                at = k * f + c
                grad_hidden = dot(g2low_ref[...], wd[c : c + CHUNK, :], NT)
                grad_preact = (grad_hidden * dv_ref[:, at : at + CHUNK].astype(F32)).astype(BF16)
                gp_ref[:, c : c + CHUNK] = grad_preact
                sums.append(column_sum(grad_preact.astype(F32)))
        parts = []
        for wi, gp_ref in ((wia, gpa_ref), (wib, gpb_ref)):
            parts.append(dot(gp_ref[...], wi[...], NT).astype(BF16).astype(F32))
        grad = g2 + (parts[0] + parts[1])
        g1 = norm_backward(grad, normed1, inv1, gain1)
        g1_ref[...] = g1
        g1low_ref[...] = g1.astype(BF16)
        put_transposed(g1t_ref, g1low_ref[...], turn, scalars[1], masks[2])
        stats = [column_sum(g1), column_sum(grad * normed1), column_sum(grad)] + stats
        width = g1.shape[1]
        lines = [
            jnp.concatenate(s, axis=1)
            for s in (sums[: f // CHUNK], sums[f // CHUNK :])
        ]
        for line, sums_ref in zip(lines, (sumsa_ref, sumsb_ref)):
            block = [line[:, c : c + width] for c in range(0, f, width)] + stats
            block = jnp.concatenate(block, axis=0)
            sums_ref[...] = block if first else sums_ref[...] + block

    @pl.when(step == 0)
    def _():
        for copy in copies:
            copy.start()
        tile(True)

    @pl.when(step > 0)
    def _():
        tile(False)


def mlp(scalars, tok, pa, pb, up, vec, ba, bb, wia, wib, wda, wdb, tile, orders):
    rows, width = pa.shape
    f = wia.shape[1]
    steps = rows // tile
    hbm = pl.BlockSpec(memory_space=pl.ANY)
    tok_spec = rows_spec(tile, width)
    mine_spec = side_spec(tile, width, steps)
    masks = [order_blocks(width, order)[0] for order in orders]
    shape = order_blocks(width, orders[0])[1]
    lines = f // width + 6
    return call(
        functools.partial(mlp_kernel, masks),
        "mlp",
        (steps,),
        [mine_spec, tok_spec, tok_spec, mine_spec]
        + [fixed_spec(vec.shape), fixed_spec(ba.shape), fixed_spec(bb.shape)]
        + [hbm] * 4,
        [mine_spec, tok_spec]
        + [transposed_spec(shape, tile)] * 3
        + [rows_spec(tile, f)] * 4
        + [tok_spec] * 2
        + [fixed_spec((lines, width))] * 2,
        [sd((2 * rows, width), BF16), sd((rows, width), BF16)]
        + [sd(shape + (rows,), BF16)] * 3
        + [sd((rows, f), BF16)] * 4
        + [sd((rows, width), F32), sd((rows, width), BF16)]
        + [sd((lines, width), F32)] * 2,
        [pltpu.VMEM((width, f), BF16)] * 2
        + [pltpu.VMEM((f, width), BF16)] * 2
        + [pltpu.VMEM((tile, 2 * f), BF16)]
        + [pltpu.VMEM((tile, width), BF16)] * 2
        + [pltpu.VMEM(shape + (tile,), BF16), pltpu.SemaphoreType.DMA((4,))],
        (16 * rows * width * f, 8 * width * f + 30 * rows * width + 8 * rows * f, 4 * rows * f),
    )(scalars, tok, pa, pb, up, vec, ba, bb, wia, wib, wda, wdb)


class Order:
    def __init__(self, count):
        self.count = count
        self.bits = list(range(count.bit_length() - 1))

    def masks(self):
        return [mask_of(self.bits, j) for j in range(self.count)]


def mask_of(bits, j):
    size = len(bits)
    return sum(((j >> (size - 1 - k)) & 1) << bit for k, bit in enumerate(bits))


def order_blocks(width, order):
    if (width // order.count) % 16 == 0:
        return (order.masks(), (order.count, width // order.count))
    return ([0], (1, width))


def transposed_spec(shape, n):
    return pl.BlockSpec(shape + (n,), lambda i, s: (0, 0, i))


def in_order(grad, order):
    rows, cols = grad.shape
    if len(order_blocks(rows, order)[0]) > 1:
        return grad.reshape(order.count, rows // order.count, cols)
    total = len(order.bits)
    index = lax.axis_index("dp")
    view = grad.reshape((2,) * total + (rows // order.count, cols))
    for bit in range(total):
        axis = total - 1 - bit
        view = jnp.where(((index >> bit) & 1) == 1, jnp.flip(view, axis), view)
    axes = [total - 1 - bit for bit in order.bits]
    view = jnp.transpose(view, axes + [total, total + 1])
    return view.reshape(order.count, rows // order.count, cols)


def swap_pair(value):
    return lax.ppermute(value, "tensor", [(0, 1), (1, 0)])


def swap_bits(value, count, mask):
    return lax.ppermute(value, "dp", [(i, i ^ mask) for i in range(count)])


def total_of(terms):
    total = terms[0].astype(F32)
    for term in terms[1:]:
        total = total + term.astype(F32)
    return total


class RowScatter:
    def __init__(self, terms, order, stages):
        self.count = order.count
        self.left = list(order.bits)
        self.terms = list(terms)
        self.marks = [tuple(order.bits)] * len(terms)
        stages = [[bit for bit in stage if bit in self.left] for stage in stages]
        used = [bit for stage in stages for bit in stage]
        stages = stages + [[bit] for bit in self.left if bit not in used]
        self.stages = [stage for stage in stages if stage]
        self.pending = []

    def pick(self, chosen):
        total = 0.0
        for term, bits in zip(self.terms, self.marks):
            view = term.reshape((2,) * len(bits) + term.shape[1:])
            at = tuple(chosen.get(bit, slice(None) if bit in self.left else 0) for bit in bits)
            total = total + view[at].reshape((-1,) + term.shape[1:]).astype(F32)
        return total

    def sums(self):
        bits = self.stages.pop(0)
        away, masks = [], []
        for j in range(1, 1 << len(bits)):
            masks.append(mask_of(bits, j))
            chosen = {bit: (masks[-1] >> bit) & 1 for bit in bits}
            away.append(self.pick(chosen).astype(BF16))
        self.left = [bit for bit in self.left if bit not in bits]
        return (away, masks)

    def send(self):
        self.away, masks = self.sums()
        self.pending = [swap_bits(away, self.count, mask) for away, mask in zip(self.away, masks)]

    def take(self, received):
        self.terms = self.terms + list(received)
        self.marks = self.marks + [tuple(self.left)] * len(received)

    def add(self):
        self.take(self.pending)
        self.pending = []

    def own(self):
        return self.pick({})[0]


class JointScatter:
    def __init__(self, left, right):
        self.chains = (left, right)
        self.pending = []

    def send(self):
        (left, masks), (right, _) = [chain.sums() for chain in self.chains]
        self.away = [jnp.stack(two) for two in zip(left, right)]
        self.pending = [
            swap_bits(away, self.chains[0].count, mask) for away, mask in zip(self.away, masks)
        ]

    def more(self):
        return bool(self.chains[0].stages)

    def add(self):
        for at, chain in enumerate(self.chains):
            chain.take([m[at] for m in self.pending])
        self.pending = []


class SumAll:
    def __init__(self, value, count):
        self.value = value
        self.count = count
        self.bit = 1

    def send(self):
        self.pending = swap_bits(self.value, self.count, self.bit)
        self.bit = 2 * self.bit

    def add(self):
        self.value = self.value + self.pending

    def finish(self):
        self.add()
        while self.bit < self.count:
            self.send()
            self.add()
        return self.value


def fence(*values):
    return lax.optimization_barrier(values)


def attend_back_kernel(
    scalars, g_ref, gt_ref, tokt_ref, q_all, k_all, v_all, p_all, c_all, wo_ref, sums_ref, *rest,
):
    wq_ref = rest[0] if len(rest) == 7 else None
    first_ref, lines_ref, grada_ref, gradb_ref, acc_ref = rest[1:6] if wq_ref is not None else rest
    d_ref = rest[6] if wq_ref is not None else first_ref
    step = pl.program_id(0)
    q_ref, k_ref, v_ref, p_ref, c_ref = [ref.at[step] for ref in (q_all, k_all, v_all, p_all, c_all)]
    rows, cols = q_ref.shape
    scale = 1.0 / math.sqrt(HEAD_DIM)
    grad_context = dot(g_ref[...], wo_ref[...], NT).astype(BF16)
    lane = lax.broadcasted_iota(jnp.int32, (rows, PAIR), 1)
    low = lane < HEAD_DIM
    zero = jnp.zeros((rows, PAIR), BF16)
    for pair in range(cols // PAIR):
        lo = pair * PAIR
        at = pl.ds(lo, PAIR)
        q = q_ref[:, at]
        v = v_ref[:, at]
        k = k_ref[:, at]
        do = grad_context[:, lo : lo + PAIR]
        product = do.astype(F32) * c_ref[:, at].astype(F32)
        q_t = q.T
        do_t = do.T
        grads_q, grads_k, grads_v = [], [], []
        for half in range(2):
            mine = low if half == 0 else lane >= HEAD_DIM
            row_dot = jnp.sum(jnp.where(mine, product, 0.0), axis=1, keepdims=True)
            probs = p_ref[pair * 2 + half]
            grad_probs = dot(jnp.where(mine, do, zero), v, NT)
            grad_scores = (probs.astype(F32) * (grad_probs - row_dot)).astype(BF16)
            grads_q.append(dot(grad_scores, k))
            own = slice(half * HEAD_DIM, (half + 1) * HEAD_DIM)
            grads_k.append(dot(q_t[own], grad_scores))
            grads_v.append(dot(do_t[own], probs))
        d_ref[0, :, at] = (jnp.where(low, grads_q[0], grads_q[1]) * scale).astype(BF16)
        d_ref[1, :, at] = jnp.concatenate(grads_k, axis=0).T.astype(BF16)
        d_ref[2, :, at] = jnp.concatenate(grads_v, axis=0).T.astype(BF16)
    if wq_ref is not None:
        first_ref[...] = input_part(d_ref, wq_ref).astype(BF16)
    tok_t = tokt_ref[...].reshape(-1, rows)
    g_t = gt_ref[...].reshape(-1, rows)
    new = [dot(tok_t, d_ref[j]) for j in range(3)] + [dot(g_t, c_ref[...])]
    bias = [column_sum(d_ref[j].astype(F32)) for j in (0, 2)]
    lines = sums_ref.shape[0]
    spots = [(slice(lines, lines + 1), slice(j * cols, (j + 1) * cols)) for j in range(2)]

    @pl.when(step == 0)
    def _():
        lines_ref[...] = jnp.zeros(lines_ref.shape, F32)
        lines_ref[:lines] = sums_ref[...]
        for j in range(4):
            acc_ref[j] = new[j]
        for spot, line in zip(spots, bias):
            lines_ref[spot] = line

    @pl.when(step > 0)
    def _():
        for j in range(4):
            acc_ref[j] = acc_ref[j] + new[j]
        for spot, line in zip(spots, bias):
            lines_ref[spot] = lines_ref[spot] + line

    @pl.when(step == pl.num_programs(0) - 1)
    def _():
        for j, grad_ref in enumerate((grada_ref, grada_ref, gradb_ref, gradb_ref)):
            at = (j % 2) * cols
            grad_ref[:, at : at + cols] = acc_ref[j].astype(BF16)


def attend_back(scalars, g, g_t, tok_t, q, k, v, p, c, wo, sums, wq=None):
    rows, width = g.shape
    seqs, heads, n, _ = p.shape
    cols = q.shape[1]
    q, k, v, c = [m.reshape(seqs, n, cols) for m in (q, k, v, c)]
    turned = transposed_spec(g_t.shape[:2], n)
    extra = () if wq is None else (wq,)
    if wq is None:
        first_spec = pl.BlockSpec((3, n, cols), lambda i, s: (0, i, 0))
        first_shape = (3, rows, cols)
    else:
        first_spec = rows_spec(n, width)
        first_shape = (rows, width)
    return call(
        attend_back_kernel,
        "attend_back",
        (seqs,),
        [rows_spec(n, width), turned, turned]
        + [pl.BlockSpec(memory_space=pltpu.VMEM)] * 5
        + [
            fixed_spec(wo.shape),
            fixed_spec(sums.shape),
        ]
        + [fixed_spec(w.shape) for w in extra],
        [first_spec, fixed_spec((16, 2 * cols))] + [fixed_spec((width, 2 * cols))] * 2,
        [sd(first_shape, BF16), sd((16, 2 * cols), F32)] + [sd((width, 2 * cols), BF16)] * 2,
        [pltpu.VMEM((4, width, cols), F32)] + [pltpu.VMEM((3, n, cols), BF16)] * len(extra),
        (
            (10 + 6 * len(extra)) * rows * width * cols + 16 * rows * n * cols,
            2 * (rows * n * heads + 8 * rows * cols + 8 * width * cols),
            0,
        ),
        32,
    )(scalars, g, g_t, tok_t, q, k, v, p, c, wo, sums, *extra)


def input_part(d_ref, w_ref):
    return dot(d_ref[0], w_ref[0], NT) + dot(d_ref[1], w_ref[1], NT) + dot(d_ref[2], w_ref[2], NT)


def input_grad_kernel(scalars, g1_ref, part_ref, d_ref, w_ref, whole_ref, mine_ref):
    own = input_part(d_ref, w_ref).astype(BF16).astype(F32)
    mine_ref[...] = (g1_ref[...] + (own + part_ref[...].astype(F32))).astype(BF16)
    whole_ref[...] = mine_ref[...]


def input_grad(scalars, g1, part, d, w, tile):
    rows, width = g1.shape
    cols = d.shape[2]
    steps = rows // tile
    tok_spec = rows_spec(tile, width)
    return call(
        input_grad_kernel,
        "input_grad",
        (steps,),
        [tok_spec, tok_spec, pl.BlockSpec((3, tile, cols), lambda i, s: (0, i, 0)), fixed_spec(w.shape)],
        [side_spec(tile, width, steps), tok_spec],
        [sd((2 * rows, width), BF16), sd((rows, width), BF16)],
        [],
        (6 * rows * width * cols, 10 * rows * width + 6 * rows * cols + 6 * width * cols, 0),
        32,
    )(scalars, g1, part, d, w)


def shards(
    dp_count,
    tokens_in,
    segment_ids,
    w_qkv,
    bias_qv,
    w_out,
    bias_out,
    norm1_gain,
    norm1_shift,
    w_in,
    bias_in,
    w_down,
    bias_down,
    norm2_gain,
    norm2_shift,
    grad_output,
):
    seq_count, seq_length = segment_ids.shape
    half_seqs = seq_count // 2
    rows = half_seqs * seq_length
    width = tokens_in.shape[1]
    local_cols = w_qkv.shape[2]
    f = w_in.shape[1]
    side = lax.axis_index("tensor")
    scalars = jnp.stack([side, lax.axis_index("dp")]).astype(jnp.int32)
    order = Order(dp_count)

    vec = jnp.stack([bias_out, norm1_gain, norm1_shift, bias_down, norm2_gain, norm2_shift])
    bias_line = bias_in.reshape(1, f)
    others = [swap_pair(w) for w in (w_qkv, w_out, w_in, w_down)]
    *kept, part, tok_t = attend(scalars, tokens_in, segment_ids, w_qkv, bias_qv, w_out, order)
    part, bias_qv, bias_line = fence(part, bias_qv, bias_line)
    bias_others = [swap_pair(w) for w in (bias_qv, bias_line)]
    saved, parts = [kept], [part]
    others = [others[0], bias_others[0], others[1], others[2], bias_others[1], others[3]]
    w_qkv_two, bias_qv_two, w_out_two, w_in_two, bias_in_two, w_down_two = [
        (own, other)
        for own, other in zip(
            (w_qkv, bias_qv, w_out, w_in, bias_line, w_down), others
        )
    ]
    *kept, part = attend(
        scalars, tokens_in, segment_ids, w_qkv_two[1], bias_qv_two[1], w_out_two[1], None
    )
    saved.append(kept)
    parts.append(part)
    output, output_mine, g2_t, low_t, g1_t, h_own, h_other, gp_own, gp_other, g1, g1low, sums_own, sums_other = mlp(
        scalars, tokens_in, *parts, grad_output, vec,
        *bias_in_two, *w_in_two, *w_down_two, 256, (order, order, order),
    )

    def whole(full, other):
        return lax.dynamic_update_slice_in_dim(full, other, (1 - side) * rows, 0)

    def outer(left, right):
        return dot(left.reshape(width, rows), right).astype(BF16)

    down_recv = swap_pair(outer(g2_t, h_other))
    in_recv = swap_pair(outer(low_t, gp_other))
    down_own = outer(g2_t, h_own)
    in_own = outer(low_t, gp_own)
    output_recv = swap_pair(output_mine)
    g1low, down_recv, in_recv, down_own, in_own = fence(g1low, down_recv, in_recv, down_own, in_own)
    down = RowScatter([in_order(m, order) for m in (down_own, down_recv)], order, ((0,), (1,)))
    inner = RowScatter([in_order(m, order) for m in (in_own, in_recv)], order, ((1,), (0,)))

    def back(at, g, *rest):
        return attend_back(scalars, g, g1_t, tok_t, *saved[at], w_out_two[at], *rest)

    down.send()
    inner.send()
    part_other, lines_other, *grads_other = back(1, g1low, sums_other, w_qkv_two[1])
    part_other, lines_other, grads_other, down.pending, inner.pending = fence(
        part_other, lines_other, grads_other, down.pending, inner.pending
    )
    grads_recv = [swap_pair(grad) for grad in grads_other]
    lines_recv = swap_pair(lines_other)
    down.add()
    inner.add()
    down.send()
    inner.send()
    g1low, part_other = fence(g1low, part_other)
    d_own, lines_own, *grads_own = back(0, g1low, sums_own)
    d_own, lines_own, grads_own, grads_recv, lines_recv, down.pending, inner.pending = fence(
        d_own, lines_own, grads_own, grads_recv, lines_recv, down.pending, inner.pending
    )
    last = [order.bits[2:4]] if dp_count <= 16 else []
    head_a, head_b = [
        RowScatter([in_order(m, order) for m in terms], order, [[first], [1 - first]] + last)
        for first, terms in enumerate(zip(grads_own, grads_recv))
    ]
    lines = SumAll(lines_own + lines_recv, dp_count)
    lines.send()
    head_a.send()
    head_b.send()
    down.add()
    inner.add()
    head_a.away, head_b.away, down.terms, inner.terms = fence(
        head_a.away, head_b.away, down.terms, inner.terms
    )
    joint = JointScatter(down, inner)
    joint.send()
    grad_input, grad_mine = input_grad(scalars, g1, part_other, d_own, w_qkv, 256)
    grad_input, grad_mine, head_a.pending, head_b.pending, lines.pending, joint.pending, output_recv = fence(
        grad_input, grad_mine, head_a.pending, head_b.pending, lines.pending, joint.pending, output_recv
    )
    lines.add()
    lines.send()
    head_a.add()
    head_b.add()
    head_a.send()
    head_b.send()
    joint.add()
    head_a.away, head_b.away, down.terms, inner.terms, output_recv, grad_mine = fence(
        head_a.away, head_b.away, down.terms, inner.terms, output_recv, grad_mine
    )
    joint.send()
    grad_recv = swap_pair(grad_mine)
    output = whole(output, output_recv)
    output, head_a.pending, head_b.pending, lines.pending, grad_recv = fence(
        output, head_a.pending, head_b.pending, lines.pending, grad_recv
    )
    head_a.add()
    head_b.add()
    heads = JointScatter(head_a, head_b)
    heads.send()
    heads.away, joint.pending, grad_recv = fence(heads.away, joint.pending, grad_recv)
    lines.add()
    lines.send()
    lines.add()
    lines.send()
    joint.add()
    while joint.more():
        joint.send()
        joint.add()
    grad_input = whole(grad_input, grad_recv)
    summed_w_down = down.own().T
    summed_w_in = inner.own()
    grad_input, summed_w_down, summed_w_in, heads.pending, lines.pending = fence(
        grad_input, summed_w_down, summed_w_in, heads.pending, lines.pending
    )
    heads.add()
    while heads.more():
        heads.send()
        heads.add()
    total = lines.finish()
    at_stats = sums_own.shape[0] - 6
    summed_bias_in = total[:at_stats].reshape(f)
    summed = [total[at_stats + i] for i in range(6)]
    summed_bias_qv = total[at_stats + 6].reshape(2, local_cols)
    summed_a, summed_b = head_a.own(), head_b.own()
    summed_w_qkv = jnp.stack([summed_a[:, :local_cols], summed_a[:, local_cols:], summed_b[:, :local_cols]])
    summed_w_out = summed_b[:, local_cols:].T

    return (
        output,
        grad_input,
        summed_w_qkv,
        summed_bias_qv,
        summed_w_out,
        summed[0],
        summed[1],
        summed[2],
        summed_w_in,
        summed_bias_in,
        summed_w_down,
        summed[3],
        summed[4],
        summed[5],
    )


def solution(mesh):
    dp_count = mesh.shape["dp"]

    def body(*args):
        return shards(dp_count, *args)

    return jax.shard_map(
        body,
        mesh=mesh,
        in_specs=(
            P("dp", None),
            P("dp", None),
            P(None, None, "tensor"),
            P(None, "tensor"),
            P("tensor", None),
            P(),
            P(),
            P(),
            P(None, "tensor"),
            P("tensor"),
            P("tensor", None),
            P(),
            P(),
            P(),
            P("dp", None),
        ),
        out_specs=(
            P("dp", None),
            P("dp", None),
            P(None, "dp", "tensor"),
            P(None, "tensor"),
            P("tensor", "dp"),
            P(),
            P(),
            P(),
            P("dp", "tensor"),
            P("tensor"),
            P("tensor", "dp"),
            P(),
            P(),
            P(),
        ),
        check_vma=False,
    )
```

```python
import functools
import math

import jax
import jax.numpy as jnp
from jax import lax
from jax.experimental import pallas as pl
from jax.experimental.pallas import tpu as pltpu
from jax.sharding import PartitionSpec as P

HEAD_DIM = 64
PAIR = 2 * HEAD_DIM
LANES = 128


EPSILON = 1e-05
NEGATIVE = -1e30
ROOT_HALF = 0.7071067811865476
ROOT_TWO_PI_INV = 0.3989422804014327
F32 = jnp.float32
BF16 = jnp.bfloat16
NT = (((1,), (1,)), ((), ()))
NN = (((1,), (0,)), ((), ()))
CHUNK = 512
sd = jax.ShapeDtypeStruct


def dot(left, right, dims=NN):
    return lax.dot_general(left, right, dims, preferred_element_type=F32)


def mean_of(value):
    return jnp.sum(value, axis=1, keepdims=True) * (1.0 / value.shape[1])


def norm_forward(summed):
    centered = summed - mean_of(summed)
    inv_std = lax.rsqrt(mean_of(centered * centered) + EPSILON)
    return (centered * inv_std, inv_std)


def norm_backward(upstream, normed, inv_std, gain_vec):
    scaled_grad = upstream * gain_vec
    second_mean = mean_of(scaled_grad * normed)
    return inv_std * (scaled_grad - mean_of(scaled_grad) - normed * second_mean)


def gelu_pair(preact):
    cumulative = 0.5 + 0.5 * lax.erf(preact * ROOT_HALF)
    derivative = cumulative + preact * (jnp.exp(-0.5 * preact * preact) * ROOT_TWO_PI_INV)
    return (preact * cumulative, derivative)


def column_sum(value):
    return jnp.sum(value, axis=0, keepdims=True)


def rows_spec(n, c):
    return pl.BlockSpec((n, c), lambda i, s: (i, 0))


def side_spec(n, c, steps):
    return pl.BlockSpec((n, c), lambda i, s: (s[0] * steps + i, 0))


def fixed_spec(shape):
    return pl.BlockSpec(shape, lambda i, s: (0,) * len(shape), pipeline_mode=pl.Buffered(1))


def call(kernel, name, grid, in_specs, out_specs, out_shape, scratch, cost, limit=56):
    flops, moved, transcendentals = cost
    return pl.pallas_call(
        kernel,
        grid_spec=pltpu.PrefetchScalarGridSpec(
            num_scalar_prefetch=1,
            grid=grid,
            in_specs=in_specs,
            out_specs=out_specs,
            scratch_shapes=scratch,
        ),
        out_shape=out_shape,
        compiler_params=pltpu.CompilerParams(vmem_limit_bytes=limit * 1024 * 1024),
        cost_estimate=pl.CostEstimate(
            flops=flops, bytes_accessed=moved, transcendentals=transcendentals
        ),
        name=name,
    )


def put_transposed(out_ref, value, scratch, me, masks):
    scratch[...] = value.T.reshape(scratch.shape)
    if len(masks) == 1:
        out_ref[...] = scratch[...]
    else:
        for j, mask in enumerate(masks):
            out_ref[j] = scratch[me ^ mask]


def page_columns(page):
    line = lax.broadcasted_iota(jnp.int32, (LANES, page.shape[1]), 0)
    same = jnp.where(line == page, 1.0, 0.0).T
    lane = lax.broadcasted_iota(jnp.int32, same.shape, 1)
    pen = jnp.where((lane < 4) & (same == 0.0), NEGATIVE, 0.0)
    return (pen.astype(BF16), same.astype(BF16))


def attend_kernel(
    masks, scalars, tok_ref, seg_ref, wq_ref, bq_ref, wo_ref, q_ref, k_ref, v_ref, p_ref, c_ref, part_ref, *rest
):
    if masks:
        put_transposed(rest[0], tok_ref[...], rest[1], scalars[1], masks)
    row = scalars[0] * pl.num_programs(0) + pl.program_id(0)
    pen, hot = page_columns(seg_ref[pl.ds(row, 1), :])
    tok = tok_ref[...]
    scale = 1.0 / math.sqrt(HEAD_DIM)
    bias = bq_ref[...].astype(F32)
    q_ref[...] = ((dot(tok, wq_ref[0]) + bias[0:1]).astype(BF16) * scale).astype(BF16)
    k_ref[...] = dot(tok, wq_ref[1]).astype(BF16)
    v_ref[...] = (dot(tok, wq_ref[2]) + bias[1:2]).astype(BF16)
    rows, cols = q_ref.shape
    lane = lax.broadcasted_iota(jnp.int32, (rows, PAIR), 1)
    zero = jnp.zeros((rows, PAIR), BF16)
    for pair in range(cols // PAIR):
        at = pl.ds(pair * PAIR, PAIR)
        q = q_ref[:, at]
        v = v_ref[:, at]
        k_wide = jnp.concatenate([k_ref[:, at], hot], axis=1)
        outs = []
        for half in range(2):
            mine = (lane < HEAD_DIM) if half == 0 else (lane >= HEAD_DIM)
            q_wide = jnp.concatenate([jnp.where(mine, q, zero), pen], axis=1)
            scores = dot(q_wide, k_wide, NT)
            top = jnp.max(scores, axis=1, keepdims=True)
            exp_scores = jnp.exp(scores - top)
            total = jnp.sum(exp_scores, axis=1, keepdims=True)
            probs = (exp_scores * (1.0 / total)).astype(BF16)
            p_ref[0, pair * 2 + half] = probs
            outs.append(dot(probs, v))
        c_ref[:, at] = jnp.where(lane < HEAD_DIM, outs[0], outs[1]).astype(BF16)
    part_ref[...] = dot(c_ref[...], wo_ref[...]).astype(BF16)


def attend(scalars, tok, seg, wq, bq, wo, order):
    width = tok.shape[1]
    seqs = seg.shape[0] // 2
    n = seg.shape[1]
    rows = seqs * n
    cols = wq.shape[2]
    heads = cols // HEAD_DIM
    masks, shape = order_blocks(width, order) if order else ((), ())
    return call(
        functools.partial(attend_kernel, masks),
        "attend",
        (seqs,),
        [
            side_spec(n, width, seqs),
            fixed_spec(seg.shape),
            fixed_spec(wq.shape),
            fixed_spec(bq.shape),
            fixed_spec(wo.shape),
        ],
        [rows_spec(n, cols)] * 3
        + [
            pl.BlockSpec((1, heads, n, n), lambda i, s: (i, 0, 0, 0)),
            rows_spec(n, cols),
            rows_spec(n, width),
        ]
        + [transposed_spec(shape, n)] * bool(masks),
        [sd((rows, cols), BF16)] * 3
        + [sd((seqs, heads, n, n), BF16), sd((rows, cols), BF16), sd((rows, width), BF16)]
        + [sd(shape + (rows,), BF16)] * bool(masks),
        [pltpu.VMEM(shape + (n,), BF16)] * bool(masks),
        (
            8 * rows * width * cols + 12 * rows * n * cols,
            2 * (rows * n * heads + 7 * rows * cols + 4 * width * cols),
            rows * n * heads,
        ),
    )(scalars, tok, seg, wq, bq, wo)


def part_of(main, rest, start):
    most = main.shape[1]
    return (main, start) if start < most else (rest, start - most)


def mlp_kernel(
    masks, scalars, tok_ref, pa_ref, pb_ref, up_ref, vec_ref, ba_ref, bb_ref,
    wia_hbm, wib_hbm, wda_hbm, wdb_hbm,
    out_ref, mine_ref, g2t_ref, lowt_ref, g1t_ref, ha_ref, hb_ref, gpa_ref, gpb_ref,
    ha_rest, hb_rest, gpa_rest, gpb_rest, g1_ref, g1low_ref,
    sumsa_ref, sumsb_ref,
    wia, wib, wda, wdb, dv_ref, low_ref, g2low_ref, turn, sem,
):
    step = pl.program_id(0)
    pairs = ((wia_hbm, wia), (wib_hbm, wib), (wda_hbm, wda), (wdb_hbm, wdb))
    copies = [pltpu.make_async_copy(s, d, sem.at[i]) for i, (s, d) in enumerate(pairs)]

    def tile(first):
        def arrive(i):
            if first:
                copies[i].wait()

        vec = vec_ref[...].astype(F32)
        bias_out, gain1, shift1, bias_down, gain2, shift2 = [vec[i : i + 1] for i in range(6)]
        attention = pa_ref[...].astype(F32) + pb_ref[...].astype(F32)
        normed1, inv1 = norm_forward(tok_ref[...].astype(F32) + attention + bias_out)
        normed_one = normed1 * gain1 + shift1
        low_ref[...] = normed_one.astype(BF16)
        f = wia.shape[1]
        for k, (wi, bi) in enumerate(((wia, ba_ref), (wib, bb_ref))):
            arrive(k)
            for c in range(0, f, CHUNK):
                preact = dot(low_ref[...], wi[:, c : c + CHUNK]) + bi[:, c : c + CHUNK].astype(F32)
                hidden, derivative = gelu_pair(preact)
                at = k * f + c
                h_ref, spot = part_of((ha_ref, hb_ref)[k], (ha_rest, hb_rest)[k], c)
                h_ref[:, spot : spot + CHUNK] = hidden.astype(BF16)
                dv_ref[:, at : at + CHUNK] = derivative.astype(BF16)
        put_transposed(lowt_ref, low_ref[...], turn, scalars[1], masks[1])
        parts = []
        for k, (wd, h_ref, h_rest) in enumerate(((wda, ha_ref, ha_rest), (wdb, hb_ref, hb_rest))):
            arrive(2 + k)
            most = h_ref.shape[1]
            part = dot(jnp.concatenate([h_ref[...], h_rest[...]], axis=1), wd[...])
            parts.append(part.astype(BF16).astype(F32))
        normed2, inv2 = norm_forward(normed_one + (parts[0] + parts[1]) + bias_down)
        mine_ref[...] = (normed2 * gain2 + shift2).astype(BF16)
        out_ref[...] = mine_ref[...]
        up = up_ref[...].astype(F32)
        g2 = norm_backward(up, normed2, inv2, gain2)
        g2low_ref[...] = g2.astype(BF16)
        stats = [column_sum(g2), column_sum(up * normed2), column_sum(up)]
        put_transposed(g2t_ref, g2low_ref[...], turn, scalars[1], masks[0])
        sums = []
        for k, wd in enumerate((wda, wdb)):
            for c in range(0, f, CHUNK):
                at = k * f + c
                grad_hidden = dot(g2low_ref[...], wd[c : c + CHUNK, :], NT)
                grad_preact = (grad_hidden * dv_ref[:, at : at + CHUNK].astype(F32)).astype(BF16)
                gp_ref, spot = part_of((gpa_ref, gpb_ref)[k], (gpa_rest, gpb_rest)[k], c)
                gp_ref[:, spot : spot + CHUNK] = grad_preact
                sums.append(column_sum(grad_preact.astype(F32)))
        parts = []
        for wi, gp_ref, gp_rest in ((wia, gpa_ref, gpa_rest), (wib, gpb_ref, gpb_rest)):
            most = gp_ref.shape[1]
            part = dot(jnp.concatenate([gp_ref[...], gp_rest[...]], axis=1), wi[...], NT)
            parts.append(part.astype(BF16).astype(F32))
        grad = g2 + (parts[0] + parts[1])
        g1 = norm_backward(grad, normed1, inv1, gain1)
        g1_ref[...] = g1
        g1low_ref[...] = g1.astype(BF16)
        put_transposed(g1t_ref, g1low_ref[...], turn, scalars[1], masks[2])
        stats = [column_sum(g1), column_sum(grad * normed1), column_sum(grad)] + stats
        width = g1.shape[1]
        lines = [
            jnp.concatenate(s, axis=1)
            for s in (sums[: f // CHUNK], sums[f // CHUNK :])
        ]
        for line, sums_ref in zip(lines, (sumsa_ref, sumsb_ref)):
            block = [line[:, c : c + width] for c in range(0, f, width)] + stats
            block = jnp.concatenate(block, axis=0)
            sums_ref[...] = block if first else sums_ref[...] + block

    @pl.when(step == 0)
    def _():
        for copy in copies:
            copy.start()
        tile(True)

    @pl.when(step > 0)
    def _():
        tile(False)


def mlp(scalars, tok, pa, pb, up, vec, ba, bb, wia, wib, wda, wdb, tile, orders):
    rows, width = pa.shape
    f = wia.shape[1]
    steps = rows // tile
    hbm = pl.BlockSpec(memory_space=pl.ANY)
    tok_spec = rows_spec(tile, width)
    mine_spec = side_spec(tile, width, steps)
    masks = [order_blocks(width, order)[0] for order in orders]
    shape = order_blocks(width, orders[0])[1]
    lines = f // width + 6
    most = f // CHUNK * 2 // 3 * CHUNK
    return call(
        functools.partial(mlp_kernel, masks),
        "mlp",
        (steps,),
        [mine_spec, tok_spec, tok_spec, mine_spec]
        + [fixed_spec(vec.shape), fixed_spec(ba.shape), fixed_spec(bb.shape)]
        + [hbm] * 4,
        [mine_spec, tok_spec]
        + [transposed_spec(shape, tile)] * 3
        + [rows_spec(tile, most)] * 4
        + [rows_spec(tile, f - most)] * 4
        + [tok_spec] * 2
        + [fixed_spec((lines, width))] * 2,
        [sd((2 * rows, width), BF16), sd((rows, width), BF16)]
        + [sd(shape + (rows,), BF16)] * 3
        + [sd((rows, most), BF16)] * 4
        + [sd((rows, f - most), BF16)] * 4
        + [sd((rows, width), F32), sd((rows, width), BF16)]
        + [sd((lines, width), F32)] * 2,
        [pltpu.VMEM((width, f), BF16)] * 2
        + [pltpu.VMEM((f, width), BF16)] * 2
        + [pltpu.VMEM((tile, 2 * f), BF16)]
        + [pltpu.VMEM((tile, width), BF16)] * 2
        + [pltpu.VMEM(shape + (tile,), BF16), pltpu.SemaphoreType.DMA((4,))],
        (16 * rows * width * f, 8 * width * f + 30 * rows * width + 8 * rows * f, 4 * rows * f),
    )(scalars, tok, pa, pb, up, vec, ba, bb, wia, wib, wda, wdb)


class Order:
    def __init__(self, count):
        self.count = count
        self.bits = list(range(count.bit_length() - 1))

    def masks(self):
        return [mask_of(self.bits, j) for j in range(self.count)]


def mask_of(bits, j):
    size = len(bits)
    return sum(((j >> (size - 1 - k)) & 1) << bit for k, bit in enumerate(bits))


def order_blocks(width, order):
    if (width // order.count) % 16 == 0:
        return (order.masks(), (order.count, width // order.count))
    return ([0], (1, width))


def transposed_spec(shape, n):
    return pl.BlockSpec(shape + (n,), lambda i, s: (0, 0, i))


def in_order(grad, order):
    rows, cols = grad.shape
    if len(order_blocks(rows, order)[0]) > 1:
        return grad.reshape(order.count, rows // order.count, cols)
    total = len(order.bits)
    index = lax.axis_index("dp")
    view = grad.reshape((2,) * total + (rows // order.count, cols))
    for bit in range(total):
        axis = total - 1 - bit
        view = jnp.where(((index >> bit) & 1) == 1, jnp.flip(view, axis), view)
    axes = [total - 1 - bit for bit in order.bits]
    view = jnp.transpose(view, axes + [total, total + 1])
    return view.reshape(order.count, rows // order.count, cols)


def swap_pair(value):
    return lax.ppermute(value, "tensor", [(0, 1), (1, 0)])


def swap_bits(value, count, mask):
    return lax.ppermute(value, "dp", [(i, i ^ mask) for i in range(count)])


def total_of(terms):
    total = terms[0].astype(F32)
    for term in terms[1:]:
        total = total + term.astype(F32)
    return total


class RowScatter:
    def __init__(self, terms, order, stages):
        self.count = order.count
        self.left = list(order.bits)
        self.terms = list(terms)
        self.marks = [tuple(order.bits)] * len(terms)
        stages = [[bit for bit in stage if bit in self.left] for stage in stages]
        used = [bit for stage in stages for bit in stage]
        stages = stages + [[bit] for bit in self.left if bit not in used]
        self.stages = [stage for stage in stages if stage]
        self.pending = []

    def pick(self, chosen):
        total = 0.0
        for term, bits in zip(self.terms, self.marks):
            view = term.reshape((2,) * len(bits) + term.shape[1:])
            at = tuple(chosen.get(bit, slice(None) if bit in self.left else 0) for bit in bits)
            total = total + view[at].reshape((-1,) + term.shape[1:]).astype(F32)
        return total

    def sums(self):
        bits = self.stages.pop(0)
        away, masks = [], []
        for j in range(1, 1 << len(bits)):
            masks.append(mask_of(bits, j))
            chosen = {bit: (masks[-1] >> bit) & 1 for bit in bits}
            away.append(self.pick(chosen).astype(BF16))
        self.left = [bit for bit in self.left if bit not in bits]
        return (away, masks)

    def send(self):
        self.away, masks = self.sums()
        self.pending = [swap_bits(away, self.count, mask) for away, mask in zip(self.away, masks)]

    def take(self, received):
        self.terms = self.terms + list(received)
        self.marks = self.marks + [tuple(self.left)] * len(received)

    def add(self):
        self.take(self.pending)
        self.pending = []

    def own(self):
        return self.pick({})[0]

    def more(self):
        return bool(self.stages)


class JointScatter:
    def __init__(self, *chains):
        self.chains = chains
        self.pending = []

    def send(self):
        stages = [chain.sums() for chain in self.chains]
        masks = stages[0][1]
        self.away = [jnp.stack(two) for two in zip(*[away for away, _ in stages])]
        count = self.chains[0].count
        self.pending = [swap_bits(away, count, mask) for away, mask in zip(self.away, masks)]

    def more(self):
        return bool(self.chains[0].stages)

    def add(self):
        for at, chain in enumerate(self.chains):
            chain.take([m[at] for m in self.pending])
        self.pending = []


class SumAll:
    def __init__(self, value, count, bits):
        self.value = value
        self.count = count
        total = count.bit_length() - 1
        bits = [bit for bit in bits if bit < total]
        self.bits = bits + [bit for bit in range(total) if bit not in bits]

    def send(self):
        self.pending = swap_bits(self.value, self.count, 1 << self.bits.pop(0))

    def add(self):
        self.value = self.value + self.pending

    def finish(self):
        self.add()
        while self.bits:
            self.send()
            self.add()
        return self.value


def fence(*values):
    return lax.optimization_barrier(values)


def attend_back_kernel(
    scalars, g_ref, gt_ref, tokt_ref, q_all, k_all, v_all, p_all, c_all, wo_ref, sums_ref, *rest,
):
    wq_ref = rest[0] if len(rest) == 7 else None
    first_ref, lines_ref, grada_ref, gradb_ref, acc_ref = rest[1:6] if wq_ref is not None else rest
    d_ref = rest[6] if wq_ref is not None else first_ref
    step = pl.program_id(0)
    q_ref, k_ref, v_ref, p_ref, c_ref = [ref.at[step] for ref in (q_all, k_all, v_all, p_all, c_all)]
    rows, cols = q_ref.shape
    scale = 1.0 / math.sqrt(HEAD_DIM)
    grad_context = dot(g_ref[...], wo_ref[...], NT).astype(BF16)
    lane = lax.broadcasted_iota(jnp.int32, (rows, PAIR), 1)
    low = lane < HEAD_DIM
    zero = jnp.zeros((rows, PAIR), BF16)
    for pair in range(cols // PAIR):
        lo = pair * PAIR
        at = pl.ds(lo, PAIR)
        q = q_ref[:, at]
        v = v_ref[:, at]
        k = k_ref[:, at]
        do = grad_context[:, lo : lo + PAIR]
        product = do.astype(F32) * c_ref[:, at].astype(F32)
        q_t = q.T
        do_t = do.T
        grads_q, grads_k, grads_v = [], [], []
        for half in range(2):
            mine = low if half == 0 else lane >= HEAD_DIM
            row_dot = jnp.sum(jnp.where(mine, product, 0.0), axis=1, keepdims=True)
            probs = p_ref[pair * 2 + half]
            grad_probs = dot(jnp.where(mine, do, zero), v, NT)
            grad_scores = (probs.astype(F32) * (grad_probs - row_dot)).astype(BF16)
            grads_q.append(dot(grad_scores, k))
            own = slice(half * HEAD_DIM, (half + 1) * HEAD_DIM)
            grads_k.append(dot(q_t[own], grad_scores))
            grads_v.append(dot(do_t[own], probs))
        d_ref[0, :, at] = (jnp.where(low, grads_q[0], grads_q[1]) * scale).astype(BF16)
        d_ref[1, :, at] = jnp.concatenate(grads_k, axis=0).T.astype(BF16)
        d_ref[2, :, at] = jnp.concatenate(grads_v, axis=0).T.astype(BF16)
    if wq_ref is not None:
        first_ref[...] = input_part(d_ref, wq_ref).astype(BF16)
    tok_t = tokt_ref[...].reshape(-1, rows)
    g_t = gt_ref[...].reshape(-1, rows)
    new = [dot(tok_t, d_ref[j]) for j in range(3)] + [dot(g_t, c_ref[...])]
    bias = [column_sum(d_ref[j].astype(F32)) for j in (0, 2)]
    lines = sums_ref.shape[0]
    spots = [(slice(lines, lines + 1), slice(j * cols, (j + 1) * cols)) for j in range(2)]

    @pl.when(step == 0)
    def _():
        lines_ref[...] = jnp.zeros(lines_ref.shape, F32)
        lines_ref[:lines] = sums_ref[...]
        for j in range(4):
            acc_ref[j] = new[j]
        for spot, line in zip(spots, bias):
            lines_ref[spot] = line

    @pl.when(step > 0)
    def _():
        for j in range(4):
            acc_ref[j] = acc_ref[j] + new[j]
        for spot, line in zip(spots, bias):
            lines_ref[spot] = lines_ref[spot] + line

    @pl.when(step == pl.num_programs(0) - 1)
    def _():
        for j, grad_ref in enumerate((grada_ref, grada_ref, gradb_ref, gradb_ref)):
            at = (j % 2) * cols
            grad_ref[:, at : at + cols] = acc_ref[j].astype(BF16)


def attend_back(scalars, g, g_t, tok_t, q, k, v, p, c, wo, sums, wq=None):
    rows, width = g.shape
    seqs, heads, n, _ = p.shape
    cols = q.shape[1]
    q, k, v, c = [m.reshape(seqs, n, cols) for m in (q, k, v, c)]
    turned = transposed_spec(g_t.shape[:2], n)
    extra = () if wq is None else (wq,)
    if wq is None:
        first_spec = pl.BlockSpec((3, n, cols), lambda i, s: (0, i, 0))
        first_shape = (3, rows, cols)
    else:
        first_spec = rows_spec(n, width)
        first_shape = (rows, width)
    return call(
        attend_back_kernel,
        "attend_back",
        (seqs,),
        [rows_spec(n, width), turned, turned]
        + [pl.BlockSpec(memory_space=pltpu.VMEM)] * 5
        + [
            fixed_spec(wo.shape),
            fixed_spec(sums.shape),
        ]
        + [fixed_spec(w.shape) for w in extra],
        [first_spec, fixed_spec((16, 2 * cols))] + [fixed_spec((width, 2 * cols))] * 2,
        [sd(first_shape, BF16), sd((16, 2 * cols), F32)] + [sd((width, 2 * cols), BF16)] * 2,
        [pltpu.VMEM((4, width, cols), F32)] + [pltpu.VMEM((3, n, cols), BF16)] * len(extra),
        (
            (10 + 6 * len(extra)) * rows * width * cols + 16 * rows * n * cols,
            2 * (rows * n * heads + 8 * rows * cols + 8 * width * cols),
            0,
        ),
        32,
    )(scalars, g, g_t, tok_t, q, k, v, p, c, wo, sums, *extra)


def input_part(d_ref, w_ref):
    return dot(d_ref[0], w_ref[0], NT) + dot(d_ref[1], w_ref[1], NT) + dot(d_ref[2], w_ref[2], NT)


def input_grad_kernel(scalars, g1_ref, part_ref, d_ref, w_ref, whole_ref, mine_ref):
    own = input_part(d_ref, w_ref).astype(BF16).astype(F32)
    mine_ref[...] = (g1_ref[...] + (own + part_ref[...].astype(F32))).astype(BF16)
    whole_ref[...] = mine_ref[...]


def input_grad(scalars, g1, part, d, w, tile):
    rows, width = g1.shape
    cols = d.shape[2]
    steps = rows // tile
    tok_spec = rows_spec(tile, width)
    return call(
        input_grad_kernel,
        "input_grad",
        (steps,),
        [tok_spec, tok_spec, pl.BlockSpec((3, tile, cols), lambda i, s: (0, i, 0)), fixed_spec(w.shape)],
        [side_spec(tile, width, steps), tok_spec],
        [sd((2 * rows, width), BF16), sd((rows, width), BF16)],
        [],
        (6 * rows * width * cols, 10 * rows * width + 6 * rows * cols + 6 * width * cols, 0),
        32,
    )(scalars, g1, part, d, w)


def shards(
    dp_count,
    tokens_in,
    segment_ids,
    w_qkv,
    bias_qv,
    w_out,
    bias_out,
    norm1_gain,
    norm1_shift,
    w_in,
    bias_in,
    w_down,
    bias_down,
    norm2_gain,
    norm2_shift,
    grad_output,
):
    seq_count, seq_length = segment_ids.shape
    half_seqs = seq_count // 2
    rows = half_seqs * seq_length
    width = tokens_in.shape[1]
    local_cols = w_qkv.shape[2]
    f = w_in.shape[1]
    side = lax.axis_index("tensor")
    scalars = jnp.stack([side, lax.axis_index("dp")]).astype(jnp.int32)
    order = Order(dp_count)

    vec = jnp.stack([bias_out, norm1_gain, norm1_shift, bias_down, norm2_gain, norm2_shift])
    bias_line = bias_in.reshape(1, f)
    others = [swap_pair(w) for w in (w_qkv, w_out, w_in, w_down)]
    *kept, part, tok_t = attend(scalars, tokens_in, segment_ids, w_qkv, bias_qv, w_out, order)
    part, bias_qv, bias_line = fence(part, bias_qv, bias_line)
    bias_others = [swap_pair(w) for w in (bias_qv, bias_line)]
    saved, parts = [kept], [part]
    others = [others[0], bias_others[0], others[1], others[2], bias_others[1], others[3]]
    w_qkv_two, bias_qv_two, w_out_two, w_in_two, bias_in_two, w_down_two = [
        (own, other)
        for own, other in zip(
            (w_qkv, bias_qv, w_out, w_in, bias_line, w_down), others
        )
    ]
    *kept, part = attend(
        scalars, tokens_in, segment_ids, w_qkv_two[1], bias_qv_two[1], w_out_two[1], None
    )
    saved.append(kept)
    parts.append(part)
    output, output_mine, g2_t, low_t, g1_t, *columns, g1, g1low, sums_own, sums_other = mlp(
        scalars, tokens_in, *parts, grad_output, vec,
        *bias_in_two, *w_in_two, *w_down_two, 256, (order, order, order),
    )

    def whole(full, other):
        return lax.dynamic_update_slice_in_dim(full, other, (1 - side) * rows, 0)

    def outer(left, right):
        return dot(left.reshape(width, rows), right).astype(BF16)

    lefts = (g2_t, g2_t, low_t, low_t)
    other_grads = [[swap_pair(outer(lefts[at], part[at])) for at in (1, 3)] for part in (columns[:4], columns[4:])]
    own_grads = [[outer(lefts[at], part[at]) for at in (0, 2)] for part in (columns[:4], columns[4:])]
    output_recv = swap_pair(output_mine)
    g1low, own_grads, other_grads = fence(g1low, own_grads, other_grads)

    def chain_of(part, at, *stages):
        return RowScatter([in_order(m[part][at], order) for m in (own_grads, other_grads)], order, stages)

    down = chain_of(0, 0, (0,), (1,), (3,), (2,))
    inner = chain_of(0, 1, (1,), (3,), (2,), (0,))
    down_rest, in_rest = [chain_of(1, at, (2,), (0,), (3,), (1,)) for at in (0, 1)]
    pair_rest = JointScatter(down_rest, in_rest)

    def back(at, g, *rest):
        return attend_back(scalars, g, g1_t, tok_t, *saved[at], w_out_two[at], *rest)

    down.send()
    inner.send()
    pair_rest.send()
    part_other, lines_other, *grads_other = back(1, g1low, sums_other, w_qkv_two[1])
    part_other, lines_other, grads_other, down.pending, inner.pending, pair_rest.pending, output_recv = fence(
        part_other, lines_other, grads_other, down.pending, inner.pending, pair_rest.pending, output_recv
    )
    grads_recv = [swap_pair(grad) for grad in grads_other]
    lines_recv = swap_pair(lines_other)

    def next_stage():
        for chain in (down, inner, pair_rest):
            chain.add()
        for chain in (down, inner, pair_rest):
            chain.send()

    next_stage()
    g1low, part_other = fence(g1low, part_other)
    d_own, lines_own, *grads_own = back(0, g1low, sums_own)
    d_own, lines_own, grads_own, grads_recv, lines_recv, down.pending, inner.pending, pair_rest.pending = fence(
        d_own, lines_own, grads_own, grads_recv, lines_recv, down.pending, inner.pending, pair_rest.pending
    )
    last = [order.bits[2:4]] if dp_count <= 16 else []
    head_a, head_b = [
        RowScatter([in_order(m, order) for m in terms], order, [[first], [1 - first]] + last)
        for first, terms in enumerate(zip(grads_own, grads_recv))
    ]
    lines = SumAll(lines_own + lines_recv, dp_count, (0, 2, 3, 1))
    lines.send()
    head_a.send()
    head_b.send()
    head_a.away, head_b.away, down.pending, inner.pending, pair_rest.pending = fence(
        head_a.away, head_b.away, down.pending, inner.pending, pair_rest.pending
    )
    next_stage()
    grad_input, grad_mine = input_grad(scalars, g1, part_other, d_own, w_qkv, 256)
    grad_input, grad_mine, head_a.pending, head_b.pending, lines.pending, output_recv = fence(
        grad_input, grad_mine, head_a.pending, head_b.pending, lines.pending, output_recv
    )
    lines.add()
    lines.send()
    head_a.add()
    head_b.add()
    head_a.send()
    head_b.send()
    head_a.away, head_b.away, down.pending, inner.pending, pair_rest.pending, output_recv, grad_mine = fence(
        head_a.away, head_b.away, down.pending, inner.pending, pair_rest.pending, output_recv, grad_mine
    )
    next_stage()
    grad_recv = swap_pair(grad_mine)
    output = whole(output, output_recv)
    output, head_a.pending, head_b.pending, lines.pending, grad_recv = fence(
        output, head_a.pending, head_b.pending, lines.pending, grad_recv
    )
    head_a.add()
    head_b.add()
    lines.add()
    lines.send()
    heads = JointScatter(head_a, head_b)
    heads.send()
    heads.away, down.pending, inner.pending, pair_rest.pending, grad_recv, lines.pending = fence(
        heads.away, down.pending, inner.pending, pair_rest.pending, grad_recv, lines.pending
    )
    lines.add()
    lines.send()
    for chain in (down, inner, pair_rest):
        chain.add()
        while chain.more():
            chain.send()
            chain.add()
    grad_input = whole(grad_input, grad_recv)
    summed_w_down = jnp.concatenate([down.own(), down_rest.own()], axis=1).T
    summed_w_in = jnp.concatenate([inner.own(), in_rest.own()], axis=1)
    grad_input, summed_w_down, summed_w_in, heads.pending, lines.pending = fence(
        grad_input, summed_w_down, summed_w_in, heads.pending, lines.pending
    )
    heads.add()
    while heads.more():
        heads.send()
        heads.add()
    total = lines.finish()
    at_stats = sums_own.shape[0] - 6
    summed_bias_in = total[:at_stats].reshape(f)
    summed = [total[at_stats + i] for i in range(6)]
    summed_bias_qv = total[at_stats + 6].reshape(2, local_cols)
    summed_a, summed_b = head_a.own(), head_b.own()
    summed_w_qkv = jnp.stack([summed_a[:, :local_cols], summed_a[:, local_cols:], summed_b[:, :local_cols]])
    summed_w_out = summed_b[:, local_cols:].T

    return (
        output,
        grad_input,
        summed_w_qkv,
        summed_bias_qv,
        summed_w_out,
        summed[0],
        summed[1],
        summed[2],
        summed_w_in,
        summed_bias_in,
        summed_w_down,
        summed[3],
        summed[4],
        summed[5],
    )


def solution(mesh):
    dp_count = mesh.shape["dp"]

    def body(*args):
        return shards(dp_count, *args)

    return jax.shard_map(
        body,
        mesh=mesh,
        in_specs=(
            P("dp", None),
            P("dp", None),
            P(None, None, "tensor"),
            P(None, "tensor"),
            P("tensor", None),
            P(),
            P(),
            P(),
            P(None, "tensor"),
            P("tensor"),
            P("tensor", None),
            P(),
            P(),
            P(),
            P("dp", None),
        ),
        out_specs=(
            P("dp", None),
            P("dp", None),
            P(None, "dp", "tensor"),
            P(None, "tensor"),
            P("tensor", "dp"),
            P(),
            P(),
            P(),
            P("dp", "tensor"),
            P("tensor"),
            P("tensor", "dp"),
            P(),
            P(),
            P(),
        ),
        check_vma=False,
    )
```

```python
import functools
import math

import jax
import jax.numpy as jnp
from jax import lax
from jax.experimental import pallas as pl
from jax.experimental.pallas import tpu as pltpu
from jax.sharding import PartitionSpec as P

HEAD_DIM = 64
PAIR = 2 * HEAD_DIM
LANES = 128


EPSILON = 1e-05
NEGATIVE = -1e30
ROOT_HALF = 0.7071067811865476
ROOT_TWO_PI_INV = 0.3989422804014327
F32 = jnp.float32
BF16 = jnp.bfloat16
NT = (((1,), (1,)), ((), ()))
NN = (((1,), (0,)), ((), ()))
CHUNK = 512
sd = jax.ShapeDtypeStruct


def dot(left, right, dims=NN):
    return lax.dot_general(left, right, dims, preferred_element_type=F32)


def mean_of(value):
    return jnp.sum(value, axis=1, keepdims=True) * (1.0 / value.shape[1])


def norm_forward(summed):
    centered = summed - mean_of(summed)
    inv_std = lax.rsqrt(mean_of(centered * centered) + EPSILON)
    return (centered * inv_std, inv_std)


def norm_backward(upstream, normed, inv_std, gain_vec):
    scaled_grad = upstream * gain_vec
    second_mean = mean_of(scaled_grad * normed)
    return inv_std * (scaled_grad - mean_of(scaled_grad) - normed * second_mean)


def gelu_pair(preact):
    cumulative = 0.5 + 0.5 * lax.erf(preact * ROOT_HALF)
    derivative = cumulative + preact * (jnp.exp(-0.5 * preact * preact) * ROOT_TWO_PI_INV)
    return (preact * cumulative, derivative)


def column_sum(value):
    return jnp.sum(value, axis=0, keepdims=True)


def rows_spec(n, c):
    return pl.BlockSpec((n, c), lambda i, s: (i, 0))


def side_spec(n, c, steps):
    return pl.BlockSpec((n, c), lambda i, s: (s[0] * steps + i, 0))


def fixed_spec(shape):
    return pl.BlockSpec(shape, lambda i, s: (0,) * len(shape), pipeline_mode=pl.Buffered(1))


def call(kernel, name, grid, in_specs, out_specs, out_shape, scratch, cost, limit=56):
    flops, moved, transcendentals = cost
    return pl.pallas_call(
        kernel,
        grid_spec=pltpu.PrefetchScalarGridSpec(
            num_scalar_prefetch=1,
            grid=grid,
            in_specs=in_specs,
            out_specs=out_specs,
            scratch_shapes=scratch,
        ),
        out_shape=out_shape,
        compiler_params=pltpu.CompilerParams(vmem_limit_bytes=limit * 1024 * 1024),
        cost_estimate=pl.CostEstimate(
            flops=flops, bytes_accessed=moved, transcendentals=transcendentals
        ),
        name=name,
    )


def put_transposed(out_ref, value, scratch, me, masks):
    scratch[...] = value.T.reshape(scratch.shape)
    if len(masks) == 1:
        out_ref[...] = scratch[...]
    else:
        for j, mask in enumerate(masks):
            out_ref[j] = scratch[me ^ mask]


def page_columns(page):
    line = lax.broadcasted_iota(jnp.int32, (LANES, page.shape[1]), 0)
    same = jnp.where(line == page, 1.0, 0.0).T
    lane = lax.broadcasted_iota(jnp.int32, same.shape, 1)
    pen = jnp.where((lane < 4) & (same == 0.0), NEGATIVE, 0.0)
    return (pen.astype(BF16), same.astype(BF16))


def attend_kernel(
    scalars, tok_ref, seg_ref, wq_ref, bq_ref, wo_ref, q_ref, k_ref, v_ref, p_ref, c_ref, part_ref
):
    row = scalars[0] * pl.num_programs(0) + pl.program_id(0)
    pen, hot = page_columns(seg_ref[pl.ds(row, 1), :])
    tok = tok_ref[...]
    scale = 1.0 / math.sqrt(HEAD_DIM)
    bias = bq_ref[...].astype(F32)
    q_ref[...] = ((dot(tok, wq_ref[0]) + bias[0:1]).astype(BF16) * scale).astype(BF16)
    k_ref[...] = dot(tok, wq_ref[1]).astype(BF16)
    v_ref[...] = (dot(tok, wq_ref[2]) + bias[1:2]).astype(BF16)
    rows, cols = q_ref.shape
    lane = lax.broadcasted_iota(jnp.int32, (rows, PAIR), 1)
    zero = jnp.zeros((rows, PAIR), BF16)
    for pair in range(cols // PAIR):
        at = pl.ds(pair * PAIR, PAIR)
        q = q_ref[:, at]
        v = v_ref[:, at]
        k_wide = jnp.concatenate([k_ref[:, at], hot], axis=1)
        outs = []
        for half in range(2):
            mine = (lane < HEAD_DIM) if half == 0 else (lane >= HEAD_DIM)
            q_wide = jnp.concatenate([jnp.where(mine, q, zero), pen], axis=1)
            scores = dot(q_wide, k_wide, NT)
            top = jnp.max(scores, axis=1, keepdims=True)
            exp_scores = jnp.exp(scores - top)
            total = jnp.sum(exp_scores, axis=1, keepdims=True)
            probs = (exp_scores * (1.0 / total)).astype(BF16)
            p_ref[0, pair * 2 + half] = probs
            outs.append(dot(probs, v))
        c_ref[:, at] = jnp.where(lane < HEAD_DIM, outs[0], outs[1]).astype(BF16)
    part_ref[...] = dot(c_ref[...], wo_ref[...]).astype(BF16)


def attend(scalars, tok, seg, wq, bq, wo):
    width = tok.shape[1]
    seqs = seg.shape[0] // 2
    n = seg.shape[1]
    rows = seqs * n
    cols = wq.shape[2]
    heads = cols // HEAD_DIM
    return call(
        attend_kernel,
        "attend",
        (seqs,),
        [
            side_spec(n, width, seqs),
            fixed_spec(seg.shape),
            fixed_spec(wq.shape),
            fixed_spec(bq.shape),
            fixed_spec(wo.shape),
        ],
        [rows_spec(n, cols)] * 3
        + [
            pl.BlockSpec((1, heads, n, n), lambda i, s: (i, 0, 0, 0)),
            rows_spec(n, cols),
            rows_spec(n, width),
        ],
        [sd((rows, cols), BF16)] * 3
        + [sd((seqs, heads, n, n), BF16), sd((rows, cols), BF16), sd((rows, width), BF16)],
        [],
        (
            8 * rows * width * cols + 12 * rows * n * cols,
            2 * (rows * n * heads + 7 * rows * cols + 4 * width * cols),
            rows * n * heads,
        ),
    )(scalars, tok, seg, wq, bq, wo)


def part_of(main, rest, start):
    most = main.shape[1]
    return (main, start) if start < most else (rest, start - most)


def mlp_kernel(
    masks, scalars, tok_ref, pa_ref, pb_ref, up_ref, vec_ref, ba_ref, bb_ref,
    wia_hbm, wib_hbm, wda_hbm, wdb_hbm,
    out_ref, mine_ref, g2t_ref, lowt_ref, g1t_ref, tokt_ref, ha_ref, hb_ref, gpa_ref, gpb_ref,
    ha_rest, hb_rest, gpa_rest, gpb_rest, g1_ref, g1low_ref,
    sumsa_ref, sumsb_ref,
    wia, wib, wda, wdb, dv_ref, low_ref, g2low_ref, turn, sem,
):
    step = pl.program_id(0)
    pairs = ((wia_hbm, wia), (wib_hbm, wib), (wda_hbm, wda), (wdb_hbm, wdb))
    copies = [pltpu.make_async_copy(s, d, sem.at[i]) for i, (s, d) in enumerate(pairs)]

    def tile(first):
        def arrive(i):
            if first:
                copies[i].wait()

        vec = vec_ref[...].astype(F32)
        bias_out, gain1, shift1, bias_down, gain2, shift2 = [vec[i : i + 1] for i in range(6)]
        attention = pa_ref[...].astype(F32) + pb_ref[...].astype(F32)
        normed1, inv1 = norm_forward(tok_ref[...].astype(F32) + attention + bias_out)
        normed_one = normed1 * gain1 + shift1
        low_ref[...] = normed_one.astype(BF16)
        f = wia.shape[1]
        for k, (wi, bi) in enumerate(((wia, ba_ref), (wib, bb_ref))):
            arrive(k)
            for c in range(0, f, CHUNK):
                preact = dot(low_ref[...], wi[:, c : c + CHUNK]) + bi[:, c : c + CHUNK].astype(F32)
                hidden, derivative = gelu_pair(preact)
                at = k * f + c
                h_ref, spot = part_of((ha_ref, hb_ref)[k], (ha_rest, hb_rest)[k], c)
                h_ref[:, spot : spot + CHUNK] = hidden.astype(BF16)
                dv_ref[:, at : at + CHUNK] = derivative.astype(BF16)
        put_transposed(lowt_ref, low_ref[...], turn, scalars[1], masks[1])
        put_transposed(tokt_ref, tok_ref[...], turn, scalars[1], masks[3])
        parts = []
        for k, (wd, h_ref, h_rest) in enumerate(((wda, ha_ref, ha_rest), (wdb, hb_ref, hb_rest))):
            arrive(2 + k)
            most = h_ref.shape[1]
            part = dot(jnp.concatenate([h_ref[...], h_rest[...]], axis=1), wd[...])
            parts.append(part.astype(BF16).astype(F32))
        normed2, inv2 = norm_forward(normed_one + (parts[0] + parts[1]) + bias_down)
        mine_ref[...] = (normed2 * gain2 + shift2).astype(BF16)
        out_ref[...] = mine_ref[...]
        up = up_ref[...].astype(F32)
        g2 = norm_backward(up, normed2, inv2, gain2)
        g2low_ref[...] = g2.astype(BF16)
        stats = [column_sum(g2), column_sum(up * normed2), column_sum(up)]
        put_transposed(g2t_ref, g2low_ref[...], turn, scalars[1], masks[0])
        sums = []
        for k, wd in enumerate((wda, wdb)):
            for c in range(0, f, CHUNK):
                at = k * f + c
                grad_hidden = dot(g2low_ref[...], wd[c : c + CHUNK, :], NT)
                grad_preact = (grad_hidden * dv_ref[:, at : at + CHUNK].astype(F32)).astype(BF16)
                gp_ref, spot = part_of((gpa_ref, gpb_ref)[k], (gpa_rest, gpb_rest)[k], c)
                gp_ref[:, spot : spot + CHUNK] = grad_preact
                sums.append(column_sum(grad_preact.astype(F32)))
        parts = []
        for wi, gp_ref, gp_rest in ((wia, gpa_ref, gpa_rest), (wib, gpb_ref, gpb_rest)):
            most = gp_ref.shape[1]
            part = dot(jnp.concatenate([gp_ref[...], gp_rest[...]], axis=1), wi[...], NT)
            parts.append(part.astype(BF16).astype(F32))
        grad = g2 + (parts[0] + parts[1])
        g1 = norm_backward(grad, normed1, inv1, gain1)
        g1_ref[...] = g1
        g1low_ref[...] = g1.astype(BF16)
        put_transposed(g1t_ref, g1low_ref[...], turn, scalars[1], masks[2])
        stats = [column_sum(g1), column_sum(grad * normed1), column_sum(grad)] + stats
        width = g1.shape[1]
        lines = [
            jnp.concatenate(s, axis=1)
            for s in (sums[: f // CHUNK], sums[f // CHUNK :])
        ]
        for line, sums_ref in zip(lines, (sumsa_ref, sumsb_ref)):
            block = [line[:, c : c + width] for c in range(0, f, width)] + stats
            block = jnp.concatenate(block, axis=0)
            sums_ref[...] = block if first else sums_ref[...] + block

    @pl.when(step == 0)
    def _():
        for copy in copies:
            copy.start()
        tile(True)

    @pl.when(step > 0)
    def _():
        tile(False)


def mlp(scalars, tok, pa, pb, up, vec, ba, bb, wia, wib, wda, wdb, tile, orders):
    rows, width = pa.shape
    f = wia.shape[1]
    steps = rows // tile
    hbm = pl.BlockSpec(memory_space=pl.ANY)
    tok_spec = rows_spec(tile, width)
    mine_spec = side_spec(tile, width, steps)
    masks = [order_blocks(width, order)[0] for order in orders]
    shape = order_blocks(width, orders[0])[1]
    lines = f // width + 6
    most = f // CHUNK * 2 // 3 * CHUNK
    return call(
        functools.partial(mlp_kernel, masks),
        "mlp",
        (steps,),
        [mine_spec, tok_spec, tok_spec, mine_spec]
        + [fixed_spec(vec.shape), fixed_spec(ba.shape), fixed_spec(bb.shape)]
        + [hbm] * 4,
        [mine_spec, tok_spec]
        + [transposed_spec(shape, tile)] * 4
        + [rows_spec(tile, most)] * 4
        + [rows_spec(tile, f - most)] * 4
        + [tok_spec] * 2
        + [fixed_spec((lines, width))] * 2,
        [sd((2 * rows, width), BF16), sd((rows, width), BF16)]
        + [sd(shape + (rows,), BF16)] * 4
        + [sd((rows, most), BF16)] * 4
        + [sd((rows, f - most), BF16)] * 4
        + [sd((rows, width), F32), sd((rows, width), BF16)]
        + [sd((lines, width), F32)] * 2,
        [pltpu.VMEM((width, f), BF16)] * 2
        + [pltpu.VMEM((f, width), BF16)] * 2
        + [pltpu.VMEM((tile, 2 * f), BF16)]
        + [pltpu.VMEM((tile, width), BF16)] * 2
        + [pltpu.VMEM(shape + (tile,), BF16), pltpu.SemaphoreType.DMA((4,))],
        (16 * rows * width * f, 8 * width * f + 30 * rows * width + 8 * rows * f, 4 * rows * f),
    )(scalars, tok, pa, pb, up, vec, ba, bb, wia, wib, wda, wdb)


class Order:
    def __init__(self, count):
        self.count = count
        self.bits = list(range(count.bit_length() - 1))

    def masks(self):
        return [mask_of(self.bits, j) for j in range(self.count)]


def mask_of(bits, j):
    size = len(bits)
    return sum(((j >> (size - 1 - k)) & 1) << bit for k, bit in enumerate(bits))


def order_blocks(width, order):
    if (width // order.count) % 16 == 0:
        return (order.masks(), (order.count, width // order.count))
    return ([0], (1, width))


def transposed_spec(shape, n):
    return pl.BlockSpec(shape + (n,), lambda i, s: (0, 0, i))


def in_order(grad, order):
    rows, cols = grad.shape
    if len(order_blocks(rows, order)[0]) > 1:
        return grad.reshape(order.count, rows // order.count, cols)
    total = len(order.bits)
    index = lax.axis_index("dp")
    view = grad.reshape((2,) * total + (rows // order.count, cols))
    for bit in range(total):
        axis = total - 1 - bit
        view = jnp.where(((index >> bit) & 1) == 1, jnp.flip(view, axis), view)
    axes = [total - 1 - bit for bit in order.bits]
    view = jnp.transpose(view, axes + [total, total + 1])
    return view.reshape(order.count, rows // order.count, cols)


def swap_pair(value):
    return lax.ppermute(value, "tensor", [(0, 1), (1, 0)])


def swap_bits(value, count, mask):
    return lax.ppermute(value, "dp", [(i, i ^ mask) for i in range(count)])


def total_of(terms):
    total = terms[0].astype(F32)
    for term in terms[1:]:
        total = total + term.astype(F32)
    return total


class RowScatter:
    def __init__(self, terms, order, stages):
        self.count = order.count
        self.left = list(order.bits)
        self.terms = list(terms)
        self.marks = [tuple(order.bits)] * len(terms)
        stages = [[bit for bit in stage if bit in self.left] for stage in stages]
        used = [bit for stage in stages for bit in stage]
        stages = stages + [[bit] for bit in self.left if bit not in used]
        self.stages = [stage for stage in stages if stage]
        self.pending = []

    def pick(self, chosen):
        total = 0.0
        for term, bits in zip(self.terms, self.marks):
            view = term.reshape((2,) * len(bits) + term.shape[1:])
            at = tuple(chosen.get(bit, slice(None) if bit in self.left else 0) for bit in bits)
            total = total + view[at].reshape((-1,) + term.shape[1:]).astype(F32)
        return total

    def sums(self):
        bits = self.stages.pop(0)
        away, masks = [], []
        for j in range(1, 1 << len(bits)):
            masks.append(mask_of(bits, j))
            chosen = {bit: (masks[-1] >> bit) & 1 for bit in bits}
            away.append(self.pick(chosen).astype(BF16))
        self.left = [bit for bit in self.left if bit not in bits]
        return (away, masks)

    def send(self):
        self.away, masks = self.sums()
        self.pending = [swap_bits(away, self.count, mask) for away, mask in zip(self.away, masks)]

    def take(self, received):
        self.terms = self.terms + list(received)
        self.marks = self.marks + [tuple(self.left)] * len(received)

    def add(self):
        self.take(self.pending)
        self.pending = []

    def own(self):
        return self.pick({})[0]

    def more(self):
        return bool(self.stages)


class JointScatter:
    def __init__(self, *chains):
        self.chains = chains
        self.pending = []

    def send(self):
        stages = [chain.sums() for chain in self.chains]
        masks = stages[0][1]
        self.away = [jnp.stack(two) for two in zip(*[away for away, _ in stages])]
        count = self.chains[0].count
        self.pending = [swap_bits(away, count, mask) for away, mask in zip(self.away, masks)]

    def more(self):
        return bool(self.chains[0].stages)

    def add(self):
        for at, chain in enumerate(self.chains):
            chain.take([m[at] for m in self.pending])
        self.pending = []


class SumAll:
    def __init__(self, value, count, bits):
        self.value = value
        self.count = count
        total = count.bit_length() - 1
        bits = [bit for bit in bits if bit < total]
        self.bits = bits + [bit for bit in range(total) if bit not in bits]

    def send(self):
        self.pending = swap_bits(self.value, self.count, 1 << self.bits.pop(0))

    def add(self):
        self.value = self.value + self.pending

    def finish(self):
        self.add()
        while self.bits:
            self.send()
            self.add()
        return self.value


def fence(*values):
    return lax.optimization_barrier(values)


def attend_back_kernel(
    scalars, g_ref, gt_ref, tokt_ref, q_all, k_all, v_all, p_all, c_all, wo_ref, sums_ref, *rest,
):
    wq_ref = rest[0] if len(rest) == 7 else None
    first_ref, lines_ref, grada_ref, gradb_ref, acc_ref = rest[1:6] if wq_ref is not None else rest
    d_ref = rest[6] if wq_ref is not None else first_ref
    step = pl.program_id(0)
    q_ref, k_ref, v_ref, p_ref, c_ref = [ref.at[step] for ref in (q_all, k_all, v_all, p_all, c_all)]
    rows, cols = q_ref.shape
    scale = 1.0 / math.sqrt(HEAD_DIM)
    grad_context = dot(g_ref[...], wo_ref[...], NT).astype(BF16)
    lane = lax.broadcasted_iota(jnp.int32, (rows, PAIR), 1)
    low = lane < HEAD_DIM
    zero = jnp.zeros((rows, PAIR), BF16)
    for pair in range(cols // PAIR):
        lo = pair * PAIR
        at = pl.ds(lo, PAIR)
        q = q_ref[:, at]
        v = v_ref[:, at]
        k = k_ref[:, at]
        do = grad_context[:, lo : lo + PAIR]
        product = do.astype(F32) * c_ref[:, at].astype(F32)
        q_t = q.T
        do_t = do.T
        grads_q, grads_k, grads_v = [], [], []
        for half in range(2):
            mine = low if half == 0 else lane >= HEAD_DIM
            row_dot = jnp.sum(jnp.where(mine, product, 0.0), axis=1, keepdims=True)
            probs = p_ref[pair * 2 + half]
            grad_probs = dot(jnp.where(mine, do, zero), v, NT)
            grad_scores = (probs.astype(F32) * (grad_probs - row_dot)).astype(BF16)
            grads_q.append(dot(grad_scores, k))
            own = slice(half * HEAD_DIM, (half + 1) * HEAD_DIM)
            grads_k.append(dot(q_t[own], grad_scores))
            grads_v.append(dot(do_t[own], probs))
        d_ref[0, :, at] = (jnp.where(low, grads_q[0], grads_q[1]) * scale).astype(BF16)
        d_ref[1, :, at] = jnp.concatenate(grads_k, axis=0).T.astype(BF16)
        d_ref[2, :, at] = jnp.concatenate(grads_v, axis=0).T.astype(BF16)
    if wq_ref is not None:
        first_ref[...] = input_part(d_ref, wq_ref).astype(BF16)
    tok_t = tokt_ref[...].reshape(-1, rows)
    g_t = gt_ref[...].reshape(-1, rows)
    new = [dot(tok_t, d_ref[j]) for j in range(3)] + [dot(g_t, c_ref[...])]
    bias = [column_sum(d_ref[j].astype(F32)) for j in (0, 2)]
    lines = sums_ref.shape[0]
    spots = [(slice(lines, lines + 1), slice(j * cols, (j + 1) * cols)) for j in range(2)]

    @pl.when(step == 0)
    def _():
        lines_ref[...] = jnp.zeros(lines_ref.shape, F32)
        lines_ref[:lines] = sums_ref[...]
        for j in range(4):
            acc_ref[j] = new[j]
        for spot, line in zip(spots, bias):
            lines_ref[spot] = line

    @pl.when(step > 0)
    def _():
        for j in range(4):
            acc_ref[j] = acc_ref[j] + new[j]
        for spot, line in zip(spots, bias):
            lines_ref[spot] = lines_ref[spot] + line

    @pl.when(step == pl.num_programs(0) - 1)
    def _():
        for j, grad_ref in enumerate((grada_ref, grada_ref, gradb_ref, gradb_ref)):
            at = (j % 2) * cols
            grad_ref[:, at : at + cols] = acc_ref[j].astype(BF16)


def attend_back(scalars, g, g_t, tok_t, q, k, v, p, c, wo, sums, wq=None):
    rows, width = g.shape
    seqs, heads, n, _ = p.shape
    cols = q.shape[1]
    q, k, v, c = [m.reshape(seqs, n, cols) for m in (q, k, v, c)]
    turned = transposed_spec(g_t.shape[:2], n)
    extra = () if wq is None else (wq,)
    if wq is None:
        first_spec = pl.BlockSpec((3, n, cols), lambda i, s: (0, i, 0))
        first_shape = (3, rows, cols)
    else:
        first_spec = rows_spec(n, width)
        first_shape = (rows, width)
    return call(
        attend_back_kernel,
        "attend_back",
        (seqs,),
        [rows_spec(n, width), turned, turned]
        + [pl.BlockSpec(memory_space=pltpu.VMEM)] * 5
        + [
            fixed_spec(wo.shape),
            fixed_spec(sums.shape),
        ]
        + [fixed_spec(w.shape) for w in extra],
        [first_spec, fixed_spec((16, 2 * cols))] + [fixed_spec((width, 2 * cols))] * 2,
        [sd(first_shape, BF16), sd((16, 2 * cols), F32)] + [sd((width, 2 * cols), BF16)] * 2,
        [pltpu.VMEM((4, width, cols), F32)] + [pltpu.VMEM((3, n, cols), BF16)] * len(extra),
        (
            (10 + 6 * len(extra)) * rows * width * cols + 16 * rows * n * cols,
            2 * (rows * n * heads + 8 * rows * cols + 8 * width * cols),
            0,
        ),
        25 + 7 * len(extra),
    )(scalars, g, g_t, tok_t, q, k, v, p, c, wo, sums, *extra)


def input_part(d_ref, w_ref):
    return dot(d_ref[0], w_ref[0], NT) + dot(d_ref[1], w_ref[1], NT) + dot(d_ref[2], w_ref[2], NT)


def input_grad_kernel(scalars, g1_ref, part_ref, d_ref, w_ref, whole_ref, mine_ref):
    own = input_part(d_ref, w_ref).astype(BF16).astype(F32)
    mine_ref[...] = (g1_ref[...] + (own + part_ref[...].astype(F32))).astype(BF16)
    whole_ref[...] = mine_ref[...]


def input_grad(scalars, g1, part, d, w, tile):
    rows, width = g1.shape
    cols = d.shape[2]
    steps = rows // tile
    tok_spec = rows_spec(tile, width)
    return call(
        input_grad_kernel,
        "input_grad",
        (steps,),
        [tok_spec, tok_spec, pl.BlockSpec((3, tile, cols), lambda i, s: (0, i, 0)), fixed_spec(w.shape)],
        [side_spec(tile, width, steps), tok_spec],
        [sd((2 * rows, width), BF16), sd((rows, width), BF16)],
        [],
        (6 * rows * width * cols, 10 * rows * width + 6 * rows * cols + 6 * width * cols, 0),
        32,
    )(scalars, g1, part, d, w)


def shards(
    dp_count,
    tokens_in,
    segment_ids,
    w_qkv,
    bias_qv,
    w_out,
    bias_out,
    norm1_gain,
    norm1_shift,
    w_in,
    bias_in,
    w_down,
    bias_down,
    norm2_gain,
    norm2_shift,
    grad_output,
):
    seq_count, seq_length = segment_ids.shape
    half_seqs = seq_count // 2
    rows = half_seqs * seq_length
    width = tokens_in.shape[1]
    local_cols = w_qkv.shape[2]
    f = w_in.shape[1]
    side = lax.axis_index("tensor")
    scalars = jnp.stack([side, lax.axis_index("dp")]).astype(jnp.int32)
    order = Order(dp_count)

    vec = jnp.stack([bias_out, norm1_gain, norm1_shift, bias_down, norm2_gain, norm2_shift])
    bias_line = bias_in.reshape(1, f)
    others = [swap_pair(w) for w in (w_qkv, w_out, w_in, w_down)]
    *kept, part = attend(scalars, tokens_in, segment_ids, w_qkv, bias_qv, w_out)
    part, bias_qv, bias_line = fence(part, bias_qv, bias_line)
    bias_others = [swap_pair(w) for w in (bias_qv, bias_line)]
    saved, parts = [kept], [part]
    others = [others[0], bias_others[0], others[1], others[2], bias_others[1], others[3]]
    w_qkv_two, bias_qv_two, w_out_two, w_in_two, bias_in_two, w_down_two = [
        (own, other)
        for own, other in zip(
            (w_qkv, bias_qv, w_out, w_in, bias_line, w_down), others
        )
    ]
    *kept, part = attend(scalars, tokens_in, segment_ids, w_qkv_two[1], bias_qv_two[1], w_out_two[1])
    saved.append(kept)
    parts.append(part)
    output, output_mine, g2_t, low_t, g1_t, tok_t, *columns, g1, g1low, sums_own, sums_other = mlp(
        scalars, tokens_in, *parts, grad_output, vec,
        *bias_in_two, *w_in_two, *w_down_two, 256, (order,) * 4,
    )

    def whole(full, other):
        return lax.dynamic_update_slice_in_dim(full, other, (1 - side) * rows, 0)

    def outer(left, right):
        return dot(left.reshape(width, rows), right).astype(BF16)

    lefts = (g2_t, g2_t, low_t, low_t)
    other_grads = [[swap_pair(outer(lefts[at], part[at])) for at in (1, 3)] for part in (columns[:4], columns[4:])]
    own_grads = [[outer(lefts[at], part[at]) for at in (0, 2)] for part in (columns[:4], columns[4:])]
    output_recv = swap_pair(output_mine)
    g1low, own_grads, other_grads = fence(g1low, own_grads, other_grads)

    def chain_of(part, at, *stages):
        return RowScatter([in_order(m[part][at], order) for m in (own_grads, other_grads)], order, stages)

    down = chain_of(0, 0, (0,), (1,), (2,), (3,))
    inner = chain_of(0, 1, (1,), (3,), (2,), (0,))
    down_rest, in_rest = [chain_of(1, at, (2,), (0,), (3,), (1,)) for at in (0, 1)]
    pair_rest = JointScatter(down_rest, in_rest)

    def back(at, g, *rest):
        return attend_back(scalars, g, g1_t, tok_t, *saved[at], w_out_two[at], *rest)

    down.send()
    inner.send()
    pair_rest.send()
    part_other, lines_other, *grads_other = back(1, g1low, sums_other, w_qkv_two[1])
    part_other, lines_other, grads_other, down.pending, inner.pending, pair_rest.pending, output_recv = fence(
        part_other, lines_other, grads_other, down.pending, inner.pending, pair_rest.pending, output_recv
    )
    grads_recv = [swap_pair(grad) for grad in grads_other]
    lines_recv = swap_pair(lines_other)

    def next_stage():
        for chain in (down, inner, pair_rest):
            chain.add()
        for chain in (down, inner, pair_rest):
            chain.send()

    next_stage()
    g1low, part_other = fence(g1low, part_other)
    d_own, lines_own, *grads_own = back(0, g1low, sums_own)
    d_own, lines_own, grads_own, grads_recv, lines_recv, down.pending, inner.pending, pair_rest.pending = fence(
        d_own, lines_own, grads_own, grads_recv, lines_recv, down.pending, inner.pending, pair_rest.pending
    )
    last = [order.bits[2:4]] if dp_count <= 16 else []
    head_a, head_b = [
        RowScatter([in_order(m, order) for m in terms], order, [[first], [1 - first]] + last)
        for first, terms in enumerate(zip(grads_own, grads_recv))
    ]
    lines = SumAll(lines_own + lines_recv, dp_count, (0, 3, 2, 1))
    lines.send()
    head_a.send()
    head_b.send()
    head_a.away, head_b.away, down.pending, inner.pending, pair_rest.pending = fence(
        head_a.away, head_b.away, down.pending, inner.pending, pair_rest.pending
    )
    next_stage()
    d_own, lines.pending = fence(d_own, lines.pending)
    grad_input, grad_mine = input_grad(scalars, g1, part_other, d_own, w_qkv, 256)
    grad_input, grad_mine, head_a.pending, head_b.pending, lines.pending, output_recv = fence(
        grad_input, grad_mine, head_a.pending, head_b.pending, lines.pending, output_recv
    )
    lines.add()
    lines.send()
    head_a.add()
    head_b.add()
    head_a.send()
    head_b.send()
    head_a.away, head_b.away, down.pending, inner.pending, pair_rest.pending, output_recv, grad_mine = fence(
        head_a.away, head_b.away, down.pending, inner.pending, pair_rest.pending, output_recv, grad_mine
    )
    next_stage()
    grad_recv = swap_pair(grad_mine)
    output = whole(output, output_recv)
    output, head_a.pending, head_b.pending, lines.pending, grad_recv = fence(
        output, head_a.pending, head_b.pending, lines.pending, grad_recv
    )
    head_a.add()
    head_b.add()
    lines.add()
    lines.send()
    heads = JointScatter(head_a, head_b)
    heads.send()
    heads.away, down.pending, inner.pending, pair_rest.pending, grad_recv, lines.pending = fence(
        heads.away, down.pending, inner.pending, pair_rest.pending, grad_recv, lines.pending
    )
    lines.add()
    lines.send()
    for chain in (down, inner, pair_rest):
        chain.add()
        while chain.more():
            chain.send()
            chain.add()
    grad_input = whole(grad_input, grad_recv)
    summed_w_down = jnp.concatenate([down.own(), down_rest.own()], axis=1).T
    summed_w_in = jnp.concatenate([inner.own(), in_rest.own()], axis=1)
    grad_input, summed_w_down, summed_w_in, heads.pending, lines.pending = fence(
        grad_input, summed_w_down, summed_w_in, heads.pending, lines.pending
    )
    heads.add()
    while heads.more():
        heads.send()
        heads.add()
    total = lines.finish()
    at_stats = sums_own.shape[0] - 6
    summed_bias_in = total[:at_stats].reshape(f)
    summed = [total[at_stats + i] for i in range(6)]
    summed_bias_qv = total[at_stats + 6].reshape(2, local_cols)
    summed_a, summed_b = head_a.own(), head_b.own()
    summed_w_qkv = jnp.stack([summed_a[:, :local_cols], summed_a[:, local_cols:], summed_b[:, :local_cols]])
    summed_w_out = summed_b[:, local_cols:].T

    return (
        output,
        grad_input,
        summed_w_qkv,
        summed_bias_qv,
        summed_w_out,
        summed[0],
        summed[1],
        summed[2],
        summed_w_in,
        summed_bias_in,
        summed_w_down,
        summed[3],
        summed[4],
        summed[5],
    )


def solution(mesh):
    dp_count = mesh.shape["dp"]

    def body(*args):
        return shards(dp_count, *args)

    return jax.shard_map(
        body,
        mesh=mesh,
        in_specs=(
            P("dp", None),
            P("dp", None),
            P(None, None, "tensor"),
            P(None, "tensor"),
            P("tensor", None),
            P(),
            P(),
            P(),
            P(None, "tensor"),
            P("tensor"),
            P("tensor", None),
            P(),
            P(),
            P(),
            P("dp", None),
        ),
        out_specs=(
            P("dp", None),
            P("dp", None),
            P(None, "dp", "tensor"),
            P(None, "tensor"),
            P("tensor", "dp"),
            P(),
            P(),
            P(),
            P("dp", "tensor"),
            P("tensor"),
            P("tensor", "dp"),
            P(),
            P(),
            P(),
        ),
        check_vma=False,
    )
```

```python
import functools
import math

import jax
import jax.numpy as jnp
from jax import lax
from jax.experimental import pallas as pl
from jax.experimental.pallas import tpu as pltpu
from jax.sharding import PartitionSpec as P

HEAD_DIM = 64
PAIR = 2 * HEAD_DIM
LANES = 128


EPSILON = 1e-05
NEGATIVE = -1e30
ROOT_HALF = 0.7071067811865476
ROOT_PI_INV = 0.5641895835477563
MINUS_LOG2_E = -1.4426950408889634
F32 = jnp.float32
BF16 = jnp.bfloat16
NT = (((1,), (1,)), ((), ()))
NN = (((1,), (0,)), ((), ()))
CHUNK = 512
sd = jax.ShapeDtypeStruct


def dot(left, right, dims=NN):
    return lax.dot_general(left, right, dims, preferred_element_type=F32)


def mean_of(value):
    return jnp.sum(value, axis=1, keepdims=True) * (1.0 / value.shape[1])


def norm_forward(summed):
    centered = summed - mean_of(summed)
    inv_std = lax.rsqrt(mean_of(centered * centered) + EPSILON)
    return (centered * inv_std, inv_std)


def norm_backward(upstream, normed, inv_std, gain_vec):
    scaled_grad = upstream * gain_vec
    second_mean = mean_of(scaled_grad * normed)
    return inv_std * (scaled_grad - mean_of(scaled_grad) - normed * second_mean)


def gelu_pair(preact):
    scaled = preact * ROOT_HALF
    cumulative = 0.5 + 0.5 * lax.erf(scaled)
    bell = jnp.exp2(scaled * scaled * MINUS_LOG2_E)
    derivative = cumulative + scaled * bell * ROOT_PI_INV
    return (preact * cumulative, derivative)


def column_sum(value):
    return jnp.sum(value, axis=0, keepdims=True)


def rows_spec(n, c):
    return pl.BlockSpec((n, c), lambda i, s: (i, 0))


def side_spec(n, c, steps):
    return pl.BlockSpec((n, c), lambda i, s: (s[0] * steps + i, 0))


def fixed_spec(shape):
    return pl.BlockSpec(shape, lambda i, s: (0,) * len(shape), pipeline_mode=pl.Buffered(1))


def call(kernel, name, grid, in_specs, out_specs, out_shape, scratch, cost, limit=56):
    flops, moved, transcendentals = cost
    return pl.pallas_call(
        kernel,
        grid_spec=pltpu.PrefetchScalarGridSpec(
            num_scalar_prefetch=1,
            grid=grid,
            in_specs=in_specs,
            out_specs=out_specs,
            scratch_shapes=scratch,
        ),
        out_shape=out_shape,
        compiler_params=pltpu.CompilerParams(vmem_limit_bytes=limit * 1024 * 1024),
        cost_estimate=pl.CostEstimate(
            flops=flops, bytes_accessed=moved, transcendentals=transcendentals
        ),
        name=name,
    )


def put_transposed(out_ref, value, scratch, me, masks):
    scratch[...] = value.T.reshape(scratch.shape)
    if len(masks) == 1:
        out_ref[...] = scratch[...]
    else:
        for j, mask in enumerate(masks):
            out_ref[j] = scratch[me ^ mask]


def page_columns(page):
    line = lax.broadcasted_iota(jnp.int32, (LANES, page.shape[1]), 0)
    same = jnp.where(line == page, 1.0, 0.0).T
    lane = lax.broadcasted_iota(jnp.int32, same.shape, 1)
    pen = jnp.where((lane < 4) & (same == 0.0), NEGATIVE, 0.0)
    return (pen.astype(BF16), same.astype(BF16))


def attend_kernel(
    scalars, tok_ref, seg_ref, wq_ref, bq_ref, wo_ref, q_ref, k_ref, v_ref, p_ref, c_ref, part_ref
):
    row = scalars[0] * pl.num_programs(0) + pl.program_id(0)
    pen, hot = page_columns(seg_ref[pl.ds(row, 1), :])
    tok = tok_ref[...]
    scale = 1.0 / math.sqrt(HEAD_DIM)
    bias = bq_ref[...].astype(F32)
    q_ref[...] = ((dot(tok, wq_ref[0]) + bias[0:1]).astype(BF16) * scale).astype(BF16)
    k_ref[...] = dot(tok, wq_ref[1]).astype(BF16)
    v_ref[...] = (dot(tok, wq_ref[2]) + bias[1:2]).astype(BF16)
    rows, cols = q_ref.shape
    lane = lax.broadcasted_iota(jnp.int32, (rows, PAIR), 1)
    zero = jnp.zeros((rows, PAIR), BF16)
    for pair in range(cols // PAIR):
        at = pl.ds(pair * PAIR, PAIR)
        q = q_ref[:, at]
        v = v_ref[:, at]
        k_wide = jnp.concatenate([k_ref[:, at], hot], axis=1)
        outs = []
        for half in range(2):
            mine = (lane < HEAD_DIM) if half == 0 else (lane >= HEAD_DIM)
            q_wide = jnp.concatenate([jnp.where(mine, q, zero), pen], axis=1)
            scores = dot(q_wide, k_wide, NT)
            top = jnp.max(scores, axis=1, keepdims=True)
            exp_scores = jnp.exp(scores - top)
            total = jnp.sum(exp_scores, axis=1, keepdims=True)
            probs = (exp_scores * (1.0 / total)).astype(BF16)
            p_ref[0, pair * 2 + half] = probs
            outs.append(dot(probs, v))
        c_ref[:, at] = jnp.where(lane < HEAD_DIM, outs[0], outs[1]).astype(BF16)
    part_ref[...] = dot(c_ref[...], wo_ref[...]).astype(BF16)


def attend(scalars, tok, seg, wq, bq, wo):
    width = tok.shape[1]
    seqs = seg.shape[0] // 2
    n = seg.shape[1]
    rows = seqs * n
    cols = wq.shape[2]
    heads = cols // HEAD_DIM
    return call(
        attend_kernel,
        "attend",
        (seqs,),
        [
            side_spec(n, width, seqs),
            fixed_spec(seg.shape),
            fixed_spec(wq.shape),
            fixed_spec(bq.shape),
            fixed_spec(wo.shape),
        ],
        [rows_spec(n, cols)] * 3
        + [
            pl.BlockSpec((1, heads, n, n), lambda i, s: (i, 0, 0, 0)),
            rows_spec(n, cols),
            rows_spec(n, width),
        ],
        [sd((rows, cols), BF16)] * 3
        + [sd((seqs, heads, n, n), BF16), sd((rows, cols), BF16), sd((rows, width), BF16)],
        [],
        (
            8 * rows * width * cols + 12 * rows * n * cols,
            2 * (rows * n * heads + 7 * rows * cols + 4 * width * cols),
            rows * n * heads,
        ),
    )(scalars, tok, seg, wq, bq, wo)


def part_of(main, rest, start):
    most = main.shape[1]
    return (main, start) if start < most else (rest, start - most)


def mlp_kernel(
    masks, scalars, tok_ref, pa_ref, pb_ref, up_ref, vec_ref, ba_ref, bb_ref,
    wia_hbm, wib_hbm, wda_hbm, wdb_hbm,
    out_ref, mine_ref, g2t_ref, lowt_ref, g1t_ref, tokt_ref, ha_ref, hb_ref, gpa_ref, gpb_ref,
    ha_rest, hb_rest, gpa_rest, gpb_rest, g1_ref, g1low_ref,
    sumsa_ref, sumsb_ref,
    wia, wib, wda, wdb, dv_ref, low_ref, g2low_ref, turn, sem,
):
    step = pl.program_id(0)
    pairs = ((wia_hbm, wia), (wib_hbm, wib), (wda_hbm, wda), (wdb_hbm, wdb))
    copies = [pltpu.make_async_copy(s, d, sem.at[i]) for i, (s, d) in enumerate(pairs)]

    def tile(first):
        def arrive(i):
            if first:
                copies[i].wait()

        vec = vec_ref[...].astype(F32)
        bias_out, gain1, shift1, bias_down, gain2, shift2 = [vec[i : i + 1] for i in range(6)]
        attention = pa_ref[...].astype(F32) + pb_ref[...].astype(F32)
        normed1, inv1 = norm_forward(tok_ref[...].astype(F32) + attention + bias_out)
        normed_one = normed1 * gain1 + shift1
        low_ref[...] = normed_one.astype(BF16)
        f = wia.shape[1]
        for k, (wi, bi) in enumerate(((wia, ba_ref), (wib, bb_ref))):
            arrive(k)
            for c in range(0, f, CHUNK):
                preact = dot(low_ref[...], wi[:, c : c + CHUNK]) + bi[:, c : c + CHUNK].astype(F32)
                hidden, derivative = gelu_pair(preact)
                at = k * f + c
                h_ref, spot = part_of((ha_ref, hb_ref)[k], (ha_rest, hb_rest)[k], c)
                h_ref[:, spot : spot + CHUNK] = hidden.astype(BF16)
                dv_ref[:, at : at + CHUNK] = derivative.astype(BF16)
        put_transposed(lowt_ref, low_ref[...], turn, scalars[1], masks[1])
        put_transposed(tokt_ref, tok_ref[...], turn, scalars[1], masks[3])
        parts = []
        for k, (wd, h_ref, h_rest) in enumerate(((wda, ha_ref, ha_rest), (wdb, hb_ref, hb_rest))):
            arrive(2 + k)
            most = h_ref.shape[1]
            part = dot(jnp.concatenate([h_ref[...], h_rest[...]], axis=1), wd[...])
            parts.append(part.astype(BF16).astype(F32))
        normed2, inv2 = norm_forward(normed_one + (parts[0] + parts[1]) + bias_down)
        mine_ref[...] = (normed2 * gain2 + shift2).astype(BF16)
        out_ref[...] = mine_ref[...]
        up = up_ref[...].astype(F32)
        g2 = norm_backward(up, normed2, inv2, gain2)
        g2low_ref[...] = g2.astype(BF16)
        stats = [column_sum(g2), column_sum(up * normed2), column_sum(up)]
        put_transposed(g2t_ref, g2low_ref[...], turn, scalars[1], masks[0])
        sums = []
        for k, wd in enumerate((wda, wdb)):
            for c in range(0, f, CHUNK):
                at = k * f + c
                grad_hidden = dot(g2low_ref[...], wd[c : c + CHUNK, :], NT)
                grad_preact = (grad_hidden * dv_ref[:, at : at + CHUNK].astype(F32)).astype(BF16)
                gp_ref, spot = part_of((gpa_ref, gpb_ref)[k], (gpa_rest, gpb_rest)[k], c)
                gp_ref[:, spot : spot + CHUNK] = grad_preact
                sums.append(column_sum(grad_preact.astype(F32)))
        parts = []
        for wi, gp_ref, gp_rest in ((wia, gpa_ref, gpa_rest), (wib, gpb_ref, gpb_rest)):
            most = gp_ref.shape[1]
            part = dot(jnp.concatenate([gp_ref[...], gp_rest[...]], axis=1), wi[...], NT)
            parts.append(part.astype(BF16).astype(F32))
        grad = g2 + (parts[0] + parts[1])
        g1 = norm_backward(grad, normed1, inv1, gain1)
        g1_ref[...] = g1
        g1low_ref[...] = g1.astype(BF16)
        put_transposed(g1t_ref, g1low_ref[...], turn, scalars[1], masks[2])
        stats = [column_sum(g1), column_sum(grad * normed1), column_sum(grad)] + stats
        width = g1.shape[1]
        lines = [
            jnp.concatenate(s, axis=1)
            for s in (sums[: f // CHUNK], sums[f // CHUNK :])
        ]
        for line, sums_ref in zip(lines, (sumsa_ref, sumsb_ref)):
            block = [line[:, c : c + width] for c in range(0, f, width)] + stats
            block = jnp.concatenate(block, axis=0)
            sums_ref[...] = block if first else sums_ref[...] + block

    @pl.when(step == 0)
    def _():
        for copy in copies:
            copy.start()
        tile(True)

    @pl.when(step > 0)
    def _():
        tile(False)


def mlp(scalars, tok, pa, pb, up, vec, ba, bb, wia, wib, wda, wdb, tile, orders):
    rows, width = pa.shape
    f = wia.shape[1]
    steps = rows // tile
    hbm = pl.BlockSpec(memory_space=pl.ANY)
    tok_spec = rows_spec(tile, width)
    mine_spec = side_spec(tile, width, steps)
    masks = [order_blocks(width, order)[0] for order in orders]
    shape = order_blocks(width, orders[0])[1]
    lines = f // width + 6
    most = f // CHUNK * 2 // 3 * CHUNK
    return call(
        functools.partial(mlp_kernel, masks),
        "mlp",
        (steps,),
        [mine_spec, tok_spec, tok_spec, mine_spec]
        + [fixed_spec(vec.shape), fixed_spec(ba.shape), fixed_spec(bb.shape)]
        + [hbm] * 4,
        [mine_spec, tok_spec]
        + [transposed_spec(shape, tile)] * 4
        + [rows_spec(tile, most)] * 4
        + [rows_spec(tile, f - most)] * 4
        + [tok_spec] * 2
        + [fixed_spec((lines, width))] * 2,
        [sd((2 * rows, width), BF16), sd((rows, width), BF16)]
        + [sd(shape + (rows,), BF16)] * 4
        + [sd((rows, most), BF16)] * 4
        + [sd((rows, f - most), BF16)] * 4
        + [sd((rows, width), F32), sd((rows, width), BF16)]
        + [sd((lines, width), F32)] * 2,
        [pltpu.VMEM((width, f), BF16)] * 2
        + [pltpu.VMEM((f, width), BF16)] * 2
        + [pltpu.VMEM((tile, 2 * f), BF16)]
        + [pltpu.VMEM((tile, width), BF16)] * 2
        + [pltpu.VMEM(shape + (tile,), BF16), pltpu.SemaphoreType.DMA((4,))],
        (16 * rows * width * f, 8 * width * f + 30 * rows * width + 8 * rows * f, 4 * rows * f),
        60,
    )(scalars, tok, pa, pb, up, vec, ba, bb, wia, wib, wda, wdb)


class Order:
    def __init__(self, count):
        self.count = count
        self.bits = list(range(count.bit_length() - 1))

    def masks(self):
        return [mask_of(self.bits, j) for j in range(self.count)]


def mask_of(bits, j):
    size = len(bits)
    return sum(((j >> (size - 1 - k)) & 1) << bit for k, bit in enumerate(bits))


def order_blocks(width, order):
    if (width // order.count) % 16 == 0:
        return (order.masks(), (order.count, width // order.count))
    return ([0], (1, width))


def transposed_spec(shape, n):
    return pl.BlockSpec(shape + (n,), lambda i, s: (0, 0, i))


def in_order(grad, order):
    rows, cols = grad.shape
    if len(order_blocks(rows, order)[0]) > 1:
        return grad.reshape(order.count, rows // order.count, cols)
    total = len(order.bits)
    index = lax.axis_index("dp")
    view = grad.reshape((2,) * total + (rows // order.count, cols))
    for bit in range(total):
        axis = total - 1 - bit
        view = jnp.where(((index >> bit) & 1) == 1, jnp.flip(view, axis), view)
    axes = [total - 1 - bit for bit in order.bits]
    view = jnp.transpose(view, axes + [total, total + 1])
    return view.reshape(order.count, rows // order.count, cols)


def swap_pair(value):
    return lax.ppermute(value, "tensor", [(0, 1), (1, 0)])


def swap_bits(value, count, mask):
    return lax.ppermute(value, "dp", [(i, i ^ mask) for i in range(count)])


def total_of(terms):
    total = terms[0].astype(F32)
    for term in terms[1:]:
        total = total + term.astype(F32)
    return total


class RowScatter:
    def __init__(self, terms, order, stages):
        self.count = order.count
        self.left = list(order.bits)
        self.terms = list(terms)
        self.marks = [tuple(order.bits)] * len(terms)
        stages = [[bit for bit in stage if bit in self.left] for stage in stages]
        used = [bit for stage in stages for bit in stage]
        stages = stages + [[bit] for bit in self.left if bit not in used]
        self.stages = [stage for stage in stages if stage]
        self.pending = []

    def pick(self, chosen):
        total = 0.0
        for term, bits in zip(self.terms, self.marks):
            view = term.reshape((2,) * len(bits) + term.shape[1:])
            at = tuple(chosen.get(bit, slice(None) if bit in self.left else 0) for bit in bits)
            total = total + view[at].reshape((-1,) + term.shape[1:]).astype(F32)
        return total

    def sums(self):
        bits = self.stages.pop(0)
        away, masks = [], []
        for j in range(1, 1 << len(bits)):
            masks.append(mask_of(bits, j))
            chosen = {bit: (masks[-1] >> bit) & 1 for bit in bits}
            away.append(self.pick(chosen).astype(BF16))
        self.left = [bit for bit in self.left if bit not in bits]
        return (away, masks)

    def send(self):
        self.away, masks = self.sums()
        self.pending = [swap_bits(away, self.count, mask) for away, mask in zip(self.away, masks)]

    def take(self, received):
        self.terms = self.terms + list(received)
        self.marks = self.marks + [tuple(self.left)] * len(received)

    def add(self):
        self.take(self.pending)
        self.pending = []

    def own(self):
        return self.pick({})[0]

    def more(self):
        return bool(self.stages)


class JointScatter:
    def __init__(self, *chains):
        self.chains = chains
        self.pending = []

    def send(self):
        stages = [chain.sums() for chain in self.chains]
        masks = stages[0][1]
        self.away = [jnp.stack(two) for two in zip(*[away for away, _ in stages])]
        count = self.chains[0].count
        self.pending = [swap_bits(away, count, mask) for away, mask in zip(self.away, masks)]

    def more(self):
        return bool(self.chains[0].stages)

    def add(self):
        for at, chain in enumerate(self.chains):
            chain.take([m[at] for m in self.pending])
        self.pending = []


class SumAll:
    def __init__(self, value, count, bits):
        self.value = value
        self.count = count
        total = count.bit_length() - 1
        bits = [bit for bit in bits if bit < total]
        self.bits = bits + [bit for bit in range(total) if bit not in bits]

    def send(self):
        self.pending = swap_bits(self.value, self.count, 1 << self.bits.pop(0))

    def add(self):
        self.value = self.value + self.pending

    def finish(self):
        self.add()
        while self.bits:
            self.send()
            self.add()
        return self.value


def fence(*values):
    return lax.optimization_barrier(values)


def attend_back_kernel(
    scalars, g_ref, gt_ref, tokt_ref, q_all, k_all, v_all, p_all, c_all, wo_ref, sums_ref, *rest,
):
    wq_ref = rest[0] if len(rest) == 7 else None
    first_ref, lines_ref, grada_ref, gradb_ref, acc_ref = rest[1:6] if wq_ref is not None else rest
    d_ref = rest[6] if wq_ref is not None else first_ref
    step = pl.program_id(0)
    q_ref, k_ref, v_ref, p_ref, c_ref = [ref.at[step] for ref in (q_all, k_all, v_all, p_all, c_all)]
    rows, cols = q_ref.shape
    scale = 1.0 / math.sqrt(HEAD_DIM)
    grad_context = dot(g_ref[...], wo_ref[...], NT).astype(BF16)
    lane = lax.broadcasted_iota(jnp.int32, (rows, PAIR), 1)
    low = lane < HEAD_DIM
    zero = jnp.zeros((rows, PAIR), BF16)
    for pair in range(cols // PAIR):
        lo = pair * PAIR
        at = pl.ds(lo, PAIR)
        q = q_ref[:, at]
        v = v_ref[:, at]
        k = k_ref[:, at]
        do = grad_context[:, lo : lo + PAIR]
        product = do.astype(F32) * c_ref[:, at].astype(F32)
        q_t = q.T
        do_t = do.T
        grads_q, grads_k, grads_v = [], [], []
        for half in range(2):
            mine = low if half == 0 else lane >= HEAD_DIM
            row_dot = jnp.sum(jnp.where(mine, product, 0.0), axis=1, keepdims=True)
            probs = p_ref[pair * 2 + half]
            grad_probs = dot(jnp.where(mine, do, zero), v, NT)
            grad_scores = (probs.astype(F32) * (grad_probs - row_dot)).astype(BF16)
            grads_q.append(dot(grad_scores, k))
            own = slice(half * HEAD_DIM, (half + 1) * HEAD_DIM)
            grads_k.append(dot(q_t[own], grad_scores))
            grads_v.append(dot(do_t[own], probs))
        d_ref[0, :, at] = (jnp.where(low, grads_q[0], grads_q[1]) * scale).astype(BF16)
        d_ref[1, :, at] = jnp.concatenate(grads_k, axis=0).T.astype(BF16)
        d_ref[2, :, at] = jnp.concatenate(grads_v, axis=0).T.astype(BF16)
    if wq_ref is not None:
        first_ref[...] = input_part(d_ref, wq_ref).astype(BF16)
    tok_t = tokt_ref[...].reshape(-1, rows)
    g_t = gt_ref[...].reshape(-1, rows)
    new = [dot(tok_t, d_ref[j]) for j in range(3)] + [dot(g_t, c_ref[...])]
    bias = [column_sum(d_ref[j].astype(F32)) for j in (0, 2)]
    lines = sums_ref.shape[0]
    spots = [(slice(lines, lines + 1), slice(j * cols, (j + 1) * cols)) for j in range(2)]

    @pl.when(step == 0)
    def _():
        lines_ref[...] = jnp.zeros(lines_ref.shape, F32)
        lines_ref[:lines] = sums_ref[...]
        for j in range(4):
            acc_ref[j] = new[j]
        for spot, line in zip(spots, bias):
            lines_ref[spot] = line

    @pl.when(step > 0)
    def _():
        for j in range(4):
            acc_ref[j] = acc_ref[j] + new[j]
        for spot, line in zip(spots, bias):
            lines_ref[spot] = lines_ref[spot] + line

    @pl.when(step == pl.num_programs(0) - 1)
    def _():
        for j, grad_ref in enumerate((grada_ref, grada_ref, gradb_ref, gradb_ref)):
            at = (j % 2) * cols
            grad_ref[:, at : at + cols] = acc_ref[j].astype(BF16)


def attend_back(scalars, g, g_t, tok_t, q, k, v, p, c, wo, sums, wq=None):
    rows, width = g.shape
    seqs, heads, n, _ = p.shape
    cols = q.shape[1]
    q, k, v, c = [m.reshape(seqs, n, cols) for m in (q, k, v, c)]
    turned = transposed_spec(g_t.shape[:2], n)
    extra = () if wq is None else (wq,)
    if wq is None:
        first_spec = pl.BlockSpec((3, n, cols), lambda i, s: (0, i, 0))
        first_shape = (3, rows, cols)
    else:
        first_spec = rows_spec(n, width)
        first_shape = (rows, width)
    return call(
        attend_back_kernel,
        "attend_back",
        (seqs,),
        [rows_spec(n, width), turned, turned]
        + [pl.BlockSpec(memory_space=pltpu.VMEM)] * 5
        + [
            fixed_spec(wo.shape),
            fixed_spec(sums.shape),
        ]
        + [fixed_spec(w.shape) for w in extra],
        [first_spec, fixed_spec((16, 2 * cols))] + [fixed_spec((width, 2 * cols))] * 2,
        [sd(first_shape, BF16), sd((16, 2 * cols), F32)] + [sd((width, 2 * cols), BF16)] * 2,
        [pltpu.VMEM((4, width, cols), F32)] + [pltpu.VMEM((3, n, cols), BF16)] * len(extra),
        (
            (10 + 6 * len(extra)) * rows * width * cols + 16 * rows * n * cols,
            2 * (rows * n * heads + 8 * rows * cols + 8 * width * cols),
            0,
        ),
        25 + 7 * len(extra),
    )(scalars, g, g_t, tok_t, q, k, v, p, c, wo, sums, *extra)


def input_part(d_ref, w_ref):
    return dot(d_ref[0], w_ref[0], NT) + dot(d_ref[1], w_ref[1], NT) + dot(d_ref[2], w_ref[2], NT)


def input_grad_kernel(scalars, g1_ref, part_ref, d_ref, w_ref, whole_ref, mine_ref):
    own = input_part(d_ref, w_ref).astype(BF16).astype(F32)
    mine_ref[...] = (g1_ref[...] + (own + part_ref[...].astype(F32))).astype(BF16)
    whole_ref[...] = mine_ref[...]


def input_grad(scalars, g1, part, d, w, tile):
    rows, width = g1.shape
    cols = d.shape[2]
    steps = rows // tile
    tok_spec = rows_spec(tile, width)
    return call(
        input_grad_kernel,
        "input_grad",
        (steps,),
        [tok_spec, tok_spec, pl.BlockSpec((3, tile, cols), lambda i, s: (0, i, 0)), fixed_spec(w.shape)],
        [side_spec(tile, width, steps), tok_spec],
        [sd((2 * rows, width), BF16), sd((rows, width), BF16)],
        [],
        (6 * rows * width * cols, 10 * rows * width + 6 * rows * cols + 6 * width * cols, 0),
        32,
    )(scalars, g1, part, d, w)


def shards(
    dp_count,
    tokens_in,
    segment_ids,
    w_qkv,
    bias_qv,
    w_out,
    bias_out,
    norm1_gain,
    norm1_shift,
    w_in,
    bias_in,
    w_down,
    bias_down,
    norm2_gain,
    norm2_shift,
    grad_output,
):
    seq_count, seq_length = segment_ids.shape
    half_seqs = seq_count // 2
    rows = half_seqs * seq_length
    width = tokens_in.shape[1]
    local_cols = w_qkv.shape[2]
    f = w_in.shape[1]
    side = lax.axis_index("tensor")
    scalars = jnp.stack([side, lax.axis_index("dp")]).astype(jnp.int32)
    order = Order(dp_count)

    vec = jnp.stack([bias_out, norm1_gain, norm1_shift, bias_down, norm2_gain, norm2_shift])
    bias_line = bias_in.reshape(1, f)
    others = [swap_pair(w) for w in (w_qkv, w_out, w_in, w_down)]
    *kept, part = attend(scalars, tokens_in, segment_ids, w_qkv, bias_qv, w_out)
    part, bias_qv, bias_line = fence(part, bias_qv, bias_line)
    bias_others = [swap_pair(w) for w in (bias_qv, bias_line)]
    saved, parts = [kept], [part]
    others = [others[0], bias_others[0], others[1], others[2], bias_others[1], others[3]]
    w_qkv_two, bias_qv_two, w_out_two, w_in_two, bias_in_two, w_down_two = [
        (own, other)
        for own, other in zip(
            (w_qkv, bias_qv, w_out, w_in, bias_line, w_down), others
        )
    ]
    *kept, part = attend(scalars, tokens_in, segment_ids, w_qkv_two[1], bias_qv_two[1], w_out_two[1])
    saved.append(kept)
    parts.append(part)
    output, output_mine, g2_t, low_t, g1_t, tok_t, *columns, g1, g1low, sums_own, sums_other = mlp(
        scalars, tokens_in, *parts, grad_output, vec,
        *bias_in_two, *w_in_two, *w_down_two, 256, (order,) * 4,
    )

    def whole(full, other):
        return lax.dynamic_update_slice_in_dim(full, other, (1 - side) * rows, 0)

    def outer(left, right):
        return dot(left.reshape(width, rows), right).astype(BF16)

    lefts = (g2_t, g2_t, low_t, low_t)
    other_grads = [[swap_pair(outer(lefts[at], part[at])) for at in (1, 3)] for part in (columns[:4], columns[4:])]
    own_grads = [[outer(lefts[at], part[at]) for at in (0, 2)] for part in (columns[:4], columns[4:])]
    output_recv = swap_pair(output_mine)
    g1low, own_grads, other_grads = fence(g1low, own_grads, other_grads)

    def chain_of(part, at, *stages):
        return RowScatter([in_order(m[part][at], order) for m in (own_grads, other_grads)], order, stages)

    down = chain_of(0, 0, (0,), (1,), (2,), (3,))
    inner = chain_of(0, 1, (1,), (3,), (2,), (0,))
    down_rest, in_rest = [chain_of(1, at, (2,), (0,), (3,), (1,)) for at in (0, 1)]
    pair_rest = JointScatter(down_rest, in_rest)

    def back(at, g, *rest):
        return attend_back(scalars, g, g1_t, tok_t, *saved[at], w_out_two[at], *rest)

    down.send()
    inner.send()
    pair_rest.send()
    part_other, lines_other, *grads_other = back(1, g1low, sums_other, w_qkv_two[1])
    part_other, lines_other, grads_other, down.pending, inner.pending, pair_rest.pending, output_recv = fence(
        part_other, lines_other, grads_other, down.pending, inner.pending, pair_rest.pending, output_recv
    )
    grads_recv = [swap_pair(grad) for grad in grads_other]
    lines_recv = swap_pair(lines_other)

    def next_stage():
        for chain in (down, inner, pair_rest):
            chain.add()
        for chain in (down, inner, pair_rest):
            chain.send()

    next_stage()
    g1low, part_other = fence(g1low, part_other)
    d_own, lines_own, *grads_own = back(0, g1low, sums_own)
    d_own, lines_own, grads_own, grads_recv, lines_recv, down.pending, inner.pending, pair_rest.pending = fence(
        d_own, lines_own, grads_own, grads_recv, lines_recv, down.pending, inner.pending, pair_rest.pending
    )
    last = [order.bits[2:4]] if dp_count <= 16 else []
    head_a, head_b = [
        RowScatter([in_order(m, order) for m in terms], order, [[first], [1 - first]] + last)
        for first, terms in enumerate(zip(grads_own, grads_recv))
    ]
    lines = SumAll(lines_own + lines_recv, dp_count, (0, 3, 2, 1))
    lines.send()
    head_a.send()
    head_b.send()
    head_a.away, head_b.away, down.pending, inner.pending, pair_rest.pending = fence(
        head_a.away, head_b.away, down.pending, inner.pending, pair_rest.pending
    )
    next_stage()
    d_own, lines.pending = fence(d_own, lines.pending)
    grad_input, grad_mine = input_grad(scalars, g1, part_other, d_own, w_qkv, 256)
    grad_input, grad_mine, head_a.pending, head_b.pending, lines.pending, output_recv = fence(
        grad_input, grad_mine, head_a.pending, head_b.pending, lines.pending, output_recv
    )
    lines.add()
    lines.send()
    head_a.add()
    head_b.add()
    head_a.send()
    head_b.send()
    head_a.away, head_b.away, down.pending, inner.pending, pair_rest.pending, output_recv, grad_mine = fence(
        head_a.away, head_b.away, down.pending, inner.pending, pair_rest.pending, output_recv, grad_mine
    )
    next_stage()
    grad_recv = swap_pair(grad_mine)
    output = whole(output, output_recv)
    output, head_a.pending, head_b.pending, lines.pending, grad_recv = fence(
        output, head_a.pending, head_b.pending, lines.pending, grad_recv
    )
    head_a.add()
    head_b.add()
    lines.add()
    lines.send()
    heads = JointScatter(head_a, head_b)
    heads.send()
    heads.away, down.pending, inner.pending, pair_rest.pending, grad_recv, lines.pending = fence(
        heads.away, down.pending, inner.pending, pair_rest.pending, grad_recv, lines.pending
    )
    lines.add()
    lines.send()
    for chain in (down, inner, pair_rest):
        chain.add()
        while chain.more():
            chain.send()
            chain.add()
    grad_input = whole(grad_input, grad_recv)
    summed_w_down = jnp.concatenate([down.own(), down_rest.own()], axis=1).T
    summed_w_in = jnp.concatenate([inner.own(), in_rest.own()], axis=1)
    grad_input, summed_w_down, summed_w_in, heads.pending, lines.pending = fence(
        grad_input, summed_w_down, summed_w_in, heads.pending, lines.pending
    )
    heads.add()
    while heads.more():
        heads.send()
        heads.add()
    total = lines.finish()
    at_stats = sums_own.shape[0] - 6
    summed_bias_in = total[:at_stats].reshape(f)
    summed = [total[at_stats + i] for i in range(6)]
    summed_bias_qv = total[at_stats + 6].reshape(2, local_cols)
    summed_a, summed_b = head_a.own(), head_b.own()
    summed_w_qkv = jnp.stack([summed_a[:, :local_cols], summed_a[:, local_cols:], summed_b[:, :local_cols]])
    summed_w_out = summed_b[:, local_cols:].T

    return (
        output,
        grad_input,
        summed_w_qkv,
        summed_bias_qv,
        summed_w_out,
        summed[0],
        summed[1],
        summed[2],
        summed_w_in,
        summed_bias_in,
        summed_w_down,
        summed[3],
        summed[4],
        summed[5],
    )


def solution(mesh):
    dp_count = mesh.shape["dp"]

    def body(*args):
        return shards(dp_count, *args)

    return jax.shard_map(
        body,
        mesh=mesh,
        in_specs=(
            P("dp", None),
            P("dp", None),
            P(None, None, "tensor"),
            P(None, "tensor"),
            P("tensor", None),
            P(),
            P(),
            P(),
            P(None, "tensor"),
            P("tensor"),
            P("tensor", None),
            P(),
            P(),
            P(),
            P("dp", None),
        ),
        out_specs=(
            P("dp", None),
            P("dp", None),
            P(None, "dp", "tensor"),
            P(None, "tensor"),
            P("tensor", "dp"),
            P(),
            P(),
            P(),
            P("dp", "tensor"),
            P("tensor"),
            P("tensor", "dp"),
            P(),
            P(),
            P(),
        ),
        check_vma=False,
    )
```

```python
import functools
import math

import jax
import jax.numpy as jnp
from jax import lax
from jax.experimental import pallas as pl
from jax.experimental.pallas import tpu as pltpu
from jax.sharding import PartitionSpec as P

HEAD_DIM = 64
PAIR = 2 * HEAD_DIM
LANES = 128


EPSILON = 1e-05
NEGATIVE = -1e30
ROOT_HALF = 0.7071067811865476
ROOT_PI_INV = 0.5641895835477563
MINUS_LOG2_E = -1.4426950408889634
F32 = jnp.float32
BF16 = jnp.bfloat16
NT = (((1,), (1,)), ((), ()))
NN = (((1,), (0,)), ((), ()))
CHUNK = 512
sd = jax.ShapeDtypeStruct


def dot(left, right, dims=NN):
    return lax.dot_general(left, right, dims, preferred_element_type=F32)


def mean_of(value):
    return jnp.sum(value, axis=1, keepdims=True) * (1.0 / value.shape[1])


def norm_forward(summed):
    centered = summed - mean_of(summed)
    inv_std = lax.rsqrt(mean_of(centered * centered) + EPSILON)
    return (centered * inv_std, inv_std)


def norm_backward(upstream, normed, inv_std, gain_vec):
    scaled_grad = upstream * gain_vec
    second_mean = mean_of(scaled_grad * normed)
    return inv_std * (scaled_grad - mean_of(scaled_grad) - normed * second_mean)


def gelu_pair(preact):
    scaled = preact * ROOT_HALF
    cumulative = 0.5 + 0.5 * lax.erf(scaled)
    bell = jnp.exp2(scaled * scaled * MINUS_LOG2_E)
    derivative = cumulative + scaled * bell * ROOT_PI_INV
    return (preact * cumulative, derivative)


def column_sum(value):
    return jnp.sum(value, axis=0, keepdims=True)


def rows_spec(n, c):
    return pl.BlockSpec((n, c), lambda i, s: (i, 0))


def side_spec(n, c, steps):
    return pl.BlockSpec((n, c), lambda i, s: (s[0] * steps + i, 0))


def fixed_spec(shape):
    return pl.BlockSpec(shape, lambda i, s: (0,) * len(shape), pipeline_mode=pl.Buffered(1))


def call(kernel, name, grid, in_specs, out_specs, out_shape, scratch, cost, limit=56):
    flops, moved, transcendentals = cost
    return pl.pallas_call(
        kernel,
        grid_spec=pltpu.PrefetchScalarGridSpec(
            num_scalar_prefetch=1,
            grid=grid,
            in_specs=in_specs,
            out_specs=out_specs,
            scratch_shapes=scratch,
        ),
        out_shape=out_shape,
        compiler_params=pltpu.CompilerParams(vmem_limit_bytes=limit * 1024 * 1024),
        cost_estimate=pl.CostEstimate(
            flops=flops, bytes_accessed=moved, transcendentals=transcendentals
        ),
        name=name,
    )


def put_transposed(out_ref, value, scratch, me, masks):
    scratch[...] = value.T.reshape(scratch.shape)
    if len(masks) == 1:
        out_ref[...] = scratch[...]
    else:
        for j, mask in enumerate(masks):
            out_ref[j] = scratch[me ^ mask]


def page_columns(page):
    line = lax.broadcasted_iota(jnp.int32, (LANES, page.shape[1]), 0)
    same = jnp.where(line == page, 1.0, 0.0).T
    lane = lax.broadcasted_iota(jnp.int32, same.shape, 1)
    pen = jnp.where((lane < 4) & (same == 0.0), NEGATIVE, 0.0)
    return (pen.astype(BF16), same.astype(BF16))


def attend_kernel(
    scalars, tok_ref, seg_ref, wq_ref, bq_ref, wo_ref, q_ref, k_ref, v_ref, p_ref, c_ref, part_ref
):
    row = scalars[0] * pl.num_programs(0) + pl.program_id(0)
    pen, hot = page_columns(seg_ref[pl.ds(row, 1), :])
    tok = tok_ref[...]
    scale = 1.0 / math.sqrt(HEAD_DIM)
    bias = bq_ref[...].astype(F32)
    q_ref[...] = ((dot(tok, wq_ref[0]) + bias[0:1]).astype(BF16) * scale).astype(BF16)
    k_ref[...] = dot(tok, wq_ref[1]).astype(BF16)
    v_ref[...] = (dot(tok, wq_ref[2]) + bias[1:2]).astype(BF16)
    rows, cols = q_ref.shape
    lane = lax.broadcasted_iota(jnp.int32, (rows, PAIR), 1)
    zero = jnp.zeros((rows, PAIR), BF16)
    for pair in range(cols // PAIR):
        at = pl.ds(pair * PAIR, PAIR)
        q = q_ref[:, at]
        v = v_ref[:, at]
        k_wide = jnp.concatenate([k_ref[:, at], hot], axis=1)
        outs = []
        for half in range(2):
            mine = (lane < HEAD_DIM) if half == 0 else (lane >= HEAD_DIM)
            q_wide = jnp.concatenate([jnp.where(mine, q, zero), pen], axis=1)
            scores = dot(q_wide, k_wide, NT)
            top = jnp.max(scores, axis=1, keepdims=True)
            exp_scores = jnp.exp(scores - top)
            total = jnp.sum(exp_scores, axis=1, keepdims=True)
            probs = (exp_scores * (1.0 / total)).astype(BF16)
            p_ref[0, pair * 2 + half] = probs
            outs.append(dot(probs, v))
        c_ref[:, at] = jnp.where(lane < HEAD_DIM, outs[0], outs[1]).astype(BF16)
    part_ref[...] = dot(c_ref[...], wo_ref[...]).astype(BF16)


def attend(scalars, tok, seg, wq, bq, wo):
    width = tok.shape[1]
    seqs = seg.shape[0] // 2
    n = seg.shape[1]
    rows = seqs * n
    cols = wq.shape[2]
    heads = cols // HEAD_DIM
    return call(
        attend_kernel,
        "attend",
        (seqs,),
        [
            side_spec(n, width, seqs),
            fixed_spec(seg.shape),
            fixed_spec(wq.shape),
            fixed_spec(bq.shape),
            fixed_spec(wo.shape),
        ],
        [rows_spec(n, cols)] * 3
        + [
            pl.BlockSpec((1, heads, n, n), lambda i, s: (i, 0, 0, 0)),
            rows_spec(n, cols),
            rows_spec(n, width),
        ],
        [sd((rows, cols), BF16)] * 3
        + [sd((seqs, heads, n, n), BF16), sd((rows, cols), BF16), sd((rows, width), BF16)],
        [],
        (
            8 * rows * width * cols + 12 * rows * n * cols,
            2 * (rows * n * heads + 7 * rows * cols + 4 * width * cols),
            rows * n * heads,
        ),
    )(scalars, tok, seg, wq, bq, wo)


def part_of(main, rest, start):
    most = main.shape[1]
    return (main, start) if start < most else (rest, start - most)


def mlp_kernel(
    masks, scalars, tok_ref, pa_ref, pb_ref, up_ref, vec_ref, ba_ref, bb_ref,
    wia_hbm, wib_hbm, wda_hbm, wdb_hbm,
    out_ref, mine_ref, g2t_ref, lowt_ref, g1t_ref, tokt_ref, ha_ref, hb_ref, gpa_ref, gpb_ref,
    ha_rest, hb_rest, gpa_rest, gpb_rest, g1_ref, g1low_ref,
    sumsa_ref, sumsb_ref,
    wia, wib, wda, wdb, dv_ref, low_ref, g2low_ref, turn, sem,
):
    step = pl.program_id(0)
    pairs = ((wia_hbm, wia), (wib_hbm, wib), (wda_hbm, wda), (wdb_hbm, wdb))
    copies = [pltpu.make_async_copy(s, d, sem.at[i]) for i, (s, d) in enumerate(pairs)]

    def tile(first):
        def arrive(i):
            if first:
                copies[i].wait()

        vec = vec_ref[...].astype(F32)
        bias_out, gain1, shift1, bias_down, gain2, shift2 = [vec[i : i + 1] for i in range(6)]
        attention = pa_ref[...].astype(F32) + pb_ref[...].astype(F32)
        normed1, inv1 = norm_forward(tok_ref[...].astype(F32) + attention + bias_out)
        normed_one = normed1 * gain1 + shift1
        low_ref[...] = normed_one.astype(BF16)
        f = wia.shape[1]
        for k, (wi, bi) in enumerate(((wia, ba_ref), (wib, bb_ref))):
            arrive(k)
            for c in range(0, f, CHUNK):
                preact = dot(low_ref[...], wi[:, c : c + CHUNK]) + bi[:, c : c + CHUNK].astype(F32)
                hidden, derivative = gelu_pair(preact)
                at = k * f + c
                h_ref, spot = part_of((ha_ref, hb_ref)[k], (ha_rest, hb_rest)[k], c)
                h_ref[:, spot : spot + CHUNK] = hidden.astype(BF16)
                dv_ref[:, at : at + CHUNK] = derivative.astype(BF16)
        put_transposed(lowt_ref, low_ref[...], turn, scalars[1], masks[1])
        put_transposed(tokt_ref, tok_ref[...], turn, scalars[1], masks[3])
        parts = []
        for k, (wd, h_ref, h_rest) in enumerate(((wda, ha_ref, ha_rest), (wdb, hb_ref, hb_rest))):
            arrive(2 + k)
            most = h_ref.shape[1]
            part = dot(jnp.concatenate([h_ref[...], h_rest[...]], axis=1), wd[...])
            parts.append(part.astype(BF16).astype(F32))
        normed2, inv2 = norm_forward(normed_one + (parts[0] + parts[1]) + bias_down)
        mine_ref[...] = (normed2 * gain2 + shift2).astype(BF16)
        out_ref[...] = mine_ref[...]
        up = up_ref[...].astype(F32)
        g2 = norm_backward(up, normed2, inv2, gain2)
        g2low_ref[...] = g2.astype(BF16)
        stats = [column_sum(g2), column_sum(up * normed2), column_sum(up)]
        put_transposed(g2t_ref, g2low_ref[...], turn, scalars[1], masks[0])
        sums = []
        for k, wd in enumerate((wda, wdb)):
            for c in range(0, f, CHUNK):
                at = k * f + c
                grad_hidden = dot(g2low_ref[...], wd[c : c + CHUNK, :], NT)
                grad_preact = (grad_hidden * dv_ref[:, at : at + CHUNK].astype(F32)).astype(BF16)
                gp_ref, spot = part_of((gpa_ref, gpb_ref)[k], (gpa_rest, gpb_rest)[k], c)
                gp_ref[:, spot : spot + CHUNK] = grad_preact
                sums.append(column_sum(grad_preact.astype(F32)))
        parts = []
        for wi, gp_ref, gp_rest in ((wia, gpa_ref, gpa_rest), (wib, gpb_ref, gpb_rest)):
            most = gp_ref.shape[1]
            part = dot(jnp.concatenate([gp_ref[...], gp_rest[...]], axis=1), wi[...], NT)
            parts.append(part.astype(BF16).astype(F32))
        grad = g2 + (parts[0] + parts[1])
        g1 = norm_backward(grad, normed1, inv1, gain1)
        g1_ref[...] = g1
        g1low_ref[...] = g1.astype(BF16)
        put_transposed(g1t_ref, g1low_ref[...], turn, scalars[1], masks[2])
        stats = [column_sum(g1), column_sum(grad * normed1), column_sum(grad)] + stats
        width = g1.shape[1]
        lines = [
            jnp.concatenate(s, axis=1)
            for s in (sums[: f // CHUNK], sums[f // CHUNK :])
        ]
        for line, sums_ref in zip(lines, (sumsa_ref, sumsb_ref)):
            block = [line[:, c : c + width] for c in range(0, f, width)] + stats
            block = jnp.concatenate(block, axis=0)
            sums_ref[...] = block if first else sums_ref[...] + block

    @pl.when(step == 0)
    def _():
        for copy in copies:
            copy.start()
        tile(True)

    @pl.when(step > 0)
    def _():
        tile(False)


def mlp(scalars, tok, pa, pb, up, vec, ba, bb, wia, wib, wda, wdb, tile, orders):
    rows, width = pa.shape
    f = wia.shape[1]
    steps = rows // tile
    hbm = pl.BlockSpec(memory_space=pl.ANY)
    tok_spec = rows_spec(tile, width)
    mine_spec = side_spec(tile, width, steps)
    masks = [order_blocks(width, order)[0] for order in orders]
    shape = order_blocks(width, orders[0])[1]
    lines = f // width + 6
    most = f // CHUNK * 2 // 3 * CHUNK
    return call(
        functools.partial(mlp_kernel, masks),
        "mlp",
        (steps,),
        [mine_spec, tok_spec, tok_spec, mine_spec]
        + [fixed_spec(vec.shape), fixed_spec(ba.shape), fixed_spec(bb.shape)]
        + [hbm] * 4,
        [mine_spec, tok_spec]
        + [transposed_spec(shape, tile)] * 4
        + [rows_spec(tile, most)] * 4
        + [rows_spec(tile, f - most)] * 4
        + [tok_spec] * 2
        + [fixed_spec((lines, width))] * 2,
        [sd((2 * rows, width), BF16), sd((rows, width), BF16)]
        + [sd(shape + (rows,), BF16)] * 4
        + [sd((rows, most), BF16)] * 4
        + [sd((rows, f - most), BF16)] * 4
        + [sd((rows, width), F32), sd((rows, width), BF16)]
        + [sd((lines, width), F32)] * 2,
        [pltpu.VMEM((width, f), BF16)] * 2
        + [pltpu.VMEM((f, width), BF16)] * 2
        + [pltpu.VMEM((tile, 2 * f), BF16)]
        + [pltpu.VMEM((tile, width), BF16)] * 2
        + [pltpu.VMEM(shape + (tile,), BF16), pltpu.SemaphoreType.DMA((4,))],
        (16 * rows * width * f, 8 * width * f + 30 * rows * width + 8 * rows * f, 4 * rows * f),
        60,
    )(scalars, tok, pa, pb, up, vec, ba, bb, wia, wib, wda, wdb)


class Order:
    def __init__(self, count):
        self.count = count
        self.bits = list(range(count.bit_length() - 1))

    def masks(self):
        return [mask_of(self.bits, j) for j in range(self.count)]


def mask_of(bits, j):
    size = len(bits)
    return sum(((j >> (size - 1 - k)) & 1) << bit for k, bit in enumerate(bits))


def order_blocks(width, order):
    if (width // order.count) % 16 == 0:
        return (order.masks(), (order.count, width // order.count))
    return ([0], (1, width))


def transposed_spec(shape, n):
    return pl.BlockSpec(shape + (n,), lambda i, s: (0, 0, i))


def in_order(grad, order):
    rows, cols = grad.shape
    if len(order_blocks(rows, order)[0]) > 1:
        return grad.reshape(order.count, rows // order.count, cols)
    total = len(order.bits)
    index = lax.axis_index("dp")
    view = grad.reshape((2,) * total + (rows // order.count, cols))
    for bit in range(total):
        axis = total - 1 - bit
        view = jnp.where(((index >> bit) & 1) == 1, jnp.flip(view, axis), view)
    axes = [total - 1 - bit for bit in order.bits]
    view = jnp.transpose(view, axes + [total, total + 1])
    return view.reshape(order.count, rows // order.count, cols)


def swap_pair(value):
    return lax.ppermute(value, "tensor", [(0, 1), (1, 0)])


def swap_bits(value, count, mask):
    return lax.ppermute(value, "dp", [(i, i ^ mask) for i in range(count)])


def total_of(terms):
    total = terms[0].astype(F32)
    for term in terms[1:]:
        total = total + term.astype(F32)
    return total


class RowScatter:
    def __init__(self, terms, order, stages):
        self.count = order.count
        self.left = list(order.bits)
        self.terms = list(terms)
        self.marks = [tuple(order.bits)] * len(terms)
        stages = [[bit for bit in stage if bit in self.left] for stage in stages]
        used = [bit for stage in stages for bit in stage]
        stages = stages + [[bit] for bit in self.left if bit not in used]
        self.stages = [stage for stage in stages if stage]
        self.pending = []

    def pick(self, chosen):
        total = 0.0
        for term, bits in zip(self.terms, self.marks):
            view = term.reshape((2,) * len(bits) + term.shape[1:])
            at = tuple(chosen.get(bit, slice(None) if bit in self.left else 0) for bit in bits)
            total = total + view[at].reshape((-1,) + term.shape[1:]).astype(F32)
        return total

    def sums(self):
        bits = self.stages.pop(0)
        away, masks = [], []
        for j in range(1, 1 << len(bits)):
            masks.append(mask_of(bits, j))
            chosen = {bit: (masks[-1] >> bit) & 1 for bit in bits}
            away.append(self.pick(chosen).astype(BF16))
        self.left = [bit for bit in self.left if bit not in bits]
        return (away, masks)

    def send(self):
        self.away, masks = self.sums()
        self.pending = [swap_bits(away, self.count, mask) for away, mask in zip(self.away, masks)]

    def take(self, received):
        self.terms = self.terms + list(received)
        self.marks = self.marks + [tuple(self.left)] * len(received)

    def add(self):
        self.take(self.pending)
        self.pending = []

    def own(self):
        return self.pick({})[0]

    def more(self):
        return bool(self.stages)


class JointScatter:
    def __init__(self, *chains):
        self.chains = chains
        self.pending = []

    def send(self):
        stages = [chain.sums() for chain in self.chains]
        masks = stages[0][1]
        self.away = [jnp.stack(two) for two in zip(*[away for away, _ in stages])]
        count = self.chains[0].count
        self.pending = [swap_bits(away, count, mask) for away, mask in zip(self.away, masks)]

    def more(self):
        return bool(self.chains[0].stages)

    def add(self):
        for at, chain in enumerate(self.chains):
            chain.take([m[at] for m in self.pending])
        self.pending = []


class SumAll:
    def __init__(self, value, count, bits):
        self.value = value
        self.count = count
        total = count.bit_length() - 1
        bits = [bit for bit in bits if bit < total]
        self.bits = bits + [bit for bit in range(total) if bit not in bits]

    def send(self):
        self.pending = swap_bits(self.value, self.count, 1 << self.bits.pop(0))

    def add(self):
        self.value = self.value + self.pending

    def finish(self):
        self.add()
        while self.bits:
            self.send()
            self.add()
        return self.value


def fence(*values):
    return lax.optimization_barrier(values)


def attend_back_kernel(
    scalars, g_ref, gt_ref, tokt_ref, q_all, k_all, v_all, p_all, c_all, wo_ref, sums_ref, *rest,
):
    wq_ref = rest[0] if len(rest) == 7 else None
    first_ref, lines_ref, grada_ref, gradb_ref, acc_ref = rest[1:6] if wq_ref is not None else rest
    d_ref = rest[6] if wq_ref is not None else first_ref
    step = pl.program_id(0)
    q_ref, k_ref, v_ref, p_ref, c_ref = [ref.at[step] for ref in (q_all, k_all, v_all, p_all, c_all)]
    rows, cols = q_ref.shape
    scale = 1.0 / math.sqrt(HEAD_DIM)
    grad_context = dot(g_ref[...], wo_ref[...], NT).astype(BF16)
    lane = lax.broadcasted_iota(jnp.int32, (rows, PAIR), 1)
    low = lane < HEAD_DIM
    zero = jnp.zeros((rows, PAIR), BF16)
    for pair in range(cols // PAIR):
        lo = pair * PAIR
        at = pl.ds(lo, PAIR)
        q = q_ref[:, at]
        v = v_ref[:, at]
        k = k_ref[:, at]
        do = grad_context[:, lo : lo + PAIR]
        product = do.astype(F32) * c_ref[:, at].astype(F32)
        q_t = q.T
        do_t = do.T
        grads_q, grads_k, grads_v = [], [], []
        for half in range(2):
            mine = low if half == 0 else lane >= HEAD_DIM
            row_dot = jnp.sum(jnp.where(mine, product, 0.0), axis=1, keepdims=True)
            probs = p_ref[pair * 2 + half]
            grad_probs = dot(jnp.where(mine, do, zero), v, NT)
            grad_scores = (probs.astype(F32) * (grad_probs - row_dot)).astype(BF16)
            grads_q.append(dot(grad_scores, k))
            own = slice(half * HEAD_DIM, (half + 1) * HEAD_DIM)
            grads_k.append(dot(q_t[own], grad_scores))
            grads_v.append(dot(do_t[own], probs))
        d_ref[0, :, at] = (jnp.where(low, grads_q[0], grads_q[1]) * scale).astype(BF16)
        d_ref[1, :, at] = jnp.concatenate(grads_k, axis=0).T.astype(BF16)
        d_ref[2, :, at] = jnp.concatenate(grads_v, axis=0).T.astype(BF16)
    if wq_ref is not None:
        first_ref[...] = input_part(d_ref, wq_ref).astype(BF16)
    tok_t = tokt_ref[...].reshape(-1, rows)
    g_t = gt_ref[...].reshape(-1, rows)
    new = [dot(tok_t, d_ref[j]) for j in range(3)] + [dot(g_t, c_ref[...])]
    bias = [column_sum(d_ref[j].astype(F32)) for j in (0, 2)]
    lines = sums_ref.shape[0]
    spots = [(slice(lines, lines + 1), slice(j * cols, (j + 1) * cols)) for j in range(2)]

    @pl.when(step == 0)
    def _():
        lines_ref[...] = jnp.zeros(lines_ref.shape, F32)
        lines_ref[:lines] = sums_ref[...]
        for j in range(4):
            acc_ref[j] = new[j]
        for spot, line in zip(spots, bias):
            lines_ref[spot] = line

    @pl.when(step > 0)
    def _():
        for j in range(4):
            acc_ref[j] = acc_ref[j] + new[j]
        for spot, line in zip(spots, bias):
            lines_ref[spot] = lines_ref[spot] + line

    @pl.when(step == pl.num_programs(0) - 1)
    def _():
        for j, grad_ref in enumerate((grada_ref, grada_ref, gradb_ref, gradb_ref)):
            at = (j % 2) * cols
            grad_ref[:, at : at + cols] = acc_ref[j].astype(BF16)


def attend_back(scalars, g, g_t, tok_t, q, k, v, p, c, wo, sums, wq=None):
    rows, width = g.shape
    seqs, heads, n, _ = p.shape
    cols = q.shape[1]
    q, k, v, c = [m.reshape(seqs, n, cols) for m in (q, k, v, c)]
    turned = transposed_spec(g_t.shape[:2], n)
    extra = () if wq is None else (wq,)
    if wq is None:
        first_spec = pl.BlockSpec((3, n, cols), lambda i, s: (0, i, 0))
        first_shape = (3, rows, cols)
    else:
        first_spec = rows_spec(n, width)
        first_shape = (rows, width)
    return call(
        attend_back_kernel,
        "attend_back",
        (seqs,),
        [rows_spec(n, width), turned, turned]
        + [pl.BlockSpec(memory_space=pltpu.VMEM)] * 5
        + [
            fixed_spec(wo.shape),
            fixed_spec(sums.shape),
        ]
        + [fixed_spec(w.shape) for w in extra],
        [first_spec, fixed_spec((16, 2 * cols))] + [fixed_spec((width, 2 * cols))] * 2,
        [sd(first_shape, BF16), sd((16, 2 * cols), F32)] + [sd((width, 2 * cols), BF16)] * 2,
        [pltpu.VMEM((4, width, cols), F32)] + [pltpu.VMEM((3, n, cols), BF16)] * len(extra),
        (
            (10 + 6 * len(extra)) * rows * width * cols + 16 * rows * n * cols,
            2 * (rows * n * heads + 8 * rows * cols + 8 * width * cols),
            0,
        ),
        25 + 2 * len(extra),
    )(scalars, g, g_t, tok_t, q, k, v, p, c, wo, sums, *extra)


def input_part(d_ref, w_ref):
    return dot(d_ref[0], w_ref[0], NT) + dot(d_ref[1], w_ref[1], NT) + dot(d_ref[2], w_ref[2], NT)


def input_grad_kernel(scalars, g1_ref, part_ref, d_ref, w_ref, whole_ref, mine_ref):
    own = input_part(d_ref, w_ref).astype(BF16).astype(F32)
    mine_ref[...] = (g1_ref[...] + (own + part_ref[...].astype(F32))).astype(BF16)
    whole_ref[...] = mine_ref[...]


def input_grad(scalars, g1, part, d, w, tile):
    rows, width = g1.shape
    cols = d.shape[2]
    steps = rows // tile
    tok_spec = rows_spec(tile, width)
    return call(
        input_grad_kernel,
        "input_grad",
        (steps,),
        [tok_spec, tok_spec, pl.BlockSpec((3, tile, cols), lambda i, s: (0, i, 0)), fixed_spec(w.shape)],
        [side_spec(tile, width, steps), tok_spec],
        [sd((2 * rows, width), BF16), sd((rows, width), BF16)],
        [],
        (6 * rows * width * cols, 10 * rows * width + 6 * rows * cols + 6 * width * cols, 0),
        32,
    )(scalars, g1, part, d, w)


def shards(
    dp_count,
    tokens_in,
    segment_ids,
    w_qkv,
    bias_qv,
    w_out,
    bias_out,
    norm1_gain,
    norm1_shift,
    w_in,
    bias_in,
    w_down,
    bias_down,
    norm2_gain,
    norm2_shift,
    grad_output,
):
    seq_count, seq_length = segment_ids.shape
    half_seqs = seq_count // 2
    rows = half_seqs * seq_length
    width = tokens_in.shape[1]
    local_cols = w_qkv.shape[2]
    f = w_in.shape[1]
    side = lax.axis_index("tensor")
    scalars = jnp.stack([side, lax.axis_index("dp")]).astype(jnp.int32)
    order = Order(dp_count)

    vec = jnp.stack([bias_out, norm1_gain, norm1_shift, bias_down, norm2_gain, norm2_shift])
    bias_line = bias_in.reshape(1, f)
    others = [swap_pair(w) for w in (w_qkv, w_out, w_in, w_down)]
    *kept, part = attend(scalars, tokens_in, segment_ids, w_qkv, bias_qv, w_out)
    part, bias_qv, bias_line = fence(part, bias_qv, bias_line)
    bias_others = [swap_pair(w) for w in (bias_qv, bias_line)]
    saved, parts = [kept], [part]
    others = [others[0], bias_others[0], others[1], others[2], bias_others[1], others[3]]
    w_qkv_two, bias_qv_two, w_out_two, w_in_two, bias_in_two, w_down_two = [
        (own, other)
        for own, other in zip(
            (w_qkv, bias_qv, w_out, w_in, bias_line, w_down), others
        )
    ]
    *kept, part = attend(scalars, tokens_in, segment_ids, w_qkv_two[1], bias_qv_two[1], w_out_two[1])
    saved.append(kept)
    parts.append(part)
    output, output_mine, g2_t, low_t, g1_t, tok_t, *columns, g1, g1low, sums_own, sums_other = mlp(
        scalars, tokens_in, *parts, grad_output, vec,
        *bias_in_two, *w_in_two, *w_down_two, 256, (order,) * 4,
    )

    def whole(full, other):
        return lax.dynamic_update_slice_in_dim(full, other, (1 - side) * rows, 0)

    def outer(left, right):
        return dot(left.reshape(width, rows), right).astype(BF16)

    lefts = (g2_t, g2_t, low_t, low_t)
    other_grads = [[swap_pair(outer(lefts[at], part[at])) for at in (1, 3)] for part in (columns[:4], columns[4:])]
    own_grads = [[outer(lefts[at], part[at]) for at in (0, 2)] for part in (columns[:4], columns[4:])]
    output_recv = swap_pair(output_mine)
    g1low, own_grads, other_grads = fence(g1low, own_grads, other_grads)

    def chain_of(part, at, *stages):
        return RowScatter([in_order(m[part][at], order) for m in (own_grads, other_grads)], order, stages)

    down = chain_of(0, 0, (0,), (1,), (2,), (3,))
    inner = chain_of(0, 1, (1,), (3,), (2,), (0,))
    down_rest, in_rest = [chain_of(1, at, (2,), (0,), (3,), (1,)) for at in (0, 1)]
    pair_rest = JointScatter(down_rest, in_rest)

    def back(at, g, *rest):
        return attend_back(scalars, g, g1_t, tok_t, *saved[at], w_out_two[at], *rest)

    down.send()
    inner.send()
    pair_rest.send()
    part_other, lines_other, *grads_other = back(1, g1low, sums_other, w_qkv_two[1])
    part_other, lines_other, grads_other, down.pending, inner.pending, pair_rest.pending, output_recv = fence(
        part_other, lines_other, grads_other, down.pending, inner.pending, pair_rest.pending, output_recv
    )
    grads_recv = [swap_pair(grad) for grad in grads_other]
    lines_recv = swap_pair(lines_other)

    def next_stage():
        for chain in (down, inner, pair_rest):
            chain.add()
        for chain in (down, inner, pair_rest):
            chain.send()

    next_stage()
    g1low, part_other = fence(g1low, part_other)
    d_own, lines_own, *grads_own = back(0, g1low, sums_own)
    d_own, lines_own, grads_own, grads_recv, lines_recv, down.pending, inner.pending, pair_rest.pending = fence(
        d_own, lines_own, grads_own, grads_recv, lines_recv, down.pending, inner.pending, pair_rest.pending
    )
    last = [order.bits[2:4]] if dp_count <= 16 else []
    head_a, head_b = [
        RowScatter([in_order(m, order) for m in terms], order, [[first], [1 - first]] + last)
        for first, terms in enumerate(zip(grads_own, grads_recv))
    ]
    lines = SumAll(lines_own + lines_recv, dp_count, (0, 3, 2, 1))
    lines.send()
    head_a.send()
    head_b.send()
    head_a.away, head_b.away, down.pending, inner.pending, pair_rest.pending = fence(
        head_a.away, head_b.away, down.pending, inner.pending, pair_rest.pending
    )
    next_stage()
    d_own, lines.pending = fence(d_own, lines.pending)
    grad_input, grad_mine = input_grad(scalars, g1, part_other, d_own, w_qkv, 256)
    grad_input, grad_mine, head_a.pending, head_b.pending, lines.pending, output_recv = fence(
        grad_input, grad_mine, head_a.pending, head_b.pending, lines.pending, output_recv
    )
    lines.add()
    lines.send()
    head_a.add()
    head_b.add()
    head_a.send()
    head_b.send()
    head_a.away, head_b.away, down.pending, inner.pending, pair_rest.pending, output_recv, grad_mine = fence(
        head_a.away, head_b.away, down.pending, inner.pending, pair_rest.pending, output_recv, grad_mine
    )
    next_stage()
    grad_recv = swap_pair(grad_mine)
    output = whole(output, output_recv)
    output, head_a.pending, head_b.pending, lines.pending, grad_recv = fence(
        output, head_a.pending, head_b.pending, lines.pending, grad_recv
    )
    head_a.add()
    head_b.add()
    lines.add()
    lines.send()
    heads = JointScatter(head_a, head_b)
    heads.send()
    heads.away, down.pending, inner.pending, pair_rest.pending, grad_recv, lines.pending = fence(
        heads.away, down.pending, inner.pending, pair_rest.pending, grad_recv, lines.pending
    )
    lines.add()
    lines.send()
    for chain in (down, inner, pair_rest):
        chain.add()
        while chain.more():
            chain.send()
            chain.add()
    grad_input = whole(grad_input, grad_recv)
    summed_w_down = jnp.concatenate([down.own(), down_rest.own()], axis=1).T
    summed_w_in = jnp.concatenate([inner.own(), in_rest.own()], axis=1)
    grad_input, summed_w_down, summed_w_in, heads.pending, lines.pending = fence(
        grad_input, summed_w_down, summed_w_in, heads.pending, lines.pending
    )
    heads.add()
    while heads.more():
        heads.send()
        heads.add()
    total = lines.finish()
    at_stats = sums_own.shape[0] - 6
    summed_bias_in = total[:at_stats].reshape(f)
    summed = [total[at_stats + i] for i in range(6)]
    summed_bias_qv = total[at_stats + 6].reshape(2, local_cols)
    summed_a, summed_b = head_a.own(), head_b.own()
    summed_w_qkv = jnp.stack([summed_a[:, :local_cols], summed_a[:, local_cols:], summed_b[:, :local_cols]])
    summed_w_out = summed_b[:, local_cols:].T

    return (
        output,
        grad_input,
        summed_w_qkv,
        summed_bias_qv,
        summed_w_out,
        summed[0],
        summed[1],
        summed[2],
        summed_w_in,
        summed_bias_in,
        summed_w_down,
        summed[3],
        summed[4],
        summed[5],
    )


def solution(mesh):
    dp_count = mesh.shape["dp"]

    def body(*args):
        return shards(dp_count, *args)

    return jax.shard_map(
        body,
        mesh=mesh,
        in_specs=(
            P("dp", None),
            P("dp", None),
            P(None, None, "tensor"),
            P(None, "tensor"),
            P("tensor", None),
            P(),
            P(),
            P(),
            P(None, "tensor"),
            P("tensor"),
            P("tensor", None),
            P(),
            P(),
            P(),
            P("dp", None),
        ),
        out_specs=(
            P("dp", None),
            P("dp", None),
            P(None, "dp", "tensor"),
            P(None, "tensor"),
            P("tensor", "dp"),
            P(),
            P(),
            P(),
            P("dp", "tensor"),
            P("tensor"),
            P("tensor", "dp"),
            P(),
            P(),
            P(),
        ),
        check_vma=False,
    )
```
